768 devices in a mesh: tile: 96 (over y_lo, z, core), scan: 8 (over x, y_hi).
Axes of the slice: x: 4, y: 8 (y_hi: 2, y_lo: 4; y = y_hi * 4 + y_lo), z: 12, core: 2. Of those that a mesh axis runs over, the one named last changes fastest.
Arguments:
- consensus: float32 [96, 2, 256, 256], P('tile'), may hold values from -4 to 4
- duals: float32 [8, 96, 2, 256, 256], P('scan', 'tile'), may hold values from -3 to 3
- probes: float32 [8, 2, 256, 256], P('scan'), may hold values from -4 to 4
- amplitudes: bfloat16 [8, 96, 4, 256, 256], P('scan', 'tile'), may hold values from 0.19921875 to 2
- offsets: int32 [8, 96, 4, 2], P('scan', 'tile'), may hold values from 0 to 128
- counts: int32 [8, 96], P('scan', 'tile'), may hold values from 1 to 4, as said below
Outputs:
- consensus_new: float32 [96, 2, 256, 256], P('tile')
- duals_new: float32 [8, 96, 2, 256, 256], P('scan', 'tile')
- probes_new: float32 [8, 2, 256, 256], P('scan')
The draws below stay inside these ranges and needn't reach their ends.
Inputs may be any that keep to these rules, and one draw needn't show every extreme that they name: counts: some group has 4 scan positions in some tile; slots at or past the count are unused. offsets: first the row, then the column.
All inputs are finite; a program needn't handle non-finite values.
Results may differ from the reference program's by a relative error of at most 0.015.
Values may be sent and summed in bfloat16 or wider, within the bound.
A program may use at most 32 MiB of HBM per device.

```python
import math
import jax
import jax.numpy as jnp
from jax import lax

PS = 256
TS = 256
OVER = 128
TGW = 4
SLOTS = 4
INNER = 2
GROUPS = 8
TILES = 96


def draw_counts(key, part):
    levels = jax.random.randint(key, (GROUPS, TILES), 0, 4)
    result = jnp.where(levels == 0, SLOTS, 1).astype(jnp.int32)
    return result.at[0, 0].set(SLOTS)


def with_ends(entries, rng, smallest, largest):
    place = [jax.random.randint(jax.random.fold_in(rng, axis), (), 0, length) for axis, length in enumerate(entries.shape)]
    widest = entries.shape.index(max(entries.shape))
    neighbour = place[:widest] + [(place[widest] + 1) % entries.shape[widest]] + place[widest + 1:]
    return entries.at[tuple(place)].set(smallest).at[tuple(neighbour)].set(largest)


def level_of(stream_key, shape, split, low, high):
    def one(position, parts):
        heights = jax.random.uniform(jax.random.fold_in(jax.random.fold_in(stream_key, 6), position), (parts,), jnp.float32, low / len(split), high / len(split))
        return jnp.repeat(jnp.exp(heights), shape[position] // parts).reshape((-1,) + (1,) * (len(shape) - position - 1))

    gain = one(*split[0])
    for cut in split[1:]:
        gain = gain * one(*cut)
    return gain


def gaussian(key, dims, scale, bound, split=(), held_as=jnp.bfloat16):
    loudness = level_of(key, dims, split, -0.22, 0.18) if split else 1.0
    values = jax.random.normal(key, dims, jnp.float32) * scale * loudness
    return jnp.minimum(jnp.maximum(values, -bound), bound).astype(held_as)


def setup_inputs(seed: int = 0) -> dict:
    key_of = jax.random.split(jax.random.key(seed), 7)
    consensus = gaussian(key_of[0], (TILES, 2, TS, TS), 0.6, 4.0, ((0, 96),), jnp.float32)
    duals = gaussian(key_of[1], (GROUPS, TILES, 2, TS, TS), 0.3, 3.0, ((0, 8), (1, 96)), jnp.float32)
    probes = gaussian(key_of[2], (GROUPS, 2, PS, PS), 0.7, 4.0, ((0, 8),), jnp.float32)
    amplitudes = jnp.clip(0.19921875 + 1.8007812 * jax.random.uniform(key_of[3], (GROUPS, TILES, SLOTS, PS, PS), jnp.float32) ** level_of(key_of[3], (GROUPS, TILES, SLOTS, PS, PS), ((0, 8), (1, 96)), -0.2, 0.2), 0.19921875, 2.0).astype(jnp.bfloat16)
    offsets = with_ends(jax.random.randint(key_of[4], (GROUPS, TILES, SLOTS, 2), 0, TS - PS + OVER + 1), jax.random.fold_in(key_of[4], 1), 0, TS - PS + OVER).astype(jnp.int32)
    counts = draw_counts(jax.random.fold_in(key_of[6], 71), 0)
    return {"consensus": consensus, "duals": duals, "probes": probes, "amplitudes": amplitudes, "offsets": offsets, "counts": counts}


penalty = 0.5
smoothing = 0.05
probe_step = 3.0

def dft_tables(length):
    indices = jnp.arange(length, dtype=jnp.int32)
    phase_index = indices[:, None] * indices[None, :] % length
    angles = phase_index.astype(jnp.float32) * (2.0 * math.pi / length)
    norm_scale = 1.0 / math.sqrt(length)
    real_part = (jnp.cos(angles) * norm_scale).astype(jnp.bfloat16)
    imag_part = (-jnp.sin(angles) * norm_scale).astype(jnp.bfloat16)
    return (real_part, imag_part)

def forward_wave(wave_real, wave_imag, stacked, spread, length):
    section_one = jnp.dot(stacked, jnp.concatenate([wave_real, wave_imag], 1), preferred_element_type=jnp.float32)
    inner_real = (section_one[:length, :length] - section_one[length:, length:]).astype(jnp.bfloat16)
    inner_imag = (section_one[:length, length:] + section_one[length:, :length]).astype(jnp.bfloat16)
    section_two = jnp.dot(jnp.concatenate([inner_real, inner_imag], 0), spread, preferred_element_type=jnp.float32)
    return (section_two[:length, :length] - section_two[length:, length:], section_two[:length, length:] + section_two[length:, :length])

def inverse_wave(wave_real, wave_imag, stacked, spread, length):
    section_one = jnp.dot(stacked, jnp.concatenate([wave_real, wave_imag], 1), preferred_element_type=jnp.float32)
    inner_real = (section_one[:length, :length] + section_one[length:, length:]).astype(jnp.bfloat16)
    inner_imag = (section_one[:length, length:] - section_one[length:, :length]).astype(jnp.bfloat16)
    section_two = jnp.dot(jnp.concatenate([inner_real, inner_imag], 0), spread, preferred_element_type=jnp.float32)
    return (section_two[:length, :length] + section_two[length:, length:], section_two[length:, :length] - section_two[:length, length:])

def patch_terms(window, probe_field, measured, stacked, spread):
    length = window.shape[1]
    object_real = window[0].astype(jnp.float32)
    object_imag = window[1].astype(jnp.float32)
    probe_real = probe_field[0]
    probe_imag = probe_field[1]
    exit_real = (probe_real * object_real - probe_imag * object_imag).astype(jnp.bfloat16)
    exit_imag = (probe_real * object_imag + probe_imag * object_real).astype(jnp.bfloat16)
    wave_real, wave_imag = forward_wave(exit_real, exit_imag, stacked, spread, length)
    modulus = jnp.sqrt(wave_real * wave_real + wave_imag * wave_imag + smoothing)
    factor = measured.astype(jnp.float32) / modulus - 1.0
    resid_real = (wave_real * factor).astype(jnp.bfloat16)
    resid_imag = (wave_imag * factor).astype(jnp.bfloat16)
    back_real, back_imag = inverse_wave(resid_real, resid_imag, stacked, spread, length)
    object_terms = jnp.stack([probe_real * back_real + probe_imag * back_imag, probe_real * back_imag - probe_imag * back_real, probe_real * probe_real + probe_imag * probe_imag])
    probe_terms = jnp.stack([object_real * back_real + object_imag * back_imag, object_real * back_imag - object_imag * back_real, object_real * object_real + object_imag * object_imag])
    return (object_terms, probe_terms)

def to_grid(blocks):
    tile_rows = TILES // TGW
    channels = blocks.shape[1]
    return blocks.reshape(tile_rows, TGW, channels, TS, TS).transpose(2, 0, 3, 1, 4).reshape(channels, tile_rows * TS, TGW * TS)

def to_tiles(grid):
    tile_rows = TILES // TGW
    channels = grid.shape[0]
    return grid.reshape(channels, tile_rows, TS, TGW, TS).transpose(1, 3, 0, 2, 4).reshape(tile_rows * TGW, channels, TS, TS)

def reference(consensus, duals, probes, amplitudes, offsets, counts):
    tile_rows = TILES // TGW
    height = tile_rows * TS
    width = TGW * TS
    span = TS + OVER
    real_part, imag_part = dft_tables(PS)
    stacked = jnp.concatenate([real_part, imag_part], 0)
    spread = jnp.concatenate([real_part, imag_part], 1)
    tile_ids = jnp.arange(TILES, dtype=jnp.int32)
    row_base = (tile_ids // TGW * TS).astype(jnp.int32)
    col_base = (tile_ids % TGW * TS).astype(jnp.int32)
    zero_index = jnp.zeros((), jnp.int32)
    grid_consensus = to_grid(consensus)

    def solve_group(operands):
        dual_tiles, probe_field, measured, corners, slot_counts = operands
        grid_dual = to_grid(dual_tiles)
        estimate = grid_consensus
        probe_sum = jnp.zeros((3, PS, PS), jnp.float32)
        for sweep_index in range(INNER):
            padded = jnp.pad(estimate.astype(jnp.bfloat16), ((0, 0), (0, OVER), (0, OVER)))

            def visit_tile(carried, tile_index):
                totals, probe_acc = carried
                row_start = row_base[tile_index]
                col_start = col_base[tile_index]
                extended = lax.dynamic_slice(padded, (zero_index, row_start, col_start), (2, span, span))

                def visit_slot(slot_index, inner_state):
                    local_totals, local_probe = inner_state
                    top_row = corners[tile_index, slot_index, 0].astype(jnp.int32)
                    left_col = corners[tile_index, slot_index, 1].astype(jnp.int32)
                    window = lax.dynamic_slice(extended, (zero_index, top_row, left_col), (2, PS, PS))
                    object_terms, probe_terms = patch_terms(window, probe_field, measured[tile_index, slot_index], stacked, spread)
                    region = lax.dynamic_slice(local_totals, (zero_index, top_row, left_col), (3, PS, PS))
                    local_totals = lax.dynamic_update_slice(local_totals, region + object_terms, (zero_index, top_row, left_col))
                    return (local_totals, local_probe + probe_terms)
                start_totals = jnp.zeros((3, span, span), jnp.float32)
                local_totals, probe_acc = lax.fori_loop(0, slot_counts[tile_index], visit_slot, (start_totals, probe_acc))
                region = lax.dynamic_slice(totals, (zero_index, row_start, col_start), (3, span, span))
                totals = lax.dynamic_update_slice(totals, region + local_totals, (zero_index, row_start, col_start))
                return ((totals, probe_acc), None)
            totals = jnp.zeros((3, height + OVER, width + OVER), jnp.float32)
            (totals, probe_sum), unused = lax.scan(visit_tile, (totals, probe_sum), tile_ids)
            returned = totals[:, :height, :width]
            estimate = estimate + (returned[0:2] + penalty * (grid_consensus - grid_dual - estimate)) / (returned[2] + penalty)
        probe_new = probe_field + probe_step * probe_sum[0:2] / jnp.sqrt(probe_sum[2] + 1.0)
        return (estimate, probe_new)
    estimates, probes_new = lax.map(solve_group, (duals, probes, amplitudes, offsets, counts))
    grid_duals = lax.map(to_grid, duals)
    average = lax.optimization_barrier(jnp.sum(estimates + grid_duals, axis=0)) / GROUPS
    magnitude = jnp.sqrt(average[0] * average[0] + average[1] * average[1])
    settled = average / jnp.maximum(magnitude, 1.0)[None]
    duals_grid_new = grid_duals + estimates - settled[None]
    return (to_tiles(settled), lax.map(to_tiles, duals_grid_new), probes_new)
```

```python
import functools
import math

import jax
import jax.numpy as jnp
import ml_dtypes
import numpy as np
from jax import lax
from jax.experimental import pallas as pl
from jax.experimental.pallas import tpu as pltpu
from jax.sharding import PartitionSpec as P

PS = 256
TS = 256
OVER = 128
SPAN = TS + OVER
TGW = 4
TILES = 96
RING = 12
RUN = 4
COLS = 4
OWNERS = 8
LANES = 128
penalty = 0.5
smoothing = 0.05
probe_step = 3.0
MESH = pl.DeviceIdType.MESH
VMEM = pl.BlockSpec(memory_space=pltpu.VMEM)
SMEM = pl.BlockSpec(memory_space=pltpu.SMEM)


def transform_tables():
    index = np.arange(PS, dtype=np.int64)
    angle = ((index[:, None] * index[None, :]) % PS).astype(np.float64) * (2.0 * math.pi / PS)
    scale = 1.0 / math.sqrt(PS)
    real = (np.cos(angle) * scale).astype(np.float32)
    imag = (-np.sin(angle) * scale).astype(np.float32)
    forward = np.block([[real, -imag], [imag, real]])
    return forward.astype(ml_dtypes.bfloat16), forward.T.astype(ml_dtypes.bfloat16)


def shifted_in(block, col, lane):
    amount = lax.rem(LANES - col, LANES)
    turned = [pltpu.roll(piece, amount, axis=1) for piece in block]
    keep = lane < LANES - col
    return [jnp.where(keep, turned[k], turned[k + 1]) for k in range(2)]


def shifted_out(left, right, col, lane):
    amount = lax.rem(col, LANES)
    left = pltpu.roll(left, amount, axis=1)
    right = pltpu.roll(right, amount, axis=1)
    past = lane >= col
    zero = jnp.zeros_like(left)
    return [jnp.where(past, left, zero), jnp.where(past, right, left), jnp.where(past, zero, right)]


def patches_kernel(first, R0, R1, *refs):
    if first:
        (off_ref, cnt_ref, wide_ref, probe_ref, amp_ref, m1_ref, m2_ref,
         center_ref, rr_ref, rb_ref, rd_ref, psum_ref,
         tot_ref, e_ref, r_ref, win_ref) = refs
        acc_ref = psum_ref
    else:
        (off_ref, cnt_ref, wide_ref, probe_ref, amp_ref, m1_ref, m2_ref, prev_ref,
         center_ref, rr_ref, rb_ref, rd_ref, psum_ref,
         tot_ref, e_ref, r_ref, win_ref, acc_ref) = refs
    channels = 3 if first else 2
    tot_ref[...] = jnp.zeros_like(tot_ref)
    if first:
        acc_ref[...] = jnp.zeros_like(acc_ref)
    else:
        acc_ref[...] = prev_ref[...]
    half = [pl.ds(0, LANES), pl.ds(LANES, LANES)]

    def visit(slot, carry):
        row = off_ref[slot, 0]
        col = off_ref[slot, 1]
        lane0 = lax.broadcasted_iota(jnp.int32, (R0, LANES), 1)
        lane1 = lax.broadcasted_iota(jnp.int32, (R1, LANES), 1)

        def gather(step, c):
            r = pl.multiple_of(step * R0, R0)
            real = shifted_in([wide_ref[0, k, pl.ds(row + r, R0), :] for k in range(3)], col, lane0)
            imag = shifted_in([wide_ref[1, k, pl.ds(row + r, R0), :] for k in range(3)], col, lane0)
            for h in range(2):
                wr, wi = real[h], imag[h]
                pr = probe_ref[0, pl.ds(r, R0), half[h]]
                pi = probe_ref[1, pl.ds(r, R0), half[h]]
                win_ref[0, pl.ds(r, R0), half[h]] = wr
                win_ref[1, pl.ds(r, R0), half[h]] = wi
                e_ref[pl.ds(r, R0), half[h]] = (pr * wr - pi * wi).astype(jnp.bfloat16)
                e_ref[pl.ds(PS + r, R0), half[h]] = (pr * wi + pi * wr).astype(jnp.bfloat16)
            return c

        lax.fori_loop(0, PS // R0, gather, 0)
        for r in range(0, PS, R1):
            re = jnp.dot(m1_ref[r:r + R1, :], e_ref[...], preferred_element_type=jnp.float32)
            im = jnp.dot(m1_ref[PS + r:PS + r + R1, :], e_ref[...], preferred_element_type=jnp.float32)
            inner = jnp.concatenate([re.astype(jnp.bfloat16), im.astype(jnp.bfloat16)], 1)
            wave = jnp.dot(inner, m2_ref[...], preferred_element_type=jnp.float32)
            wr, wi = wave[:, :PS], wave[:, PS:]
            factor = amp_ref[slot, r:r + R1, :].astype(jnp.float32) * lax.rsqrt(wr * wr + wi * wi + smoothing) - 1.0
            r_ref[r:r + R1, :] = (wr * factor).astype(jnp.bfloat16)
            r_ref[PS + r:PS + r + R1, :] = (wi * factor).astype(jnp.bfloat16)
        for r in range(0, PS, R1):
            re = jnp.dot(m2_ref[r:r + R1, :], r_ref[...], preferred_element_type=jnp.float32)
            im = jnp.dot(m2_ref[PS + r:PS + r + R1, :], r_ref[...], preferred_element_type=jnp.float32)
            inner = jnp.concatenate([re.astype(jnp.bfloat16), im.astype(jnp.bfloat16)], 1)
            back = jnp.dot(inner, m1_ref[...], preferred_element_type=jnp.float32)
            rows = pl.ds(r, R1)
            terms = [[], [], []]
            for h in range(2):
                br = back[:, h * LANES:(h + 1) * LANES]
                bi = back[:, PS + h * LANES:PS + (h + 1) * LANES]
                pr = probe_ref[0, rows, half[h]]
                pi = probe_ref[1, rows, half[h]]
                wr = win_ref[0, rows, half[h]]
                wi = win_ref[1, rows, half[h]]
                terms[0].append(pr * br + pi * bi)
                terms[1].append(pr * bi - pi * br)
                if first:
                    terms[2].append(pr * pr + pi * pi)
                acc_ref[0, rows, half[h]] += wr * br + wi * bi
                acc_ref[1, rows, half[h]] += wr * bi - wi * br
                acc_ref[2, rows, half[h]] += wr * wr + wi * wi
            for c in range(channels):
                out = shifted_out(terms[c][0], terms[c][1], col, lane1)
                for k in range(3):
                    tot_ref[c, k, pl.ds(row + r, R1), :] += out[k]
        return carry

    lax.fori_loop(0, cnt_ref[0, 0], visit, 0)
    for k in range(2):
        center_ref[:, :, half[k]] = tot_ref[:, k, :TS, :]
        rb_ref[:, :, half[k]] = tot_ref[:, k, TS:, :].astype(jnp.bfloat16)
    rr_ref[...] = tot_ref[:, 2, :TS, :].astype(jnp.bfloat16)
    rd_ref[...] = tot_ref[:, 2, TS:, :].astype(jnp.bfloat16)
    if not first:
        for part in range(8):
            rows = pl.ds(part * 32, 32)
            for c in range(3):
                psum_ref[part // 4, part % 4, c] = acc_ref[c, rows, :].astype(jnp.bfloat16)


def patches(first, corners, count, wide, probe, measured, m1, m2, prev=None, R0=256, R1=256):
    channels = 3 if first else 2
    shape = jax.ShapeDtypeStruct
    out_shape = (
        shape((channels, TS, TS), jnp.float32),
        shape((channels, TS, OVER), jnp.bfloat16),
        shape((channels, OVER, TS), jnp.bfloat16),
        shape((channels, OVER, OVER), jnp.bfloat16),
        shape((3, PS, PS), jnp.float32) if first else shape((2, 4, 3, 32, PS), jnp.bfloat16),
    )
    scratch = [
        pltpu.VMEM((channels, 3, SPAN, LANES), jnp.float32),
        pltpu.VMEM((2 * PS, PS), jnp.bfloat16),
        pltpu.VMEM((2 * PS, PS), jnp.bfloat16),
        pltpu.VMEM((2, PS, PS), jnp.float32),
    ]
    args = [corners, count, wide, probe, measured, m1, m2]
    if not first:
        args.append(prev)
        scratch.append(pltpu.VMEM((3, PS, PS), jnp.float32))
    return pl.pallas_call(
        functools.partial(patches_kernel, first, R0, R1),
        out_shape=out_shape,
        in_specs=[SMEM, SMEM] + [VMEM] * (len(args) - 2),
        out_specs=(VMEM,) * 5,
        scratch_shapes=scratch,
        compiler_params=pltpu.CompilerParams(vmem_limit_bytes=28 * 1024 * 1024),
        name="patches",
    )(*args)


def place():
    t = lax.axis_index("tile")
    return t, lax.rem(t, TGW)


def moved(t, by):
    return lax.rem(t + (by + TILES), TILES)


def remote(src, dst, sends, recvs, at, slot, target):
    return pltpu.make_async_remote_copy(
        src_ref=src, dst_ref=dst, send_sem=sends.at[at], recv_sem=recvs.at[slot],
        device_id=target, device_id_type=MESH,
    )


def greet(targets):
    barrier = pltpu.get_barrier_semaphore()
    for target in targets:
        pl.semaphore_signal(barrier, inc=1, device_id=target, device_id_type=MESH)
    pl.semaphore_wait(barrier, len(targets))


def as_float(flag):
    return jnp.where(flag, 1.0, 0.0).astype(jnp.float32)


def split_estimate(value, c, a, b, wide_ref, side_ref, top_ref, corner_ref):
    rounded = value.astype(jnp.bfloat16)
    rows, cols = pl.ds(a * OVER, OVER), pl.ds(b * OVER, OVER)
    wide_ref[c, b, rows, :] = rounded.astype(jnp.float32)
    if b == 0:
        side_ref[c, rows, :] = rounded
    if a == 0:
        top_ref[c, :, cols] = rounded
    if a == 0 and b == 0:
        corner_ref[c] = rounded


def take_rims(t, column, wide_ref, side_in, top_in, corner_in):
    right = as_float(column < TGW - 1)
    below = as_float(t < TILES - TGW)
    for c in range(2):
        wide_ref[c, 2, :TS, :] = side_in[c].astype(jnp.float32) * right
        for b in range(2):
            wide_ref[c, b, TS:, :] = top_in[c, :, b * OVER:(b + 1) * OVER].astype(jnp.float32) * below
        wide_ref[c, 2, TS:, :] = corner_in[c].astype(jnp.float32) * (right * below)


def pull_copies(t, side, top, corner, side_in, top_in, corner_in, sends, recvs, base):
    return (
        remote(corner, corner_in, sends, recvs, base, base, {"tile": moved(t, -TGW - 1)}),
        remote(top, top_in, sends, recvs, base + 1, base + 1, {"tile": moved(t, -TGW)}),
        remote(side, side_in, sends, recvs, base + 2, base + 2, {"tile": moved(t, -1)}),
    )


def push_copies(t, rr, rb, rd, left_in, above_in, corner_in, sends, recvs):
    return (
        remote(rb, above_in, sends, recvs, 0, 0, {"tile": moved(t, TGW)}),
        remote(rr, left_in, sends, recvs, 1, 1, {"tile": moved(t, 1)}),
        remote(rd, corner_in, sends, recvs, 2, 2, {"tile": moved(t, TGW + 1)}),
    )


def quadrant_total(c, a, b, center_ref, left_in, above_in, corner_in, left, above):
    rows, cols = pl.ds(a * OVER, OVER), pl.ds(b * OVER, OVER)
    value = center_ref[c, rows, cols]
    if a == 0:
        value = value + above_in[c, :, cols].astype(jnp.float32) * above
    if b == 0:
        value = value + left_in[c, rows, :].astype(jnp.float32) * left
    if a == 0 and b == 0:
        value = value + corner_in[c].astype(jnp.float32) * (left * above)
    return value


QUADRANTS = ((0, 0), (0, 1), (1, 0), (1, 1))


def open_kernel(cons_ref, wide_ref, side, top, corner, side_in, top_in, corner_in, sends, recvs):
    t, column = place()
    for a, b in QUADRANTS:
        for c in range(2):
            value = cons_ref[c, a * OVER:(a + 1) * OVER, b * OVER:(b + 1) * OVER]
            split_estimate(value, c, a, b, wide_ref, side, top, corner)
    greet([{"tile": moved(t, by)} for by in (1, TGW, TGW + 1)])
    copies = pull_copies(t, side, top, corner, side_in, top_in, corner_in, sends, recvs, 0)
    for copy in copies:
        copy.start()
    for copy in copies:
        copy.wait()
    take_rims(t, column, wide_ref, side_in, top_in, corner_in)


def middle_kernel(center_ref, rr, rb, rd, cons_ref, dual_ref, est_ref, inv_ref, wide_ref,
                  left_in, above_in, rim_in, side, top, corner, side_in, top_in, corner_in, sends, recvs):
    t, column = place()
    greet([{"tile": moved(t, by)} for by in (1, TGW, TGW + 1, -1, -TGW, -TGW - 1)])
    pushes = push_copies(t, rr, rb, rd, left_in, above_in, rim_in, sends, recvs)
    for copy in pushes:
        copy.start()
    for copy in pushes:
        copy.wait_recv()
    pulls = pull_copies(t, side, top, corner, side_in, top_in, corner_in, sends, recvs, 3)
    left = as_float(column > 0)
    above = as_float(t >= TGW)
    for at, (a, b) in enumerate(QUADRANTS):
        rows, cols = pl.ds(a * OVER, OVER), pl.ds(b * OVER, OVER)
        total = [quadrant_total(c, a, b, center_ref, left_in, above_in, rim_in, left, above) for c in range(3)]
        inv = 1.0 / (total[2] + penalty)
        inv_ref[rows, cols] = inv
        for c in range(2):
            value = cons_ref[c, rows, cols] + (total[c] - penalty * dual_ref[c, rows, cols]) * inv
            est_ref[c, rows, cols] = value
            split_estimate(value, c, a, b, wide_ref, side, top, corner)
        if at < 3:
            pulls[at].start()
    for copy in pulls:
        copy.wait_recv()
    take_rims(t, column, wide_ref, side_in, top_in, corner_in)
    for copy in pushes + pulls:
        copy.wait_send()


def close_kernel(center_ref, rr, rb, rd, cons_ref, dual_ref, est_ref, inv_ref, psum, probe_ref,
                 cons_out, dual_out, probe_out,
                 left_in, above_in, rim_in, half_in, half, run_in, ring_out, ring_in, grown,
                 mine, cols_in, part, part_in, settled, kept,
                 rim_s, rim_r, half_s, half_r, run_s, run_r, ring_s, ring_r, grow_s, grow_r,
                 wide_s, wide_r, back_s, back_r, col_s, col_r, pair_s, pair_r, out_s, out_r):
    t, column = place()
    core = lax.rem(t, 2)
    z = lax.rem(lax.div(t, 2), RING)
    y = lax.div(t, 2 * RING)
    scan = lax.axis_index("scan")
    yh = lax.rem(scan, 2)
    x = lax.div(scan, 2)
    tile_at = lambda y_, z_, c_: {"tile": (y_ * RING + z_) * 2 + c_}
    scan_at = lambda x_, h_: {"scan": x_ * 2 + h_}
    ys = [lax.rem(y + k, RUN) for k in range(1, RUN)]
    xs = [lax.rem(x + k, COLS) for k in range(1, COLS)]
    sibling = tile_at(y, z, 1 - core)
    twin = scan_at(x, 1 - yh)

    greet([{"tile": moved(t, by)} for by in (-1, -TGW, -TGW - 1)] + [sibling, twin]
          + [tile_at(k, z, core) for k in ys] + [scan_at(k, yh) for k in xs]
          + [tile_at(y, lax.rem(z + k, RING), core) for k in range(1, RING)])

    pushes = push_copies(t, rr, rb, rd, left_in, above_in, rim_in, rim_s, rim_r)
    for copy in pushes:
        copy.start()
    to_half = remote(psum.at[1 - core], half_in, half_s, half_r, 0, 0, sibling)
    to_half.start()

    to_half.wait_recv()
    for q in range(RUN):
        half[q] = (psum[core, q].astype(jnp.float32) + half_in[q].astype(jnp.float32)).astype(jnp.bfloat16)
    for k in ys:
        remote(half.at[k], run_in.at[y], run_s, run_r, k, y, tile_at(k, z, core)).start()

    for copy in pushes:
        copy.wait_recv()
    left = as_float(column > 0)
    above = as_float(t >= TGW)
    for a, b in QUADRANTS:
        rows, cols = pl.ds(a * OVER, OVER), pl.ds(b * OVER, OVER)
        inv = inv_ref[rows, cols]
        for c in range(2):
            total = quadrant_total(c, a, b, center_ref, left_in, above_in, rim_in, left, above)
            dual = dual_ref[c, rows, cols]
            estimate = est_ref[c, rows, cols]
            value = estimate + (total + penalty * (cons_ref[c, rows, cols] - dual - estimate)) * inv + dual
            kept[c, rows, cols] = value
            value = value.astype(jnp.bfloat16)
            for q in range(2):
                mine[2 * a + q, c, :, cols] = value[q * 64:(q + 1) * 64]
    for k in xs:
        remote(mine.at[k], cols_in.at[x], col_s, col_r, k, x, scan_at(k, yh)).start()

    for k in ys:
        remote(half.at[k], run_in.at[k], run_s, run_r, k, k, tile_at(k, z, core)).wait_recv()
    run_in[y] = half[y]
    for c in range(3):
        summed = run_in[0, c].astype(jnp.float32)
        for k in range(1, RUN):
            summed = summed + run_in[k, c].astype(jnp.float32)
        summed = summed.astype(jnp.bfloat16)
        for k in range(OWNERS):
            ring_out[k, c] = summed[(k // 2) * 8:(k // 2) * 8 + 8, (k % 2) * LANES:(k % 2 + 1) * LANES]

    def ring_step(k, c):
        other = lax.rem(z + k, RING)

        @pl.when(other < OWNERS)
        def _():
            remote(ring_out.at[other], ring_in.at[z], ring_s, ring_r, other, z, tile_at(y, other, core)).start()

        return c

    lax.fori_loop(1, RING, ring_step, 0)

    for k in xs:
        remote(mine.at[k], cols_in.at[k], col_s, col_r, k, k, scan_at(k, yh)).wait_recv()
    cols_in[x] = mine[x]
    for c in range(2):
        summed = cols_in[0, c].astype(jnp.float32)
        for k in range(1, COLS):
            summed = summed + cols_in[k, c].astype(jnp.float32)
        part[c] = summed.astype(jnp.bfloat16)
    to_twin = remote(part, part_in, pair_s, pair_r, 0, 0, twin)
    to_twin.start()

    @pl.when(z < OWNERS)
    def _():
        ring_in[z] = ring_out[z]

        def ring_wait(k, c):
            other = lax.rem(z + k, RING)
            remote(ring_in.at[other], ring_in.at[other], ring_s, ring_r, 0, other, tile_at(y, other, core)).wait_recv()
            return c

        lax.fori_loop(1, RING, ring_wait, 0)
        sums = []
        for c in range(3):
            summed = ring_in[0, c].astype(jnp.float32)
            for k in range(1, RING):
                summed = summed + ring_in[k, c].astype(jnp.float32)
            sums.append(summed)
        scale = probe_step * lax.rsqrt(sums[2] + 1.0)
        for c in range(2):
            grown[core, y, z, c] = (sums[c] * scale).astype(jnp.bfloat16)

        def grow_step(k, c):
            other = lax.rem(z + k, RING)
            own = grown.at[core, y, z]
            remote(own, own, grow_s, grow_r, other, z, tile_at(y, other, core)).start()
            return c

        lax.fori_loop(1, RING, grow_step, 0)

    to_twin.wait_recv()
    shares = []
    for c in range(2):
        shares.append((part[c].astype(jnp.float32) + part_in[c].astype(jnp.float32)) * 0.125)
    modulus = jnp.sqrt(shares[0] * shares[0] + shares[1] * shares[1])
    bound = 1.0 / jnp.maximum(modulus, 1.0)
    for c in range(2):
        settled[x, c] = (shares[c] * bound).astype(jnp.bfloat16)
    for k in xs:
        own = settled.at[x]
        remote(own, own, out_s, out_r, k, x, scan_at(k, yh)).start()

    def grow_wait(k, c):
        other = lax.rem(z + k, RING)

        @pl.when(other < OWNERS)
        def _():
            slot = grown.at[core, y, other]
            remote(slot, slot, grow_s, grow_r, 0, other, tile_at(y, other, core)).wait_recv()

        return c

    lax.fori_loop(1, RING, grow_wait, 0)
    for k in ys:
        own = grown.at[core, y]
        remote(own, own, wide_s, wide_r, k, y, tile_at(k, z, core)).start()

    for k in xs:
        slot = settled.at[k]
        remote(slot, slot, out_s, out_r, k, k, scan_at(k, yh)).wait_recv()
    for q in range(COLS):
        rows = pl.ds(q * 64, 64)
        for c in range(2):
            value = settled[q, c].astype(jnp.float32)
            cons_out[c, rows, :] = value
            dual_out[c, rows, :] = kept[c, rows, :] - value

    for k in ys:
        slot = grown.at[core, k]
        remote(slot, slot, wide_s, wide_r, k, k, tile_at(k, z, core)).wait_recv()
    own = grown.at[core]
    to_back = remote(own, own, back_s, back_r, 0, 0, sibling)
    to_back.start()
    slot = grown.at[1 - core]
    remote(slot, slot, back_s, back_r, 0, 0, sibling).wait_recv()
    for part_at in range(8):
        for k in range(OWNERS):
            rows = pl.ds(part_at * 32 + (k // 2) * 8, 8)
            cols = pl.ds((k % 2) * LANES, LANES)
            for c in range(2):
                step = grown[part_at // 4, part_at % 4, k, c].astype(jnp.float32)
                probe_out[c, rows, cols] = probe_ref[c, rows, cols] + step

    for copy in pushes:
        copy.wait_send()
    to_half.wait_send()
    to_twin.wait_send()
    to_back.wait_send()
    for k in ys:
        remote(half.at[k], run_in.at[y], run_s, run_r, k, y, tile_at(k, z, core)).wait_send()
        own = grown.at[core, y]
        remote(own, own, wide_s, wide_r, k, y, tile_at(k, z, core)).wait_send()
    for k in xs:
        remote(mine.at[k], cols_in.at[x], col_s, col_r, k, x, scan_at(k, yh)).wait_send()
        own = settled.at[x]
        remote(own, own, out_s, out_r, k, x, scan_at(k, yh)).wait_send()

    def ring_sent(k, c):
        other = lax.rem(z + k, RING)

        @pl.when(other < OWNERS)
        def _():
            remote(ring_out.at[other], ring_in.at[z], ring_s, ring_r, other, z, tile_at(y, other, core)).wait_send()

        @pl.when(z < OWNERS)
        def _():
            own = grown.at[core, y, z]
            remote(own, own, grow_s, grow_r, other, z, tile_at(y, other, core)).wait_send()

        return c

    lax.fori_loop(1, RING, ring_sent, 0)


def params(identity):
    return pltpu.CompilerParams(
        collective_id=identity, has_side_effects=True, vmem_limit_bytes=20 * 1024 * 1024
    )


def rim_buffers(channels):
    return [
        pltpu.VMEM((channels, TS, OVER), jnp.bfloat16),
        pltpu.VMEM((channels, OVER, TS), jnp.bfloat16),
        pltpu.VMEM((channels, OVER, OVER), jnp.bfloat16),
    ]


def copies_of(count):
    return [pltpu.SemaphoreType.DMA((count,)), pltpu.SemaphoreType.DMA((count,))]


WIDE = jax.ShapeDtypeStruct((2, 3, SPAN, LANES), jnp.float32)
FIELD = jax.ShapeDtypeStruct((2, TS, TS), jnp.float32)


def open_halo(cons):
    return pl.pallas_call(
        open_kernel, out_shape=WIDE, in_specs=[VMEM], out_specs=VMEM,
        scratch_shapes=rim_buffers(2) + rim_buffers(2) + copies_of(3),
        compiler_params=params(1), name="open_halo",
    )(cons)


def middle(center, rr, rb, rd, cons, dual):
    return pl.pallas_call(
        middle_kernel,
        out_shape=(FIELD, jax.ShapeDtypeStruct((TS, TS), jnp.float32), WIDE),
        in_specs=[VMEM] * 6, out_specs=(VMEM,) * 3,
        scratch_shapes=rim_buffers(3) + rim_buffers(2) + rim_buffers(2) + copies_of(6),
        compiler_params=params(2), name="middle",
    )(center, rr, rb, rd, cons, dual)


def close(center, rr, rb, rd, cons, dual, est, inv, psum, probe):
    buffer = lambda *shape: pltpu.VMEM(shape, jnp.bfloat16)
    scratch = rim_buffers(2) + [
        buffer(RUN, 3, 32, PS), buffer(RUN, 3, 32, PS), buffer(RUN, 3, 32, PS),
        buffer(OWNERS, 3, 8, LANES), buffer(RING, 3, 8, LANES), buffer(2, RUN, OWNERS, 2, 8, LANES),
        buffer(COLS, 2, 64, TS), buffer(COLS, 2, 64, TS), buffer(2, 64, TS), buffer(2, 64, TS),
        buffer(COLS, 2, 64, TS), pltpu.VMEM((2, TS, TS), jnp.float32),
    ]
    for count in (3, 1, RUN, RING, RING, RUN, 1, COLS, 1, COLS):
        scratch += copies_of(count)
    return pl.pallas_call(
        close_kernel, out_shape=(FIELD,) * 3, in_specs=[VMEM] * 10, out_specs=(VMEM,) * 3,
        scratch_shapes=scratch, compiler_params=params(3), name="close",
    )(center, rr, rb, rd, cons, dual, est, inv, psum, probe)


def shards(consensus, duals, probes, amplitudes, offsets, counts):
    m1, m2 = (jnp.asarray(table) for table in transform_tables())
    cons, dual, probe = consensus[0], duals[0, 0], probes[0]
    measured, corners = amplitudes[0, 0], offsets[0, 0]
    wide = open_halo(cons)
    center, rr, rb, rd, psum = patches(True, corners, counts, wide, probe, measured, m1, m2)
    est, inv, wide = middle(center, rr, rb, rd, cons, dual)
    center, rr, rb, rd, psum = patches(False, corners, counts, wide, probe, measured, m1, m2, psum)
    cons_new, dual_new, probe_new = close(center, rr, rb, rd, cons, dual, est, inv, psum, probe)
    return cons_new[None], dual_new[None, None], probe_new[None]


def solution(mesh):
    placed = (
        P("tile", None, None, None),
        P("scan", "tile", None, None, None),
        P("scan", None, None, None),
        P("scan", "tile", None, None, None),
        P("scan", "tile", None, None),
        P("scan", "tile"),
    )
    return jax.shard_map(
        shards,
        mesh=mesh,
        in_specs=placed,
        out_specs=(
            P("tile", None, None, None),
            P("scan", "tile", None, None, None),
            P("scan", None, None, None),
        ),
        check_vma=False,
    )
```

```python
import functools
import math

import jax
import jax.numpy as jnp
import ml_dtypes
import numpy as np
from jax import lax
from jax.experimental import pallas as pl
from jax.experimental.pallas import tpu as pltpu
from jax.sharding import PartitionSpec as P

PS = 256
TS = 256
OVER = 128
SPAN = TS + OVER
TGW = 4
SLOTS = 4
TILES = 96
RING = 12
RUN = 4
COLS = 4
OWNERS = 8
LANES = 128
penalty = 0.5
smoothing = 0.05
probe_step = 3.0
MESH = pl.DeviceIdType.MESH
VMEM = pl.BlockSpec(memory_space=pltpu.VMEM)
SMEM = pl.BlockSpec(memory_space=pltpu.SMEM)


def transform_tables():
    index = np.arange(PS, dtype=np.int64)
    angle = ((index[:, None] * index[None, :]) % PS).astype(np.float64) * (2.0 * math.pi / PS)
    scale = 1.0 / math.sqrt(PS)
    real = (np.cos(angle) * scale).astype(np.float32)
    imag = (-np.sin(angle) * scale).astype(np.float32)
    forward = np.block([[real, -imag], [imag, real]])
    return forward.astype(ml_dtypes.bfloat16), forward.T.astype(ml_dtypes.bfloat16)


def shifted_in(block, col, lane):
    amount = lax.rem(LANES - col, LANES)
    turned = [pltpu.roll(piece, amount, axis=1) for piece in block]
    keep = lane < LANES - col
    return [jnp.where(keep, turned[k], turned[k + 1]) for k in range(2)]


def shifted_out(left, right, col, lane):
    amount = lax.rem(col, LANES)
    left = pltpu.roll(left, amount, axis=1)
    right = pltpu.roll(right, amount, axis=1)
    past = lane >= col
    zero = jnp.zeros_like(left)
    return [jnp.where(past, left, zero), jnp.where(past, right, left), jnp.where(past, zero, right)]


def patches_kernel(first, *refs):
    if first:
        (off_ref, cnt_ref, near_ref, wide_ref, probe_ref, amp_ref, m1_ref, m2_ref,
         center_ref, rr_ref, rb_ref, acc_ref, inv_ref,
         tot_ref, e_ref, r_ref, win_ref, power_ref, weight_ref) = refs
    else:
        (off_ref, cnt_ref, wide_ref, probe_ref, amp_ref, m1_ref, m2_ref, prev_ref,
         center_ref, rr_ref, rb_ref, psum_ref,
         tot_ref, e_ref, r_ref, win_ref, acc_ref) = refs
    tot_ref[...] = jnp.zeros_like(tot_ref)
    if first:
        acc_ref[...] = jnp.zeros_like(acc_ref)
    else:
        acc_ref[...] = prev_ref[...]
    half = [pl.ds(0, LANES), pl.ds(LANES, LANES)]
    lane = lax.broadcasted_iota(jnp.int32, (PS, LANES), 1)

    def visit(slot, carry):
        row = off_ref[slot, 0]
        col = off_ref[slot, 1]
        real = shifted_in([wide_ref[0, k, pl.ds(row, PS), :] for k in range(3)], col, lane)
        imag = shifted_in([wide_ref[1, k, pl.ds(row, PS), :] for k in range(3)], col, lane)
        for h in range(2):
            wr, wi = real[h], imag[h]
            pr = probe_ref[0, :, half[h]]
            pi = probe_ref[1, :, half[h]]
            win_ref[0, :, half[h]] = wr
            win_ref[1, :, half[h]] = wi
            e_ref[:PS, half[h]] = (pr * wr - pi * wi).astype(jnp.bfloat16)
            e_ref[PS:, half[h]] = (pr * wi + pi * wr).astype(jnp.bfloat16)
        re = jnp.dot(m1_ref[:PS, :], e_ref[...], preferred_element_type=jnp.float32)
        im = jnp.dot(m1_ref[PS:, :], e_ref[...], preferred_element_type=jnp.float32)
        inner = jnp.concatenate([re.astype(jnp.bfloat16), im.astype(jnp.bfloat16)], 1)
        wave = jnp.dot(inner, m2_ref[...], preferred_element_type=jnp.float32)
        wr, wi = wave[:, :PS], wave[:, PS:]
        factor = amp_ref[slot].astype(jnp.float32) * lax.rsqrt(wr * wr + wi * wi + smoothing) - 1.0
        r_ref[:PS, :] = (wr * factor).astype(jnp.bfloat16)
        r_ref[PS:, :] = (wi * factor).astype(jnp.bfloat16)
        re = jnp.dot(m2_ref[:PS, :], r_ref[...], preferred_element_type=jnp.float32)
        im = jnp.dot(m2_ref[PS:, :], r_ref[...], preferred_element_type=jnp.float32)
        inner = jnp.concatenate([re.astype(jnp.bfloat16), im.astype(jnp.bfloat16)], 1)
        back = jnp.dot(inner, m1_ref[...], preferred_element_type=jnp.float32)
        terms = [[], []]
        for h in range(2):
            br = back[:, h * LANES:(h + 1) * LANES]
            bi = back[:, PS + h * LANES:PS + (h + 1) * LANES]
            pr = probe_ref[0, :, half[h]]
            pi = probe_ref[1, :, half[h]]
            wr = win_ref[0, :, half[h]]
            wi = win_ref[1, :, half[h]]
            terms[0].append(pr * br + pi * bi)
            terms[1].append(pr * bi - pi * br)
            acc_ref[0, :, half[h]] += wr * br + wi * bi
            acc_ref[1, :, half[h]] += wr * bi - wi * br
            acc_ref[2, :, half[h]] += wr * wr + wi * wi
        for c in range(2):
            out = shifted_out(terms[c][0], terms[c][1], col, lane)
            for k in range(3):
                tot_ref[c, k, pl.ds(row, PS), :] += out[k]
        return carry

    lax.fori_loop(0, cnt_ref[0, 0], visit, 0)
    for k in range(2):
        center_ref[:, :, half[k]] = tot_ref[:, k, :TS, :]
        rb_ref[k] = tot_ref[:, k, TS:, :].astype(jnp.bfloat16)
    rr_ref[...] = tot_ref[:, 2].astype(jnp.bfloat16)
    if first:
        weight_ref[...] = jnp.zeros_like(weight_ref)
        power_ref[...] = probe_ref[0] * probe_ref[0] + probe_ref[1] * probe_ref[1]

        def weigh(at, col, aside):
            out = shifted_out(power_ref[:, half[0]], power_ref[:, half[1]], col, lane)
            if aside:
                weight_ref[0, pl.ds(at, PS), :] += out[2]
            else:
                weight_ref[0, pl.ds(at, PS), :] += out[0]
                weight_ref[1, pl.ds(at, PS), :] += out[1]

        def own(slot, carry):
            weigh(off_ref[slot, 0] + TS, off_ref[slot, 1], False)
            return carry

        def left(slot, carry):
            weigh(near_ref[0, slot, 0] + TS, near_ref[0, slot, 1], True)
            return carry

        def above(slot, carry):
            weigh(near_ref[1, slot, 0], near_ref[1, slot, 1], False)
            return carry

        def corner(slot, carry):
            weigh(near_ref[2, slot, 0], near_ref[2, slot, 1], True)
            return carry

        lax.fori_loop(0, cnt_ref[0, 0], own, 0)
        lax.fori_loop(0, near_ref[0, SLOTS, 0], left, 0)
        lax.fori_loop(0, near_ref[1, SLOTS, 0], above, 0)
        lax.fori_loop(0, near_ref[2, SLOTS, 0], corner, 0)
        for k in range(2):
            inv_ref[:, half[k]] = 1.0 / (weight_ref[k, TS:2 * TS, :] + penalty)
    else:
        for part in range(8):
            rows = pl.ds(part * 32, 32)
            for c in range(3):
                psum_ref[part // 4, part % 4, c] = acc_ref[c, rows, :].astype(jnp.bfloat16)


def patches(first, corners, count, wide, probe, measured, m1, m2, near=None, prev=None):
    shape = jax.ShapeDtypeStruct
    out_shape = [
        shape((2, TS, TS), jnp.float32),
        shape((2, SPAN, OVER), jnp.bfloat16),
        shape((2, 2, OVER, OVER), jnp.bfloat16),
    ]
    scratch = [
        pltpu.VMEM((2, 3, SPAN, LANES), jnp.float32),
        pltpu.VMEM((2 * PS, PS), jnp.bfloat16),
        pltpu.VMEM((2 * PS, PS), jnp.bfloat16),
        pltpu.VMEM((2, PS, PS), jnp.float32),
    ]
    if first:
        args = [corners, count, near, wide, probe, measured, m1, m2]
        scalars = 3
        out_shape += [shape((3, PS, PS), jnp.float32), shape((TS, TS), jnp.float32)]
        scratch += [pltpu.VMEM((PS, PS), jnp.float32), pltpu.VMEM((2, TS + SPAN, LANES), jnp.float32)]
    else:
        args = [corners, count, wide, probe, measured, m1, m2, prev]
        scalars = 2
        out_shape += [shape((2, RUN, 3, 32, PS), jnp.bfloat16)]
        scratch += [pltpu.VMEM((3, PS, PS), jnp.float32)]
    return pl.pallas_call(
        functools.partial(patches_kernel, first),
        out_shape=tuple(out_shape),
        in_specs=[SMEM] * scalars + [VMEM] * (len(args) - scalars),
        out_specs=(VMEM,) * len(out_shape),
        scratch_shapes=scratch,
        compiler_params=pltpu.CompilerParams(vmem_limit_bytes=28 * 1024 * 1024),
        name="patches",
    )(*args)


def moved(t, by):
    return lax.rem(t + (by + TILES), TILES)


def remote(src, dst, sends, recvs, at, slot, target):
    return pltpu.make_async_remote_copy(
        src_ref=src, dst_ref=dst, send_sem=sends.at[at], recv_sem=recvs.at[slot],
        device_id=target, device_id_type=MESH,
    )


def greet(targets):
    barrier = pltpu.get_barrier_semaphore()
    for target in targets:
        pl.semaphore_signal(barrier, inc=1, device_id=target, device_id_type=MESH)
    pl.semaphore_wait(barrier, len(targets))


def start_if(flag, *copies):
    @pl.when(flag)
    def _():
        for copy in copies:
            copy.start()


def wait_if(flag, *copies):
    @pl.when(flag)
    def _():
        for copy in copies:
            copy.wait_recv()


def sent_if(flag, *copies):
    @pl.when(flag)
    def _():
        for copy in copies:
            copy.wait_send()


def clear_if(flag, *refs):
    @pl.when(flag)
    def _():
        for ref in refs:
            ref[...] = jnp.zeros_like(ref)


def sides(t):
    column = lax.rem(t, TGW)
    return column > 0, column < TGW - 1, t >= TGW, t < TILES - TGW


def block(at):
    return pl.ds(at * OVER, OVER)


class Pull:
    def __init__(self, t, quads, below_in, right_in, corner_in, sends, recvs, base):
        self.left, self.right, self.above, self.below = sides(t)
        self.refs = quads, below_in, right_in, corner_in
        up, back = {"tile": moved(t, -TGW)}, {"tile": moved(t, -1)}
        make = lambda src, dst, at, to: remote(src, dst, sends, recvs, at, at, to)
        self.up = [[make(quads.at[b, c], below_in.at[b, c], base + 2 * b + c, up) for c in range(2)] for b in range(2)]
        self.side = [[make(quads.at[2 * a, c], right_in.at[a, c], base + 4 + 2 * a + c, back) for c in range(2)] for a in range(2)]
        self.relay = [make(below_in.at[0, c], corner_in.at[c], base + 8 + c, back) for c in range(2)]

    def clear(self):
        quads, below_in, right_in, corner_in = self.refs
        clear_if(jnp.logical_not(self.right), right_in, corner_in)
        clear_if(jnp.logical_not(self.below), below_in)

    def offer(self, value, c, a, b, wide_ref):
        rounded = value.astype(jnp.bfloat16)
        wide_ref[c, b, block(a), :] = rounded.astype(jnp.float32)
        if not (a and b):
            self.refs[0][2 * a + b, c] = rounded

    def begin(self, c, a, b):
        if a == 0:
            start_if(self.above, self.up[b][c])
        if b == 0:
            start_if(self.left, self.side[a][c])

    def finish(self, wide_ref):
        quads, below_in, right_in, corner_in = self.refs
        for c in range(2):
            wait_if(self.below, self.up[0][c])
            start_if(self.left, self.relay[c])
        for c in range(2):
            wait_if(self.below, self.up[1][c])
            wait_if(self.right, self.side[0][c], self.side[1][c])
            for a in range(2):
                wide_ref[c, 2, block(a), :] = right_in[a, c].astype(jnp.float32)
            for b in range(2):
                wide_ref[c, b, TS:, :] = below_in[b, c].astype(jnp.float32)
        for c in range(2):
            wait_if(self.right, self.relay[c])
            wide_ref[c, 2, TS:, :] = corner_in[c].astype(jnp.float32)
        for c in range(2):
            sent_if(self.above, self.up[0][c], self.up[1][c])
            sent_if(self.left, self.side[0][c], self.side[1][c], self.relay[c])


QUADRANTS = ((1, 1), (1, 0), (0, 1), (0, 0))


def open_kernel(cons_ref, corner_ref, count_ref, wide_ref, near_ref,
                quads, below_in, right_in, corner_in, note, note_in, sends, recvs):
    t = lax.axis_index("tile")
    pull = Pull(t, quads, below_in, right_in, corner_in, sends, recvs, 0)
    pull.clear()
    note[...] = jnp.zeros_like(note)
    note[0:SLOTS, 0:2] = corner_ref[...]
    note[SLOTS:SLOTS + 1, 0:1] = count_ref[...]
    for a, b in QUADRANTS:
        for c in range(2):
            pull.offer(cons_ref[c, block(a), block(b)], c, a, b, wide_ref)
    greet([{"tile": moved(t, by)} for by in (1, TGW, -1, -TGW, -TGW - 1)])
    notes = [
        remote(note, note_in.at[k], sends, recvs, 10 + k, 10 + k, {"tile": moved(t, by)})
        for k, by in enumerate((1, TGW, TGW + 1))
    ]
    for b in range(2):
        for c in range(2):
            pull.begin(c, 0, b)
    for c in range(2):
        pull.begin(c, 1, 0)
    for copy in notes:
        copy.start()
    pull.finish(wide_ref)
    for copy in notes:
        copy.wait()
    for k, flag in enumerate((pull.left, pull.above, jnp.logical_and(pull.left, pull.above))):
        near_ref[k] = note_in[k] * jnp.where(flag, 1, 0)


def middle_kernel(center_ref, rr, rb, inv_ref, cons_ref, dual_ref, est_ref, wide_ref,
                  left_in, above_in, lowered, quads, below_in, right_in, corner_in, sends, recvs):
    t = lax.axis_index("tile")
    left, right, above, below = sides(t)
    pull = Pull(t, quads, below_in, right_in, corner_in, sends, recvs, 6)
    pull.clear()
    clear_if(jnp.logical_not(left), left_in)
    clear_if(jnp.logical_not(above), above_in)
    on, down = {"tile": moved(t, 1)}, {"tile": moved(t, TGW)}
    make = lambda src, dst, at, to: remote(src, dst, sends, recvs, at, at, to)
    push_on = [make(rr.at[c], left_in.at[c], c, on) for c in range(2)]
    push_far = [make(rb.at[1, c], above_in.at[1, c], 2 + c, down) for c in range(2)]
    push_low = [make(lowered.at[c], above_in.at[0, c], 4 + c, down) for c in range(2)]
    greet([{"tile": moved(t, by)} for by in (1, TGW, -1, -TGW)])

    def push(c):
        start_if(right, push_on[c])
        start_if(below, push_far[c])

    def relay(c):
        wait_if(left, push_on[c])
        lowered[c] = (rb[0, c].astype(jnp.float32) + left_in[c, TS:, :].astype(jnp.float32)).astype(jnp.bfloat16)
        start_if(below, push_low[c])

    def update(c, a, b):
        rows, cols = block(a), block(b)
        total = center_ref[c, rows, cols]
        if a == 0:
            total = total + above_in[b, c].astype(jnp.float32)
        if b == 0:
            total = total + left_in[c, rows, :].astype(jnp.float32)
        value = cons_ref[c, rows, cols] + (total - penalty * dual_ref[c, rows, cols]) * inv_ref[rows, cols]
        est_ref[c, rows, cols] = value
        pull.offer(value, c, a, b, wide_ref)
        pull.begin(c, a, b)

    push(0)
    update(0, 1, 1)
    relay(0)
    push(1)
    for c in range(2):
        if c == 1:
            update(1, 1, 1)
            relay(1)
        update(c, 1, 0)
        wait_if(above, push_far[c])
        update(c, 0, 1)
        wait_if(above, push_low[c])
        update(c, 0, 0)
    pull.finish(wide_ref)
    for c in range(2):
        sent_if(right, push_on[c])
        sent_if(below, push_far[c], push_low[c])


def close_kernel(center_ref, rr, rb, cons_ref, dual_ref, est_ref, inv_ref, psum, probe_ref,
                 cons_out, dual_out, probe_out,
                 left_in, above_in, lowered, half_in, half, run_in, ring_out, ring_in, grown,
                 mine, cols_in, part, part_in, settled, kept,
                 rim_s, rim_r, half_s, half_r, run_s, run_r, ring_s, ring_r, grow_s, grow_r,
                 wide_s, wide_r, back_s, back_r, col_s, col_r, pair_s, pair_r, out_s, out_r):
    t = lax.axis_index("tile")
    left, right, above, below = sides(t)
    core = lax.rem(t, 2)
    z = lax.rem(lax.div(t, 2), RING)
    y = lax.div(t, 2 * RING)
    scan = lax.axis_index("scan")
    yh = lax.rem(scan, 2)
    x = lax.div(scan, 2)
    tile_at = lambda y_, z_, c_: {"tile": (y_ * RING + z_) * 2 + c_}
    scan_at = lambda x_, h_: {"scan": x_ * 2 + h_}
    ys = [lax.rem(y + k, RUN) for k in range(1, RUN)]
    xs = [lax.rem(x + k, COLS) for k in range(1, COLS)]
    sibling = tile_at(y, z, 1 - core)
    twin = scan_at(x, 1 - yh)
    on, down = {"tile": moved(t, 1)}, {"tile": moved(t, TGW)}
    push_on = remote(rr, left_in, rim_s, rim_r, 0, 0, on)
    push_far = remote(rb.at[1], above_in.at[1], rim_s, rim_r, 1, 1, down)
    push_low = remote(lowered, above_in.at[0], rim_s, rim_r, 2, 2, down)
    to_half = remote(psum.at[1 - core], half_in, half_s, half_r, 0, 0, sibling)

    clear_if(jnp.logical_not(left), left_in)
    clear_if(jnp.logical_not(above), above_in)
    greet([{"tile": moved(t, by)} for by in (-1, -TGW)] + [sibling, twin]
          + [tile_at(k, z, core) for k in ys] + [scan_at(k, yh) for k in xs]
          + [tile_at(y, lax.rem(z + k, RING), core) for k in range(1, RING)])

    start_if(right, push_on)
    start_if(below, push_far)
    to_half.start()

    def cross(n, k, at, other):
        return remote(mine.at[n, k], cols_in.at[n, at], col_s, col_r, (n, k), (n, at), scan_at(other, yh))

    def pair(n):
        return remote(part.at[n], part_in.at[n], pair_s, pair_r, n, n, twin)

    def spread(n, k, at, other):
        own = settled.at[n, at]
        return remote(own, own, out_s, out_r, (n, k), (n, at), scan_at(other, yh))

    def update(n):
        a, b = QUADRANTS[n]
        rows, cols = block(a), block(b)
        inv = inv_ref[rows, cols]
        for c in range(2):
            total = center_ref[c, rows, cols]
            if a == 0:
                total = total + above_in[b, c].astype(jnp.float32)
            if b == 0:
                total = total + left_in[c, rows, :].astype(jnp.float32)
            dual = dual_ref[c, rows, cols]
            estimate = est_ref[c, rows, cols]
            value = estimate + (total + penalty * (cons_ref[c, rows, cols] - dual - estimate)) * inv + dual
            kept[c, rows, cols] = value
            value = value.astype(jnp.bfloat16)
            for q in range(COLS):
                mine[n, q, c] = value[q * 32:(q + 1) * 32]
        for k in xs:
            cross(n, k, x, k).start()

    def combine(n):
        for k in xs:
            cross(n, k, k, k).wait_recv()
        cols_in[n, x] = mine[n, x]
        for c in range(2):
            summed = cols_in[n, 0, c].astype(jnp.float32)
            for k in range(1, COLS):
                summed = summed + cols_in[n, k, c].astype(jnp.float32)
            part[n, c] = summed.astype(jnp.bfloat16)
        pair(n).start()

    def settle(n):
        pair(n).wait_recv()
        shares = [(part[n, c].astype(jnp.float32) + part_in[n, c].astype(jnp.float32)) * 0.125 for c in range(2)]
        modulus = jnp.sqrt(shares[0] * shares[0] + shares[1] * shares[1])
        bound = 1.0 / jnp.maximum(modulus, 1.0)
        for c in range(2):
            settled[n, x, c] = (shares[c] * bound).astype(jnp.bfloat16)
        for k in xs:
            spread(n, k, x, k).start()

    def give(n):
        a, b = QUADRANTS[n]
        for k in xs:
            spread(n, k, k, k).wait_recv()
        for q in range(COLS):
            rows, cols = pl.ds(a * OVER + q * 32, 32), block(b)
            for c in range(2):
                value = settled[n, q, c].astype(jnp.float32)
                cons_out[c, rows, cols] = value
                dual_out[c, rows, cols] = kept[c, rows, cols] - value

    def run_copy(k, at):
        return remote(half.at[k], run_in.at[at], run_s, run_r, k, at, tile_at(k, z, core))

    def ring_copy(other, at):
        return remote(ring_out.at[other], ring_in.at[at], ring_s, ring_r, other, at, tile_at(y, other, core))

    def grow_copy(other, at):
        own = grown.at[core, y, at]
        return remote(own, own, grow_s, grow_r, other, at, tile_at(y, other, core))

    def wide_copy(k, at):
        own = grown.at[core, at]
        return remote(own, own, wide_s, wide_r, k, at, tile_at(k, z, core))

    def back_copy(at):
        own = grown.at[at]
        return remote(own, own, back_s, back_r, 0, 0, sibling)

    def around(step):
        def body(k, carry):
            step(lax.rem(z + k, RING))
            return carry

        lax.fori_loop(1, RING, body, 0)

    def probe_run():
        to_half.wait_recv()
        for q in range(RUN):
            half[q] = (psum[core, q].astype(jnp.float32) + half_in[q].astype(jnp.float32)).astype(jnp.bfloat16)
        for k in ys:
            run_copy(k, y).start()

    def probe_ring():
        for k in ys:
            run_copy(k, k).wait_recv()
        run_in[y] = half[y]
        for c in range(3):
            summed = run_in[0, c].astype(jnp.float32)
            for k in range(1, RUN):
                summed = summed + run_in[k, c].astype(jnp.float32)
            summed = summed.astype(jnp.bfloat16)
            for k in range(OWNERS):
                ring_out[k, c] = summed[(k // 2) * 8:(k // 2) * 8 + 8, (k % 2) * LANES:(k % 2 + 1) * LANES]

        def step(other):
            @pl.when(other < OWNERS)
            def _():
                ring_copy(other, z).start()

        around(step)

    def probe_grow():
        @pl.when(z < OWNERS)
        def _():
            ring_in[z] = ring_out[z]
            around(lambda other: ring_copy(z, other).wait_recv())
            sums = []
            for c in range(3):
                summed = ring_in[0, c].astype(jnp.float32)
                for k in range(1, RING):
                    summed = summed + ring_in[k, c].astype(jnp.float32)
                sums.append(summed)
            scale = probe_step * lax.rsqrt(sums[2] + 1.0)
            for c in range(2):
                grown[core, y, z, c] = (sums[c] * scale).astype(jnp.bfloat16)
            around(lambda other: grow_copy(other, z).start())

    def probe_wide():
        def step(other):
            @pl.when(other < OWNERS)
            def _():
                grow_copy(other, other).wait_recv()

        around(step)
        for k in ys:
            wide_copy(k, y).start()

    def probe_back():
        for k in ys:
            wide_copy(k, k).wait_recv()
        back_copy(core).start()

    def probe_give():
        back_copy(1 - core).wait_recv()
        for part_at in range(8):
            for k in range(OWNERS):
                rows = pl.ds(part_at * 32 + (k // 2) * 8, 8)
                cols = pl.ds((k % 2) * LANES, LANES)
                for c in range(2):
                    step = grown[part_at // 4, part_at % 4, k, c].astype(jnp.float32)
                    probe_out[c, rows, cols] = probe_ref[c, rows, cols] + step

    update(0)
    probe_run()
    wait_if(left, push_on)
    for c in range(2):
        lowered[c] = (rb[0, c].astype(jnp.float32) + left_in[c, TS:, :].astype(jnp.float32)).astype(jnp.bfloat16)
    start_if(below, push_low)
    update(1)
    combine(0)
    probe_ring()
    wait_if(above, push_far)
    update(2)
    settle(0)
    combine(1)
    wait_if(above, push_low)
    update(3)
    combine(2)
    settle(1)
    probe_grow()
    combine(3)
    settle(2)
    probe_wide()
    settle(3)
    give(0)
    give(1)
    probe_back()
    give(2)
    give(3)
    probe_give()

    sent_if(right, push_on)
    sent_if(below, push_far, push_low)
    to_half.wait_send()
    back_copy(core).wait_send()
    for k in ys:
        run_copy(k, y).wait_send()
        wide_copy(k, y).wait_send()
    for n in range(4):
        pair(n).wait_send()
        for k in xs:
            cross(n, k, x, k).wait_send()
            spread(n, k, x, k).wait_send()

    def sent(other):
        @pl.when(other < OWNERS)
        def _():
            ring_copy(other, z).wait_send()

        @pl.when(z < OWNERS)
        def _():
            grow_copy(other, z).wait_send()

    around(sent)


def params(identity):
    return pltpu.CompilerParams(
        collective_id=identity, has_side_effects=True, vmem_limit_bytes=20 * 1024 * 1024
    )


def buffer(*shape):
    return pltpu.VMEM(shape, jnp.bfloat16)


def pull_buffers():
    return [
        buffer(3, 2, OVER, OVER), buffer(2, 2, OVER, OVER), buffer(2, 2, OVER, OVER), buffer(2, OVER, OVER)
    ]


def copies_of(*count):
    return [pltpu.SemaphoreType.DMA(count), pltpu.SemaphoreType.DMA(count)]


WIDE = jax.ShapeDtypeStruct((2, 3, SPAN, LANES), jnp.float32)
FIELD = jax.ShapeDtypeStruct((2, TS, TS), jnp.float32)


def open_halo(cons, corners, counts):
    return pl.pallas_call(
        open_kernel, out_shape=(WIDE, jax.ShapeDtypeStruct((3, 8, LANES), jnp.int32)),
        in_specs=[VMEM] * 3, out_specs=(VMEM,) * 2,
        scratch_shapes=pull_buffers() + [pltpu.VMEM((8, LANES), jnp.int32), pltpu.VMEM((3, 8, LANES), jnp.int32)]
        + copies_of(13),
        compiler_params=params(1), name="open_halo",
    )(cons, corners, counts)


def middle(center, rr, rb, inv, cons, dual):
    return pl.pallas_call(
        middle_kernel,
        out_shape=(FIELD, WIDE),
        in_specs=[VMEM] * 6, out_specs=(VMEM,) * 2,
        scratch_shapes=[buffer(2, SPAN, OVER), buffer(2, 2, OVER, OVER), buffer(2, OVER, OVER)]
        + pull_buffers() + copies_of(16),
        compiler_params=params(2), name="middle",
    )(center, rr, rb, inv, cons, dual)


def close(center, rr, rb, cons, dual, est, inv, psum, probe):
    scratch = [
        buffer(2, SPAN, OVER), buffer(2, 2, OVER, OVER), buffer(2, OVER, OVER),
        buffer(RUN, 3, 32, PS), buffer(RUN, 3, 32, PS), buffer(RUN, 3, 32, PS),
        buffer(OWNERS, 3, 8, LANES), buffer(RING, 3, 8, LANES), buffer(2, RUN, OWNERS, 2, 8, LANES),
        buffer(4, COLS, 2, 32, LANES), buffer(4, COLS, 2, 32, LANES), buffer(4, 2, 32, LANES),
        buffer(4, 2, 32, LANES), buffer(4, COLS, 2, 32, LANES), pltpu.VMEM((2, TS, TS), jnp.float32),
    ]
    for count in ((3,), (1,), (RUN,), (RING,), (RING,), (RUN,), (1,), (4, COLS), (4,), (4, COLS)):
        scratch += copies_of(*count)
    return pl.pallas_call(
        close_kernel, out_shape=(FIELD,) * 3, in_specs=[VMEM] * 9, out_specs=(VMEM,) * 3,
        scratch_shapes=scratch, compiler_params=params(3), name="close",
    )(center, rr, rb, cons, dual, est, inv, psum, probe)


def shards(consensus, duals, probes, amplitudes, offsets, counts):
    m1, m2 = (jnp.asarray(table) for table in transform_tables())
    cons, dual, probe = consensus[0], duals[0, 0], probes[0]
    measured, corners = amplitudes[0, 0], offsets[0, 0]
    wide, near = open_halo(cons, corners, counts)
    center, rr, rb, psum, inv = patches(True, corners, counts, wide, probe, measured, m1, m2, near=near)
    est, wide = middle(center, rr, rb, inv, cons, dual)
    center, rr, rb, psum = patches(False, corners, counts, wide, probe, measured, m1, m2, prev=psum)
    cons_new, dual_new, probe_new = close(center, rr, rb, cons, dual, est, inv, psum, probe)
    return cons_new[None], dual_new[None, None], probe_new[None]


def solution(mesh):
    placed = (
        P("tile", None, None, None),
        P("scan", "tile", None, None, None),
        P("scan", None, None, None),
        P("scan", "tile", None, None, None),
        P("scan", "tile", None, None),
        P("scan", "tile"),
    )
    return jax.shard_map(
        shards,
        mesh=mesh,
        in_specs=placed,
        out_specs=(
            P("tile", None, None, None),
            P("scan", "tile", None, None, None),
            P("scan", None, None, None),
        ),
        check_vma=False,
    )
```

```python
import functools
import math

import jax
import jax.numpy as jnp
import ml_dtypes
import numpy as np
from jax import lax
from jax.experimental import pallas as pl
from jax.experimental.pallas import tpu as pltpu
from jax.sharding import PartitionSpec as P

PS = 256
TS = 256
OVER = 128
SPAN = TS + OVER
TGW = 4
SLOTS = 4
TILES = 96
RING = 12
RUN = 4
COLS = 4
LAPS = 3
LANES = 128
penalty = 0.5
smoothing = 0.05
probe_step = 3.0
MESH = pl.DeviceIdType.MESH
VMEM = pl.BlockSpec(memory_space=pltpu.VMEM)
SMEM = pl.BlockSpec(memory_space=pltpu.SMEM)


def transform_tables():
    index = np.arange(PS, dtype=np.int64)
    angle = ((index[:, None] * index[None, :]) % PS).astype(np.float64) * (2.0 * math.pi / PS)
    scale = 1.0 / math.sqrt(PS)
    real = (np.cos(angle) * scale).astype(np.float32)
    imag = (-np.sin(angle) * scale).astype(np.float32)
    forward = np.block([[real, -imag], [imag, real]])
    return forward.astype(ml_dtypes.bfloat16), forward.T.astype(ml_dtypes.bfloat16)


def shifted_in(block, col, lane):
    amount = lax.rem(LANES - col, LANES)
    turned = [pltpu.roll(piece, amount, axis=1) for piece in block]
    keep = lane < LANES - col
    return [jnp.where(keep, turned[k], turned[k + 1]) for k in range(2)]


def shifted_out(left, right, col, lane):
    amount = lax.rem(col, LANES)
    left = pltpu.roll(left, amount, axis=1)
    right = pltpu.roll(right, amount, axis=1)
    past = lane >= col
    zero = jnp.zeros_like(left)
    return [jnp.where(past, left, zero), jnp.where(past, right, left), jnp.where(past, zero, right)]


def patches_kernel(first, *refs):
    if first:
        (off_ref, cnt_ref, near_ref, wide_ref, probe_ref, amp_ref, m1_ref, m2_ref,
         center_ref, rr_ref, rb_ref, acc_ref, inv_ref,
         tot_ref, e_ref, r_ref, win_ref, power_ref, weight_ref) = refs
    else:
        (off_ref, cnt_ref, wide_ref, probe_ref, amp_ref, m1_ref, m2_ref, prev_ref,
         center_ref, rr_ref, rb_ref, psum_ref,
         tot_ref, e_ref, r_ref, win_ref, acc_ref) = refs
    tot_ref[...] = jnp.zeros_like(tot_ref)
    if first:
        acc_ref[...] = jnp.zeros_like(acc_ref)
    else:
        acc_ref[...] = prev_ref[...]
    half = [pl.ds(0, LANES), pl.ds(LANES, LANES)]
    lane = lax.broadcasted_iota(jnp.int32, (PS, LANES), 1)

    def visit(slot, carry):
        row = off_ref[0, slot]
        col = off_ref[1, slot]
        real = shifted_in([wide_ref[0, k, pl.ds(row, PS), :] for k in range(3)], col, lane)
        imag = shifted_in([wide_ref[1, k, pl.ds(row, PS), :] for k in range(3)], col, lane)
        for h in range(2):
            wr, wi = real[h], imag[h]
            pr = probe_ref[0, :, half[h]]
            pi = probe_ref[1, :, half[h]]
            win_ref[0, :, half[h]] = wr
            win_ref[1, :, half[h]] = wi
            e_ref[:PS, half[h]] = (pr * wr - pi * wi).astype(jnp.bfloat16)
            e_ref[PS:, half[h]] = (pr * wi + pi * wr).astype(jnp.bfloat16)
        re = jnp.dot(m1_ref[:PS, :], e_ref[...], preferred_element_type=jnp.float32)
        im = jnp.dot(m1_ref[PS:, :], e_ref[...], preferred_element_type=jnp.float32)
        inner = jnp.concatenate([re.astype(jnp.bfloat16), im.astype(jnp.bfloat16)], 1)
        wave = jnp.dot(inner, m2_ref[...], preferred_element_type=jnp.float32)
        wr, wi = wave[:, :PS], wave[:, PS:]
        factor = amp_ref[slot].astype(jnp.float32) * lax.rsqrt(wr * wr + wi * wi + smoothing) - 1.0
        r_ref[:PS, :] = (wr * factor).astype(jnp.bfloat16)
        r_ref[PS:, :] = (wi * factor).astype(jnp.bfloat16)
        re = jnp.dot(m2_ref[:PS, :], r_ref[...], preferred_element_type=jnp.float32)
        im = jnp.dot(m2_ref[PS:, :], r_ref[...], preferred_element_type=jnp.float32)
        inner = jnp.concatenate([re.astype(jnp.bfloat16), im.astype(jnp.bfloat16)], 1)
        back = jnp.dot(inner, m1_ref[...], preferred_element_type=jnp.float32)
        terms = [[], []]
        for h in range(2):
            br = back[:, h * LANES:(h + 1) * LANES]
            bi = back[:, PS + h * LANES:PS + (h + 1) * LANES]
            pr = probe_ref[0, :, half[h]]
            pi = probe_ref[1, :, half[h]]
            wr = win_ref[0, :, half[h]]
            wi = win_ref[1, :, half[h]]
            terms[0].append(pr * br + pi * bi)
            terms[1].append(pr * bi - pi * br)
            acc_ref[0, :, half[h]] += wr * br + wi * bi
            acc_ref[1, :, half[h]] += wr * bi - wi * br
            acc_ref[2, :, half[h]] += wr * wr + wi * wi
        for c in range(2):
            out = shifted_out(terms[c][0], terms[c][1], col, lane)
            for k in range(3):
                tot_ref[c, k, pl.ds(row, PS), :] += out[k]
        return carry

    lax.fori_loop(0, cnt_ref[0, 0], visit, 0)
    for k in range(2):
        center_ref[:, :, half[k]] = tot_ref[:, k, :TS, :]
        rb_ref[k] = tot_ref[:, k, TS:, :].astype(jnp.bfloat16)
    rr_ref[...] = tot_ref[:, 2].astype(jnp.bfloat16)
    if first:
        weight_ref[...] = jnp.zeros_like(weight_ref)
        power_ref[...] = probe_ref[0] * probe_ref[0] + probe_ref[1] * probe_ref[1]

        def weigh(at, col, aside):
            out = shifted_out(power_ref[:, half[0]], power_ref[:, half[1]], col, lane)
            if aside:
                weight_ref[0, pl.ds(at, PS), :] += out[2]
            else:
                weight_ref[0, pl.ds(at, PS), :] += out[0]
                weight_ref[1, pl.ds(at, PS), :] += out[1]

        def own(slot, carry):
            weigh(off_ref[0, slot] + TS, off_ref[1, slot], False)
            return carry

        def left(slot, carry):
            weigh(near_ref[0, 0, slot] + TS, near_ref[0, 1, slot], True)
            return carry

        def above(slot, carry):
            weigh(near_ref[1, 0, slot], near_ref[1, 1, slot], False)
            return carry

        def corner(slot, carry):
            weigh(near_ref[2, 0, slot], near_ref[2, 1, slot], True)
            return carry

        lax.fori_loop(0, cnt_ref[0, 0], own, 0)
        lax.fori_loop(0, near_ref[0, 2, 0], left, 0)
        lax.fori_loop(0, near_ref[1, 2, 0], above, 0)
        lax.fori_loop(0, near_ref[2, 2, 0], corner, 0)
        for k in range(2):
            inv_ref[:, half[k]] = 1.0 / (weight_ref[k, TS:2 * TS, :] + penalty)
    else:
        for part in range(8):
            rows = pl.ds(part * 32, 32)
            for c in range(3):
                psum_ref[part // 4, part % 4, c] = acc_ref[c, rows, :].astype(jnp.bfloat16)


def busy(microseconds):
    return pl.CostEstimate(flops=microseconds * 1_000_000_000, bytes_accessed=microseconds * 3_000_000, transcendentals=0)


def patches(first, corners, count, wide, probe, measured, m1, m2, near=None, prev=None):
    shape = jax.ShapeDtypeStruct
    out_shape = [
        shape((2, TS, TS), jnp.float32),
        shape((2, SPAN, OVER), jnp.bfloat16),
        shape((2, 2, OVER, OVER), jnp.bfloat16),
    ]
    scratch = [
        pltpu.VMEM((2, 3, SPAN, LANES), jnp.float32),
        pltpu.VMEM((2 * PS, PS), jnp.bfloat16),
        pltpu.VMEM((2 * PS, PS), jnp.bfloat16),
        pltpu.VMEM((2, PS, PS), jnp.float32),
    ]
    if first:
        args = [corners, count, near, wide, probe, measured, m1, m2]
        scalars = 3
        out_shape += [shape((3, PS, PS), jnp.float32), shape((TS, TS), jnp.float32)]
        scratch += [pltpu.VMEM((PS, PS), jnp.float32), pltpu.VMEM((2, TS + SPAN, LANES), jnp.float32)]
    else:
        args = [corners, count, wide, probe, measured, m1, m2, prev]
        scalars = 2
        out_shape += [shape((2, RUN, 3, 32, PS), jnp.bfloat16)]
        scratch += [pltpu.VMEM((3, PS, PS), jnp.float32)]
    return pl.pallas_call(
        functools.partial(patches_kernel, first),
        out_shape=tuple(out_shape),
        in_specs=[SMEM] * scalars + [VMEM] * (len(args) - scalars),
        out_specs=(VMEM,) * len(out_shape),
        scratch_shapes=scratch,
        compiler_params=pltpu.CompilerParams(vmem_limit_bytes=16 * 1024 * 1024),
        name="patches", cost_estimate=busy(8),
    )(*args)


def moved(t, by):
    return lax.rem(t + (by + TILES), TILES)


def remote(src, dst, sends, recvs, at, slot, target):
    return pltpu.make_async_remote_copy(
        src_ref=src, dst_ref=dst, send_sem=sends.at[at], recv_sem=recvs.at[slot],
        device_id=target, device_id_type=MESH,
    )


def greet(targets):
    barrier = pltpu.get_barrier_semaphore()
    for target in targets:
        pl.semaphore_signal(barrier, inc=1, device_id=target, device_id_type=MESH)
    pl.semaphore_wait(barrier, len(targets))


def start_if(flag, *copies):
    @pl.when(flag)
    def _():
        for copy in copies:
            copy.start()


def wait_if(flag, *copies):
    @pl.when(flag)
    def _():
        for copy in copies:
            copy.wait_recv()


def sent_if(flag, *copies):
    @pl.when(flag)
    def _():
        for copy in copies:
            copy.wait_send()


def clear_if(flag, *refs):
    @pl.when(flag)
    def _():
        for ref in refs:
            ref[...] = jnp.zeros_like(ref)


def sides(t):
    column = lax.rem(t, TGW)
    return column > 0, column < TGW - 1, t >= TGW, t < TILES - TGW


def block(at):
    return pl.ds(at * OVER, OVER)


class Pull:
    def __init__(self, t, quads, below_in, right_in, corner_in, sends, recvs, base):
        self.left, self.right, self.above, self.below = sides(t)
        self.gives = jnp.logical_and(self.left, self.above)
        self.takes = jnp.logical_and(self.right, self.below)
        self.refs = quads, below_in, right_in, corner_in
        up, back, far = ({"tile": moved(t, by)} for by in (-TGW, -1, -TGW - 1))
        make = lambda src, dst, at, to: remote(src, dst, sends, recvs, at, at, to)
        self.up = [[make(quads.at[b, c], below_in.at[b, c], base + 2 * b + c, up) for c in range(2)] for b in range(2)]
        self.side = [[make(quads.at[2 * a, c], right_in.at[a, c], base + 4 + 2 * a + c, back) for c in range(2)] for a in range(2)]
        self.corner = [make(quads.at[0, c], corner_in.at[c], base + 8 + c, far) for c in range(2)]

    def clear(self):
        quads, below_in, right_in, corner_in = self.refs
        clear_if(jnp.logical_not(self.right), right_in)
        clear_if(jnp.logical_not(self.below), below_in)
        clear_if(jnp.logical_not(self.takes), corner_in)

    def offer(self, value, c, a, b, wide_ref):
        rounded = value.astype(jnp.bfloat16)
        wide_ref[c, b, block(a), :] = rounded.astype(jnp.float32)
        if not (a and b):
            self.refs[0][2 * a + b, c] = rounded

    def begin(self, c, a, b):
        if a == 0 and b == 0:
            start_if(self.gives, self.corner[c])
        if a == 0:
            start_if(self.above, self.up[b][c])
        if b == 0:
            start_if(self.left, self.side[a][c])

    def finish(self, wide_ref):
        quads, below_in, right_in, corner_in = self.refs
        for c in range(2):
            wait_if(self.right, self.side[0][c], self.side[1][c])
            for a in range(2):
                wide_ref[c, 2, block(a), :] = right_in[a, c].astype(jnp.float32)
            wait_if(self.below, self.up[0][c], self.up[1][c])
            for b in range(2):
                wide_ref[c, b, TS:, :] = below_in[b, c].astype(jnp.float32)
            wait_if(self.takes, self.corner[c])
            wide_ref[c, 2, TS:, :] = corner_in[c].astype(jnp.float32)
        for c in range(2):
            sent_if(self.above, self.up[0][c], self.up[1][c])
            sent_if(self.left, self.side[0][c], self.side[1][c])
            sent_if(self.gives, self.corner[c])


def open_kernel(cons_ref, corner_ref, count_ref, wide_ref, near_ref,
                quads, below_in, right_in, corner_in, note, note_in, sends, recvs):
    t = lax.axis_index("tile")
    pull = Pull(t, quads, below_in, right_in, corner_in, sends, recvs, 0)
    greet([{"tile": moved(t, by)} for by in (1, TGW, TGW + 1, -1, -TGW, -TGW - 1)])
    note[...] = jnp.zeros_like(note)
    note[0:2, 0:SLOTS] = corner_ref[...]
    note[2:3, 0:1] = count_ref[...]
    notes = [
        remote(note, note_in.at[k], sends, recvs, 10 + k, 10 + k, {"tile": moved(t, by)})
        for k, by in enumerate((1, TGW, TGW + 1))
    ]
    for a, b in ((0, 0), (0, 1), (1, 0), (1, 1)):
        for c in range(2):
            pull.offer(cons_ref[c, block(a), block(b)], c, a, b, wide_ref)
            pull.begin(c, a, b)
    for copy in notes:
        copy.start()
    pull.clear()
    pull.finish(wide_ref)
    for copy in notes:
        copy.wait()
    for k, flag in enumerate((pull.left, pull.above, pull.gives)):
        near_ref[k] = note_in[k] * jnp.where(flag, 1, 0)


def middle_kernel(center_ref, rr, rb, inv_ref, cons_ref, dual_ref, est_ref, wide_ref,
                  left_in, above_in, lowered, quads, below_in, right_in, corner_in, sends, recvs):
    t = lax.axis_index("tile")
    left, right, above, below = sides(t)
    pull = Pull(t, quads, below_in, right_in, corner_in, sends, recvs, 6)
    pull.clear()
    clear_if(jnp.logical_not(left), left_in)
    clear_if(jnp.logical_not(above), above_in)
    on, down = {"tile": moved(t, 1)}, {"tile": moved(t, TGW)}
    make = lambda src, dst, at, to: remote(src, dst, sends, recvs, at, at, to)
    push_on = [make(rr.at[c], left_in.at[c], c, on) for c in range(2)]
    push_far = [make(rb.at[1, c], above_in.at[1, c], 2 + c, down) for c in range(2)]
    push_low = [make(lowered.at[c], above_in.at[0, c], 4 + c, down) for c in range(2)]
    greet([{"tile": moved(t, by)} for by in (1, TGW, TGW + 1, -1, -TGW)])

    def push(c):
        start_if(right, push_on[c])
        start_if(below, push_far[c])

    def relay(c):
        wait_if(left, push_on[c])
        lowered[c] = (rb[0, c].astype(jnp.float32) + left_in[c, TS:, :].astype(jnp.float32)).astype(jnp.bfloat16)
        start_if(below, push_low[c])

    def update(c, a, b):
        rows, cols = block(a), block(b)
        total = center_ref[c, rows, cols]
        if a == 0:
            total = total + above_in[b, c].astype(jnp.float32)
        if b == 0:
            total = total + left_in[c, rows, :].astype(jnp.float32)
        value = cons_ref[c, rows, cols] + (total - penalty * dual_ref[c, rows, cols]) * inv_ref[rows, cols]
        est_ref[c, rows, cols] = value
        pull.offer(value, c, a, b, wide_ref)
        pull.begin(c, a, b)

    push(0)
    update(0, 1, 1)
    relay(0)
    push(1)
    for c in range(2):
        if c == 1:
            update(1, 1, 1)
            relay(1)
        update(c, 1, 0)
        wait_if(above, push_far[c])
        update(c, 0, 1)
        wait_if(above, push_low[c])
        update(c, 0, 0)
    pull.finish(wide_ref)
    for c in range(2):
        sent_if(right, push_on[c])
        sent_if(below, push_far[c], push_low[c])


def close_kernel(center_ref, rr, rb, cons_ref, dual_ref, est_ref, inv_ref, psum, probe_ref,
                 cons_out, dual_out, probe_out,
                 left_in, above_in, lowered, half_in, half, run_in, ring_out, ring_in, tri_out, tri_in, grown,
                 mine, cols_in, part, part_in, settled, kept,
                 rim_s, rim_r, half_s, half_r, run_s, run_r, ring_s, ring_r, tri_s, tri_r, grow_s, grow_r,
                 wide_s, wide_r, back_s, back_r, col_s, col_r, pair_s, pair_r, out_s, out_r):
    t = lax.axis_index("tile")
    left, right, above, below = sides(t)
    core = lax.rem(t, 2)
    z = lax.rem(lax.div(t, 2), RING)
    y = lax.div(t, 2 * RING)
    scan = lax.axis_index("scan")
    yh = lax.rem(scan, 2)
    x = lax.div(scan, 2)
    tile_at = lambda y_, z_, c_: {"tile": (y_ * RING + z_) * 2 + c_}
    scan_at = lambda x_, h_: {"scan": x_ * 2 + h_}
    ys = [lax.rem(y + k, RUN) for k in range(1, RUN)]
    xs = [lax.rem(x + k, COLS) for k in range(1, COLS)]
    lap, seat = lax.div(z, RUN), lax.rem(z, RUN)
    seats = [lax.rem(seat + k, RUN) for k in range(1, RUN)]
    laps = [lax.rem(lap + k, LAPS) for k in range(1, LAPS)]
    at_seat = lambda k: tile_at(y, lap * RUN + k, core)
    at_lap = lambda k: tile_at(y, k * RUN + seat, core)
    sibling = tile_at(y, z, 1 - core)
    twin = scan_at(x, 1 - yh)
    on, down = {"tile": moved(t, 1)}, {"tile": moved(t, TGW)}
    push_on = remote(rr, left_in, rim_s, rim_r, 0, 0, on)
    push_far = remote(rb.at[1], above_in.at[1], rim_s, rim_r, 1, 1, down)
    push_low = remote(lowered, above_in.at[0], rim_s, rim_r, 2, 2, down)
    to_half = remote(psum.at[1 - core], half_in, half_s, half_r, 0, 0, sibling)

    clear_if(jnp.logical_not(left), left_in)
    clear_if(jnp.logical_not(above), above_in)
    greet([{"tile": moved(t, by)} for by in (-1, -TGW)] + [sibling, twin]
          + [tile_at(k, z, core) for k in ys] + [scan_at(k, yh) for k in xs]
          + [at_seat(k) for k in seats] + [at_lap(k) for k in laps])

    start_if(right, push_on)
    start_if(below, push_far)
    to_half.start()

    def cross(n, k, at, other):
        return remote(mine.at[n, k], cols_in.at[n, at], col_s, col_r, (n, k), (n, at), scan_at(other, yh))

    def pair(n):
        return remote(part.at[n], part_in.at[n], pair_s, pair_r, n, n, twin)

    def spread(n, k, at, other):
        own = settled.at[n, at]
        return remote(own, own, out_s, out_r, (n, k), (n, at), scan_at(other, yh))

    def update(a, b):
        rows, cols = block(a), block(b)
        inv = inv_ref[rows, cols]
        for c in range(2):
            total = center_ref[c, rows, cols]
            if a == 0:
                total = total + above_in[b, c].astype(jnp.float32)
            if b == 0:
                total = total + left_in[c, rows, :].astype(jnp.float32)
            dual = dual_ref[c, rows, cols]
            estimate = est_ref[c, rows, cols]
            value = estimate + (total + penalty * (cons_ref[c, rows, cols] - dual - estimate)) * inv + dual
            kept[c, rows, cols] = value
            value = value.astype(jnp.bfloat16)
            for q in range(COLS):
                mine[a, q, c, :, cols] = value[q * 32:(q + 1) * 32]

    def share(n):
        for k in xs:
            cross(n, k, x, k).start()

    def combine(n):
        for k in xs:
            cross(n, k, k, k).wait_recv()
        cols_in[n, x] = mine[n, x]
        for c in range(2):
            summed = cols_in[n, 0, c].astype(jnp.float32)
            for k in range(1, COLS):
                summed = summed + cols_in[n, k, c].astype(jnp.float32)
            part[n, c] = summed.astype(jnp.bfloat16)
        pair(n).start()

    def settle(n):
        pair(n).wait_recv()
        shares = [(part[n, c].astype(jnp.float32) + part_in[n, c].astype(jnp.float32)) * 0.125 for c in range(2)]
        modulus = jnp.sqrt(shares[0] * shares[0] + shares[1] * shares[1])
        bound = 1.0 / jnp.maximum(modulus, 1.0)
        for c in range(2):
            settled[n, x, c] = (shares[c] * bound).astype(jnp.bfloat16)
        for k in xs:
            spread(n, k, x, k).start()

    def give(n):
        for k in xs:
            spread(n, k, k, k).wait_recv()
        for q in range(COLS):
            rows = pl.ds(n * OVER + q * 32, 32)
            for c in range(2):
                value = settled[n, q, c].astype(jnp.float32)
                cons_out[c, rows, :] = value
                dual_out[c, rows, :] = kept[c, rows, :] - value

    def run_copy(k, at):
        return remote(half.at[k], run_in.at[at], run_s, run_r, k, at, tile_at(k, z, core))

    def ring_copy(k, at):
        return remote(ring_out.at[k], ring_in.at[at], ring_s, ring_r, k, at, at_seat(k))

    def tri_copy(k, at):
        return remote(tri_out, tri_in.at[at], tri_s, tri_r, k, at, at_lap(k))

    def grow_copy(k, at):
        own = grown.at[core, y, at]
        return remote(own, own, grow_s, grow_r, k, at, at_seat(k))

    def wide_copy(k, at):
        own = grown.at[core, at]
        return remote(own, own, wide_s, wide_r, k, at, tile_at(k, z, core))

    def back_copy(at):
        own = grown.at[at]
        return remote(own, own, back_s, back_r, 0, 0, sibling)

    def probe_run():
        to_half.wait_recv()
        for q in range(RUN):
            half[q] = (psum[core, q].astype(jnp.float32) + half_in[q].astype(jnp.float32)).astype(jnp.bfloat16)
        for k in ys:
            run_copy(k, y).start()

    def probe_ring():
        for k in ys:
            run_copy(k, k).wait_recv()
        run_in[y] = half[y]
        for c in range(3):
            summed = run_in[0, c].astype(jnp.float32)
            for k in range(1, RUN):
                summed = summed + run_in[k, c].astype(jnp.float32)
            summed = summed.astype(jnp.bfloat16)
            for k in range(RUN):
                ring_out[k, c] = summed[k * 8:k * 8 + 8]
        for k in seats:
            ring_copy(k, seat).start()

    def probe_tri():
        for k in seats:
            ring_copy(k, k).wait_recv()
        ring_in[seat] = ring_out[seat]
        for c in range(3):
            summed = ring_in[0, c].astype(jnp.float32)
            for k in range(1, RUN):
                summed = summed + ring_in[k, c].astype(jnp.float32)
            tri_out[c] = summed.astype(jnp.bfloat16)
        for k in laps:
            tri_copy(k, lap).start()

    def probe_grow():
        for k in laps:
            tri_copy(k, k).wait_recv()
        tri_in[lap] = tri_out[...]
        sums = []
        for c in range(3):
            summed = tri_in[0, c].astype(jnp.float32)
            for k in range(1, LAPS):
                summed = summed + tri_in[k, c].astype(jnp.float32)
            sums.append(summed)
        scale = probe_step * lax.rsqrt(sums[2] + 1.0)
        for c in range(2):
            grown[core, y, seat, c] = (sums[c] * scale).astype(jnp.bfloat16)
        for k in seats:
            grow_copy(k, seat).start()

    def probe_wide():
        for k in seats:
            grow_copy(k, k).wait_recv()
        for k in ys:
            wide_copy(k, y).start()

    def probe_back():
        for k in ys:
            wide_copy(k, k).wait_recv()
        back_copy(core).start()

    def probe_give():
        back_copy(1 - core).wait_recv()
        for part_at in range(8):
            for k in range(RUN):
                rows = pl.ds(part_at * 32 + k * 8, 8)
                for c in range(2):
                    step = grown[part_at // 4, part_at % 4, k, c].astype(jnp.float32)
                    probe_out[c, rows, :] = probe_ref[c, rows, :] + step

    update(1, 1)
    probe_run()
    wait_if(left, push_on)
    for c in range(2):
        lowered[c] = (rb[0, c].astype(jnp.float32) + left_in[c, TS:, :].astype(jnp.float32)).astype(jnp.bfloat16)
    start_if(below, push_low)
    update(1, 0)
    share(1)
    probe_ring()
    wait_if(above, push_far)
    update(0, 1)
    combine(1)
    wait_if(above, push_low)
    update(0, 0)
    share(0)
    probe_tri()
    combine(0)
    settle(1)
    probe_grow()
    settle(0)
    probe_wide()
    give(1)
    probe_back()
    give(0)
    probe_give()

    sent_if(right, push_on)
    sent_if(below, push_far, push_low)
    to_half.wait_send()
    back_copy(core).wait_send()
    for k in ys:
        run_copy(k, y).wait_send()
        wide_copy(k, y).wait_send()
    for k in seats:
        ring_copy(k, seat).wait_send()
        grow_copy(k, seat).wait_send()
    for k in laps:
        tri_copy(k, lap).wait_send()
    for n in range(2):
        pair(n).wait_send()
        for k in xs:
            cross(n, k, x, k).wait_send()
            spread(n, k, x, k).wait_send()


def params(identity, grant):
    return pltpu.CompilerParams(
        collective_id=identity, has_side_effects=True, vmem_limit_bytes=grant * 1024 * 1024
    )


def buffer(*shape):
    return pltpu.VMEM(shape, jnp.bfloat16)


def pull_buffers():
    return [
        buffer(3, 2, OVER, OVER), buffer(2, 2, OVER, OVER), buffer(2, 2, OVER, OVER), buffer(2, OVER, OVER)
    ]


def copies_of(*count):
    return [pltpu.SemaphoreType.DMA(count), pltpu.SemaphoreType.DMA(count)]


WIDE = jax.ShapeDtypeStruct((2, 3, SPAN, LANES), jnp.float32)
FIELD = jax.ShapeDtypeStruct((2, TS, TS), jnp.float32)


def open_halo(cons, corners, counts):
    return pl.pallas_call(
        open_kernel, out_shape=(WIDE, jax.ShapeDtypeStruct((3, 8, LANES), jnp.int32)),
        in_specs=[VMEM] * 3, out_specs=(VMEM,) * 2,
        scratch_shapes=pull_buffers() + [pltpu.VMEM((8, LANES), jnp.int32), pltpu.VMEM((3, 8, LANES), jnp.int32)]
        + copies_of(13),
        compiler_params=params(1, 6), name="open_halo", cost_estimate=busy(10),
    )(cons, corners, counts)


def middle(center, rr, rb, inv, cons, dual):
    return pl.pallas_call(
        middle_kernel,
        out_shape=(FIELD, WIDE),
        in_specs=[VMEM] * 6, out_specs=(VMEM,) * 2,
        scratch_shapes=[buffer(2, SPAN, OVER), buffer(2, 2, OVER, OVER), buffer(2, OVER, OVER)]
        + pull_buffers() + copies_of(16),
        compiler_params=params(2, 10), name="middle", cost_estimate=busy(15),
    )(center, rr, rb, inv, cons, dual)


def close(center, rr, rb, cons, dual, est, inv, psum, probe):
    scratch = [
        buffer(2, SPAN, OVER), buffer(2, 2, OVER, OVER), buffer(2, OVER, OVER),
        buffer(RUN, 3, 32, PS), buffer(RUN, 3, 32, PS), buffer(RUN, 3, 32, PS),
        buffer(RUN, 3, 8, PS), buffer(RUN, 3, 8, PS), buffer(3, 8, PS), buffer(LAPS, 3, 8, PS),
        buffer(2, RUN, RUN, 2, 8, PS),
        buffer(2, COLS, 2, 32, TS), buffer(2, COLS, 2, 32, TS), buffer(2, 2, 32, TS),
        buffer(2, 2, 32, TS), buffer(2, COLS, 2, 32, TS), pltpu.VMEM((2, TS, TS), jnp.float32),
    ]
    for count in ((3,), (1,), (RUN,), (RUN,), (LAPS,), (RUN,), (RUN,), (1,), (2, COLS), (2,), (2, COLS)):
        scratch += copies_of(*count)
    return pl.pallas_call(
        close_kernel, out_shape=(FIELD,) * 3, in_specs=[VMEM] * 9, out_specs=(VMEM,) * 3,
        scratch_shapes=scratch, compiler_params=params(3, 12), name="close", cost_estimate=busy(25),
    )(center, rr, rb, cons, dual, est, inv, psum, probe)


def shards(consensus, duals, probes, amplitudes, offsets, counts):
    m1, m2 = (jnp.asarray(table) for table in transform_tables())
    cons, dual, probe = consensus[0], duals[0, 0], probes[0]
    measured, corners = amplitudes[0, 0], jnp.swapaxes(offsets[0, 0], 0, 1)
    wide, near = open_halo(cons, corners, counts)
    center, rr, rb, psum, inv = patches(True, corners, counts, wide, probe, measured, m1, m2, near=near)
    est, wide = middle(center, rr, rb, inv, cons, dual)
    center, rr, rb, psum = patches(False, corners, counts, wide, probe, measured, m1, m2, prev=psum)
    cons_new, dual_new, probe_new = close(center, rr, rb, cons, dual, est, inv, psum, probe)
    return cons_new[None], dual_new[None, None], probe_new[None]


def solution(mesh):
    placed = (
        P("tile", None, None, None),
        P("scan", "tile", None, None, None),
        P("scan", None, None, None),
        P("scan", "tile", None, None, None),
        P("scan", "tile", None, None),
        P("scan", "tile"),
    )
    return jax.shard_map(
        shards,
        mesh=mesh,
        in_specs=placed,
        out_specs=(
            P("tile", None, None, None),
            P("scan", "tile", None, None, None),
            P("scan", None, None, None),
        ),
        check_vma=False,
    )
```

```python
import functools
import math

import jax
import jax.numpy as jnp
import ml_dtypes
import numpy as np
from jax import lax
from jax.experimental import pallas as pl
from jax.experimental.pallas import tpu as pltpu
from jax.sharding import PartitionSpec as P

PS = 256
TS = 256
OVER = 128
SPAN = TS + OVER
TGW = 4
SLOTS = 4
TILES = 96
RING = 12
RUN = 4
COLS = 4
LAPS = 3
LANES = 128
penalty = 0.5
smoothing = 0.05
probe_step = 3.0
MESH = pl.DeviceIdType.MESH
VMEM = pl.BlockSpec(memory_space=pltpu.VMEM)
SMEM = pl.BlockSpec(memory_space=pltpu.SMEM)


def transform_tables():
    index = np.arange(PS, dtype=np.int64)
    angle = ((index[:, None] * index[None, :]) % PS).astype(np.float64) * (2.0 * math.pi / PS)
    scale = 1.0 / math.sqrt(PS)
    real = (np.cos(angle) * scale).astype(np.float32)
    imag = (-np.sin(angle) * scale).astype(np.float32)
    forward = np.block([[real, -imag], [imag, real]])
    return forward.astype(ml_dtypes.bfloat16), forward.T.astype(ml_dtypes.bfloat16)


def shifted_in(block, col, lane):
    amount = lax.rem(LANES - col, LANES)
    turned = [pltpu.roll(piece, amount, axis=1) for piece in block]
    keep = lane < LANES - col
    return [jnp.where(keep, turned[k], turned[k + 1]) for k in range(2)]


def shifted_out(left, right, col, lane):
    amount = lax.rem(col, LANES)
    left = pltpu.roll(left, amount, axis=1)
    right = pltpu.roll(right, amount, axis=1)
    past = lane >= col
    zero = jnp.zeros_like(left)
    return [jnp.where(past, left, zero), jnp.where(past, right, left), jnp.where(past, zero, right)]


def patches_kernel(first, *refs):
    if first:
        (off_ref, cnt_ref, near_ref, wide_ref, probe_ref, amp_ref, m1_ref, m2_ref,
         center_ref, rr_ref, rb_ref, acc_ref, inv_ref,
         tot_ref, e_ref, r_ref, win_ref, power_ref, weight_ref) = refs
    else:
        (off_ref, cnt_ref, wide_ref, probe_ref, amp_ref, m1_ref, m2_ref, prev_ref,
         center_ref, rr_ref, rb_ref, psum_ref,
         tot_ref, e_ref, r_ref, win_ref, acc_ref) = refs
    tot_ref[...] = jnp.zeros_like(tot_ref)
    if first:
        acc_ref[...] = jnp.zeros_like(acc_ref)
    else:
        acc_ref[...] = prev_ref[...]
    half = [pl.ds(0, LANES), pl.ds(LANES, LANES)]
    lane = lax.broadcasted_iota(jnp.int32, (PS, LANES), 1)

    def gather(slot, at):
        row = off_ref[0, slot]
        col = off_ref[1, slot]
        real = shifted_in([wide_ref[0, k, pl.ds(row, PS), :] for k in range(3)], col, lane)
        imag = shifted_in([wide_ref[1, k, pl.ds(row, PS), :] for k in range(3)], col, lane)
        for h in range(2):
            wr, wi = real[h], imag[h]
            pr = probe_ref[0, :, half[h]]
            pi = probe_ref[1, :, half[h]]
            win_ref[at, 0, :, half[h]] = wr
            win_ref[at, 1, :, half[h]] = wi
            e_ref[at, :PS, half[h]] = (pr * wr - pi * wi).astype(jnp.bfloat16)
            e_ref[at, PS:, half[h]] = (pr * wi + pi * wr).astype(jnp.bfloat16)

    def transform(left_ref, right_ref, field_ref, at):
        re = jnp.dot(left_ref[:PS, :], field_ref[at], preferred_element_type=jnp.float32)
        im = jnp.dot(left_ref[PS:, :], field_ref[at], preferred_element_type=jnp.float32)
        inner = jnp.concatenate([re.astype(jnp.bfloat16), im.astype(jnp.bfloat16)], 1)
        return jnp.dot(inner, right_ref[...], preferred_element_type=jnp.float32)

    def replace(slot, at):
        wave = transform(m1_ref, m2_ref, e_ref, at)
        wr, wi = wave[:, :PS], wave[:, PS:]
        factor = amp_ref[slot].astype(jnp.float32) * lax.rsqrt(wr * wr + wi * wi + smoothing) - 1.0
        r_ref[at, :PS, :] = (wr * factor).astype(jnp.bfloat16)
        r_ref[at, PS:, :] = (wi * factor).astype(jnp.bfloat16)

    def scatter(slot, at):
        row = off_ref[0, slot]
        col = off_ref[1, slot]
        back = transform(m2_ref, m1_ref, r_ref, at)
        terms = [[], []]
        for h in range(2):
            br = back[:, h * LANES:(h + 1) * LANES]
            bi = back[:, PS + h * LANES:PS + (h + 1) * LANES]
            pr = probe_ref[0, :, half[h]]
            pi = probe_ref[1, :, half[h]]
            wr = win_ref[at, 0, :, half[h]]
            wi = win_ref[at, 1, :, half[h]]
            terms[0].append(pr * br + pi * bi)
            terms[1].append(pr * bi - pi * br)
            acc_ref[0, :, half[h]] += wr * br + wi * bi
            acc_ref[1, :, half[h]] += wr * bi - wi * br
            acc_ref[2, :, half[h]] += wr * wr + wi * wi
        for c in range(2):
            out = shifted_out(terms[c][0], terms[c][1], col, lane)
            for k in range(3):
                tot_ref[c, k, pl.ds(row, PS), :] += out[k]

    def visit(slots):
        for stage in (gather, replace, scatter):
            for at, slot in enumerate(slots):
                stage(slot, at)

    count = cnt_ref[0, 0]

    for full in range(1, SLOTS + 1):
        @pl.when(count == full)
        def _(full=full):
            visit(list(range(full)))

    for k in range(2):
        center_ref[:, :, half[k]] = tot_ref[:, k, :TS, :]
        rb_ref[k] = tot_ref[:, k, TS:, :].astype(jnp.bfloat16)
    rr_ref[...] = tot_ref[:, 2].astype(jnp.bfloat16)
    if first:
        weight_ref[...] = jnp.zeros_like(weight_ref)
        power_ref[...] = probe_ref[0] * probe_ref[0] + probe_ref[1] * probe_ref[1]

        def weigh(at, col, aside, skip=0):
            rows = pl.ds(skip, PS - skip)
            out = shifted_out(power_ref[rows, half[0]], power_ref[rows, half[1]], col, lane[skip:])
            at = pl.ds(at + skip, PS - skip)
            if aside:
                weight_ref[0, at, :] += out[2]
            else:
                weight_ref[0, at, :] += out[0]
                weight_ref[1, at, :] += out[1]

        def own(slot, carry):
            weigh(off_ref[0, slot] + TS, off_ref[1, slot], False)
            return carry

        def left(slot, carry):
            weigh(near_ref[0, 0, slot] + TS, near_ref[0, 1, slot], True)
            return carry

        def above(slot, carry):
            weigh(near_ref[1, 0, slot], near_ref[1, 1, slot], False, OVER)
            return carry

        def corner(slot, carry):
            weigh(near_ref[2, 0, slot], near_ref[2, 1, slot], True, OVER)
            return carry

        lax.fori_loop(0, cnt_ref[0, 0], own, 0)
        lax.fori_loop(0, near_ref[0, 2, 0], left, 0)
        lax.fori_loop(0, near_ref[1, 2, 0], above, 0)
        lax.fori_loop(0, near_ref[2, 2, 0], corner, 0)
        for k in range(2):
            inv_ref[:, half[k]] = 1.0 / (weight_ref[k, TS:2 * TS, :] + penalty)
    else:
        for part in range(8):
            rows = pl.ds(part * 32, 32)
            for c in range(3):
                psum_ref[part // 4, part % 4, c] = acc_ref[c, rows, :].astype(jnp.bfloat16)


def busy(microseconds):
    return pl.CostEstimate(flops=microseconds * 1_000_000_000, bytes_accessed=microseconds * 3_000_000, transcendentals=0)


def patches(first, corners, count, wide, probe, measured, m1, m2, near=None, prev=None):
    shape = jax.ShapeDtypeStruct
    out_shape = [
        shape((2, TS, TS), jnp.float32),
        shape((2, SPAN, OVER), jnp.bfloat16),
        shape((2, 2, OVER, OVER), jnp.bfloat16),
    ]
    scratch = [
        pltpu.VMEM((2, 3, SPAN, LANES), jnp.float32),
        pltpu.VMEM((4, 2 * PS, PS), jnp.bfloat16),
        pltpu.VMEM((4, 2 * PS, PS), jnp.bfloat16),
        pltpu.VMEM((4, 2, PS, PS), jnp.float32),
    ]
    if first:
        args = [corners, count, near, wide, probe, measured, m1, m2]
        scalars = 3
        out_shape += [shape((3, PS, PS), jnp.float32), shape((TS, TS), jnp.float32)]
        scratch += [pltpu.VMEM((PS, PS), jnp.float32), pltpu.VMEM((2, TS + SPAN, LANES), jnp.float32)]
    else:
        args = [corners, count, wide, probe, measured, m1, m2, prev]
        scalars = 2
        out_shape += [shape((2, RUN, 3, 32, PS), jnp.bfloat16)]
        scratch += [pltpu.VMEM((3, PS, PS), jnp.float32)]
    return pl.pallas_call(
        functools.partial(patches_kernel, first),
        out_shape=tuple(out_shape),
        in_specs=[SMEM] * scalars + [VMEM] * (len(args) - scalars),
        out_specs=(VMEM,) * len(out_shape),
        scratch_shapes=scratch,
        compiler_params=pltpu.CompilerParams(vmem_limit_bytes=16 * 1024 * 1024),
        name="patches", cost_estimate=busy(8),
    )(*args)


def moved(t, by):
    return lax.rem(t + (by + TILES), TILES)


def remote(src, dst, sends, recvs, at, slot, target):
    return pltpu.make_async_remote_copy(
        src_ref=src, dst_ref=dst, send_sem=sends.at[at], recv_sem=recvs.at[slot],
        device_id=target, device_id_type=MESH,
    )


def hail(targets):
    for target in targets:
        pl.semaphore_signal(pltpu.get_barrier_semaphore(), inc=1, device_id=target, device_id_type=MESH)
    return len(targets)


def meet(count):
    pl.semaphore_wait(pltpu.get_barrier_semaphore(), count)


def start_if(flag, *copies):
    @pl.when(flag)
    def _():
        for copy in copies:
            copy.start()


def wait_if(flag, *copies):
    @pl.when(flag)
    def _():
        for copy in copies:
            copy.wait_recv()


def sent_if(flag, *copies):
    @pl.when(flag)
    def _():
        for copy in copies:
            copy.wait_send()


def clear_if(flag, *refs):
    @pl.when(flag)
    def _():
        for ref in refs:
            ref[...] = jnp.zeros_like(ref)


def sides(t):
    column = lax.rem(t, TGW)
    return column > 0, column < TGW - 1, t >= TGW, t < TILES - TGW


def block(at):
    return pl.ds(at * OVER, OVER)


class Pull:
    def __init__(self, t, quads, below_in, right_in, corner_in, sends, recvs, base):
        self.left, self.right, self.above, self.below = sides(t)
        self.gives = jnp.logical_and(self.left, self.above)
        self.takes = jnp.logical_and(self.right, self.below)
        self.refs = quads, below_in, right_in, corner_in
        up, back, far = ({"tile": moved(t, by)} for by in (-TGW, -1, -TGW - 1))
        make = lambda src, dst, at, to: remote(src, dst, sends, recvs, at, at, to)
        self.up = [[make(quads.at[b, c], below_in.at[b, c], base + 2 * b + c, up) for c in range(2)] for b in range(2)]
        self.side = [[make(quads.at[2 * a, c], right_in.at[a, c], base + 4 + 2 * a + c, back) for c in range(2)] for a in range(2)]
        self.corner = [make(quads.at[0, c], corner_in.at[c], base + 8 + c, far) for c in range(2)]

    def clear(self):
        quads, below_in, right_in, corner_in = self.refs
        clear_if(jnp.logical_not(self.right), right_in)
        clear_if(jnp.logical_not(self.below), below_in)
        clear_if(jnp.logical_not(self.takes), corner_in)

    def offer(self, value, c, a, b, wide_ref):
        rounded = value.astype(jnp.bfloat16)
        wide_ref[c, b, block(a), :] = rounded.astype(jnp.float32)
        if not (a and b):
            self.refs[0][2 * a + b, c] = rounded

    def begin(self, c, a, b):
        if a == 0 and b == 0:
            start_if(self.gives, self.corner[c])
        if a == 0:
            start_if(self.above, self.up[b][c])
        if b == 0:
            start_if(self.left, self.side[a][c])

    def finish(self, wide_ref):
        quads, below_in, right_in, corner_in = self.refs
        for c in range(2):
            wait_if(self.right, self.side[0][c], self.side[1][c])
            for a in range(2):
                wide_ref[c, 2, block(a), :] = right_in[a, c].astype(jnp.float32)
            wait_if(self.below, self.up[0][c], self.up[1][c])
            for b in range(2):
                wide_ref[c, b, TS:, :] = below_in[b, c].astype(jnp.float32)
            wait_if(self.takes, self.corner[c])
            wide_ref[c, 2, TS:, :] = corner_in[c].astype(jnp.float32)
        for c in range(2):
            sent_if(self.above, self.up[0][c], self.up[1][c])
            sent_if(self.left, self.side[0][c], self.side[1][c])
            sent_if(self.gives, self.corner[c])


def open_kernel(cons_ref, corner_ref, count_ref, wide_ref, near_ref,
                quads, below_in, right_in, corner_in, note, note_in, sends, recvs):
    t = lax.axis_index("tile")
    hailed = hail([{"tile": moved(t, by)} for by in (1, TGW, TGW + 1, -1, -TGW, -TGW - 1)])
    pull = Pull(t, quads, below_in, right_in, corner_in, sends, recvs, 0)
    pull.clear()
    line = lax.broadcasted_iota(jnp.int32, note.shape, 0)
    lane = lax.broadcasted_iota(jnp.int32, note.shape, 1)
    filled = jnp.where(jnp.logical_and(line == 2, lane == 0), count_ref[0, 0], 0)
    for axis in range(2):
        for slot in range(SLOTS):
            filled = jnp.where(jnp.logical_and(line == axis, lane == slot), corner_ref[axis, slot], filled)
    note[...] = filled
    notes = [
        remote(note, note_in.at[k], sends, recvs, 10 + k, 10 + k, {"tile": moved(t, by)})
        for k, by in enumerate((1, TGW, TGW + 1))
    ]
    quarters = ((0, 0), (0, 1), (1, 0), (1, 1))
    for a, b in quarters:
        for c in range(2):
            pull.offer(cons_ref[c, block(a), block(b)], c, a, b, wide_ref)
    meet(hailed)
    for a, b in quarters:
        for c in range(2):
            pull.begin(c, a, b)
    for copy in notes:
        copy.start()
    pull.finish(wide_ref)
    for copy in notes:
        copy.wait()
    for k, flag in enumerate((pull.left, pull.above, pull.gives)):
        near_ref[k] = note_in[k] * jnp.where(flag, 1, 0)


def middle_kernel(center_ref, rr, rb, inv_ref, cons_ref, dual_ref, est_ref, wide_ref,
                  left_in, above_in, lowered, quads, below_in, right_in, corner_in, sends, recvs):
    t = lax.axis_index("tile")
    left, right, above, below = sides(t)
    hailed = hail([{"tile": moved(t, by)} for by in (1, TGW, TGW + 1, -1, -TGW)])
    pull = Pull(t, quads, below_in, right_in, corner_in, sends, recvs, 6)
    pull.clear()
    clear_if(jnp.logical_not(left), left_in)
    clear_if(jnp.logical_not(above), above_in)
    on, down = {"tile": moved(t, 1)}, {"tile": moved(t, TGW)}
    make = lambda src, dst, at, to: remote(src, dst, sends, recvs, at, at, to)
    push_on = [make(rr.at[c], left_in.at[c], c, on) for c in range(2)]
    push_far = [make(rb.at[1, c], above_in.at[1, c], 2 + c, down) for c in range(2)]
    push_low = [make(lowered.at[c], above_in.at[0, c], 4 + c, down) for c in range(2)]

    def push(c):
        start_if(right, push_on[c])
        start_if(below, push_far[c])

    def relay(c):
        wait_if(left, push_on[c])
        lowered[c] = (rb[0, c].astype(jnp.float32) + left_in[c, TS:, :].astype(jnp.float32)).astype(jnp.bfloat16)
        start_if(below, push_low[c])

    def update(c, a, b):
        rows, cols = block(a), block(b)
        total = center_ref[c, rows, cols]
        if a == 0:
            total = total + above_in[b, c].astype(jnp.float32)
        if b == 0:
            total = total + left_in[c, rows, :].astype(jnp.float32)
        value = cons_ref[c, rows, cols] + (total - penalty * dual_ref[c, rows, cols]) * inv_ref[rows, cols]
        est_ref[c, rows, cols] = value
        pull.offer(value, c, a, b, wide_ref)
        pull.begin(c, a, b)

    update(0, 1, 1)
    update(1, 1, 1)
    meet(hailed)
    push(0)
    relay(0)
    push(1)
    for c in range(2):
        if c == 1:
            relay(1)
        update(c, 1, 0)
        wait_if(above, push_far[c])
        update(c, 0, 1)
        wait_if(above, push_low[c])
        update(c, 0, 0)
    pull.finish(wide_ref)
    for c in range(2):
        sent_if(right, push_on[c])
        sent_if(below, push_far[c], push_low[c])


def close_kernel(center_ref, rr, rb, cons_ref, dual_ref, est_ref, inv_ref, psum,
                 settled_out, kept, grown_out,
                 left_in, above_in, lowered, half_in, half, run_in, ring_out, ring_in, tri_out, tri_in, grown,
                 mine, cols_in, part, part_in, settled,
                 rim_s, rim_r, half_s, half_r, run_s, run_r, ring_s, ring_r, tri_s, tri_r, grow_s, grow_r,
                 wide_s, wide_r, back_s, back_r, col_s, col_r, pair_s, pair_r, out_s, out_r):
    t = lax.axis_index("tile")
    left, right, above, below = sides(t)
    core = lax.rem(t, 2)
    z = lax.rem(lax.div(t, 2), RING)
    y = lax.div(t, 2 * RING)
    scan = lax.axis_index("scan")
    yh = lax.rem(scan, 2)
    x = lax.div(scan, 2)
    tile_at = lambda y_, z_, c_: {"tile": (y_ * RING + z_) * 2 + c_}
    scan_at = lambda x_, h_: {"scan": x_ * 2 + h_}
    ys = [lax.rem(y + k, RUN) for k in range(1, RUN)]
    xs = [lax.rem(x + k, COLS) for k in range(1, COLS)]
    lap, seat = lax.div(z, RUN), lax.rem(z, RUN)
    seats = [lax.rem(seat + k, RUN) for k in range(1, RUN)]
    laps = [lax.rem(lap + k, LAPS) for k in range(1, LAPS)]
    at_seat = lambda k: tile_at(y, lap * RUN + k, core)
    at_lap = lambda k: tile_at(y, k * RUN + seat, core)
    sibling = tile_at(y, z, 1 - core)
    twin = scan_at(x, 1 - yh)
    on, down = {"tile": moved(t, 1)}, {"tile": moved(t, TGW)}
    push_on = remote(rr, left_in, rim_s, rim_r, 0, 0, on)
    push_far = remote(rb.at[1], above_in.at[1], rim_s, rim_r, 1, 1, down)
    push_low = remote(lowered, above_in.at[0], rim_s, rim_r, 2, 2, down)
    to_half = remote(psum.at[1 - core], half_in, half_s, half_r, 0, 0, sibling)

    hailed = hail([{"tile": moved(t, by)} for by in (-1, -TGW)] + [sibling, twin]
                  + [tile_at(k, z, core) for k in ys] + [scan_at(k, yh) for k in xs]
                  + [at_seat(k) for k in seats] + [at_lap(k) for k in laps])
    clear_if(jnp.logical_not(left), left_in)
    clear_if(jnp.logical_not(above), above_in)

    def cross(n, k, at, other):
        return remote(mine.at[n, k], cols_in.at[n, at], col_s, col_r, (n, k), (n, at), scan_at(other, yh))

    def pair(n):
        return remote(part.at[n], part_in.at[n], pair_s, pair_r, n, n, twin)

    def spread(n, k, at, other):
        own = settled.at[n, at]
        return remote(own, own, out_s, out_r, (n, k), (n, at), scan_at(other, yh))

    def update(a, b):
        rows, cols = block(a), block(b)
        inv = inv_ref[rows, cols]
        for c in range(2):
            total = center_ref[c, rows, cols]
            if a == 0:
                total = total + above_in[b, c].astype(jnp.float32)
            if b == 0:
                total = total + left_in[c, rows, :].astype(jnp.float32)
            dual = dual_ref[c, rows, cols]
            estimate = est_ref[c, rows, cols]
            value = estimate + (total + penalty * (cons_ref[c, rows, cols] - dual - estimate)) * inv + dual
            kept[c, rows, cols] = value
            value = value.astype(jnp.bfloat16)
            for q in range(COLS):
                mine[a, q, c, :, cols] = value[q * 32:(q + 1) * 32]

    def share(n):
        for k in xs:
            cross(n, k, x, k).start()

    def combine(n):
        for k in xs:
            cross(n, k, k, k).wait_recv()
        cols_in[n, x] = mine[n, x]
        for c in range(2):
            summed = cols_in[n, 0, c].astype(jnp.float32)
            for k in range(1, COLS):
                summed = summed + cols_in[n, k, c].astype(jnp.float32)
            part[n, c] = summed.astype(jnp.bfloat16)
        pair(n).start()

    def settle(n):
        pair(n).wait_recv()
        shares = [(part[n, c].astype(jnp.float32) + part_in[n, c].astype(jnp.float32)) * 0.125 for c in range(2)]
        modulus = jnp.sqrt(shares[0] * shares[0] + shares[1] * shares[1])
        bound = 1.0 / jnp.maximum(modulus, 1.0)
        for c in range(2):
            settled[n, x, c] = (shares[c] * bound).astype(jnp.bfloat16)
        for k in xs:
            spread(n, k, x, k).start()

    def give(n):
        for k in xs:
            spread(n, k, k, k).wait_recv()
        settled_out[n] = settled[n]

    def run_copy(k, at):
        return remote(half.at[k], run_in.at[at], run_s, run_r, k, at, tile_at(k, z, core))

    def ring_copy(k, at):
        return remote(ring_out.at[k], ring_in.at[at], ring_s, ring_r, k, at, at_seat(k))

    def tri_copy(k, at):
        return remote(tri_out, tri_in.at[at], tri_s, tri_r, k, at, at_lap(k))

    def grow_copy(k, at):
        own = grown.at[core, y, at]
        return remote(own, own, grow_s, grow_r, k, at, at_seat(k))

    def wide_copy(k, at):
        own = grown.at[core, at]
        return remote(own, own, wide_s, wide_r, k, at, tile_at(k, z, core))

    def back_copy(at):
        own = grown.at[at]
        return remote(own, own, back_s, back_r, 0, 0, sibling)

    def probe_run():
        to_half.wait_recv()
        for k in ys + [y]:
            half[k] = (psum[core, k].astype(jnp.float32) + half_in[k].astype(jnp.float32)).astype(jnp.bfloat16)
            if k is not y:
                run_copy(k, y).start()

    def probe_ring():
        for k in ys:
            run_copy(k, k).wait_recv()
        run_in[y] = half[y]
        for c in range(3):
            summed = run_in[0, c].astype(jnp.float32)
            for k in range(1, RUN):
                summed = summed + run_in[k, c].astype(jnp.float32)
            summed = summed.astype(jnp.bfloat16)
            for k in range(RUN):
                ring_out[k, c] = summed[k * 8:k * 8 + 8]
        for k in seats:
            ring_copy(k, seat).start()

    def probe_tri():
        for k in seats:
            ring_copy(k, k).wait_recv()
        ring_in[seat] = ring_out[seat]
        for c in range(3):
            summed = ring_in[0, c].astype(jnp.float32)
            for k in range(1, RUN):
                summed = summed + ring_in[k, c].astype(jnp.float32)
            tri_out[c] = summed.astype(jnp.bfloat16)
        for k in laps:
            tri_copy(k, lap).start()

    def probe_grow():
        for k in laps:
            tri_copy(k, k).wait_recv()
        tri_in[lap] = tri_out[...]
        sums = []
        for c in range(3):
            summed = tri_in[0, c].astype(jnp.float32)
            for k in range(1, LAPS):
                summed = summed + tri_in[k, c].astype(jnp.float32)
            sums.append(summed)
        scale = probe_step * lax.rsqrt(sums[2] + 1.0)
        for c in range(2):
            grown[core, y, seat, c] = (sums[c] * scale).astype(jnp.bfloat16)
        for k in seats:
            grow_copy(k, seat).start()

    def probe_wide():
        for k in seats:
            grow_copy(k, k).wait_recv()
        for k in ys:
            wide_copy(k, y).start()

    def probe_back():
        for k in ys:
            wide_copy(k, k).wait_recv()
        back_copy(core).start()

    def probe_give():
        back_copy(1 - core).wait_recv()
        grown_out[...] = grown[...]

    update(1, 1)
    meet(hailed)
    to_half.start()
    start_if(right, push_on)
    start_if(below, push_far)
    probe_run()
    wait_if(left, push_on)
    for c in range(2):
        lowered[c] = (rb[0, c].astype(jnp.float32) + left_in[c, TS:, :].astype(jnp.float32)).astype(jnp.bfloat16)
    start_if(below, push_low)
    update(1, 0)
    share(1)
    probe_ring()
    wait_if(above, push_far)
    update(0, 1)
    combine(1)
    wait_if(above, push_low)
    update(0, 0)
    share(0)
    probe_tri()
    combine(0)
    settle(1)
    probe_grow()
    probe_wide()
    settle(0)
    give(1)
    probe_back()
    give(0)
    probe_give()

    sent_if(right, push_on)
    sent_if(below, push_far, push_low)
    to_half.wait_send()
    back_copy(core).wait_send()
    for k in ys:
        run_copy(k, y).wait_send()
        wide_copy(k, y).wait_send()
    for k in seats:
        ring_copy(k, seat).wait_send()
        grow_copy(k, seat).wait_send()
    for k in laps:
        tri_copy(k, lap).wait_send()
    for n in range(2):
        pair(n).wait_send()
        for k in xs:
            cross(n, k, x, k).wait_send()
            spread(n, k, x, k).wait_send()


def params(identity, grant):
    return pltpu.CompilerParams(
        collective_id=identity, has_side_effects=True, vmem_limit_bytes=grant * 1024 * 1024
    )


def buffer(*shape):
    return pltpu.VMEM(shape, jnp.bfloat16)


def pull_buffers():
    return [
        buffer(3, 2, OVER, OVER), buffer(2, 2, OVER, OVER), buffer(2, 2, OVER, OVER), buffer(2, OVER, OVER)
    ]


def copies_of(*count):
    return [pltpu.SemaphoreType.DMA(count), pltpu.SemaphoreType.DMA(count)]


WIDE = jax.ShapeDtypeStruct((2, 3, SPAN, LANES), jnp.float32)
FIELD = jax.ShapeDtypeStruct((2, TS, TS), jnp.float32)


def open_halo(cons, corners, counts):
    return pl.pallas_call(
        open_kernel, out_shape=(WIDE, jax.ShapeDtypeStruct((3, 8, LANES), jnp.int32)),
        in_specs=[VMEM, SMEM, SMEM], out_specs=(VMEM,) * 2,
        scratch_shapes=pull_buffers() + [pltpu.VMEM((8, LANES), jnp.int32), pltpu.VMEM((3, 8, LANES), jnp.int32)]
        + copies_of(13),
        compiler_params=params(1, 6), name="open_halo", cost_estimate=busy(10),
    )(cons, corners, counts)


def middle(center, rr, rb, inv, cons, dual):
    return pl.pallas_call(
        middle_kernel,
        out_shape=(FIELD, WIDE),
        in_specs=[VMEM] * 6, out_specs=(VMEM,) * 2,
        scratch_shapes=[buffer(2, SPAN, OVER), buffer(2, 2, OVER, OVER), buffer(2, OVER, OVER)]
        + pull_buffers() + copies_of(16),
        compiler_params=params(2, 10), name="middle", cost_estimate=busy(15),
    )(center, rr, rb, inv, cons, dual)


def close(center, rr, rb, cons, dual, est, inv, psum):
    scratch = [
        buffer(2, SPAN, OVER), buffer(2, 2, OVER, OVER), buffer(2, OVER, OVER),
        buffer(RUN, 3, 32, PS), buffer(RUN, 3, 32, PS), buffer(RUN, 3, 32, PS),
        buffer(RUN, 3, 8, PS), buffer(RUN, 3, 8, PS), buffer(3, 8, PS), buffer(LAPS, 3, 8, PS),
        buffer(2, RUN, RUN, 2, 8, PS),
        buffer(2, COLS, 2, 32, TS), buffer(2, COLS, 2, 32, TS), buffer(2, 2, 32, TS),
        buffer(2, 2, 32, TS), buffer(2, COLS, 2, 32, TS),
    ]
    for count in ((3,), (1,), (RUN,), (RUN,), (LAPS,), (RUN,), (RUN,), (1,), (2, COLS), (2,), (2, COLS)):
        scratch += copies_of(*count)
    return pl.pallas_call(
        close_kernel,
        out_shape=(
            jax.ShapeDtypeStruct((2, COLS, 2, 32, TS), jnp.bfloat16), FIELD,
            jax.ShapeDtypeStruct((2, RUN, RUN, 2, 8, PS), jnp.bfloat16),
        ),
        in_specs=[VMEM] * 8, out_specs=(VMEM,) * 3,
        scratch_shapes=scratch, compiler_params=params(3, 12), name="close", cost_estimate=busy(25),
    )(center, rr, rb, cons, dual, est, inv, psum)


def finish_kernel(settled, kept, grown, probe_ref, cons_out, dual_out, probe_out):
    for n in range(2):
        for q in range(COLS):
            rows = pl.ds(n * OVER + q * 32, 32)
            for c in range(2):
                value = settled[n, q, c].astype(jnp.float32)
                cons_out[c, rows, :] = value
                dual_out[c, rows, :] = kept[c, rows, :] - value
    for part_at in range(8):
        for k in range(RUN):
            rows = pl.ds(part_at * 32 + k * 8, 8)
            for c in range(2):
                step = grown[part_at // 4, part_at % 4, k, c].astype(jnp.float32)
                probe_out[c, rows, :] = probe_ref[c, rows, :] + step


def finish(settled, kept, grown, probe):
    return pl.pallas_call(
        finish_kernel, out_shape=(FIELD,) * 3, in_specs=[VMEM] * 4, out_specs=(VMEM,) * 3,
        compiler_params=pltpu.CompilerParams(vmem_limit_bytes=8 * 1024 * 1024),
        name="finish", cost_estimate=busy(1),
    )(settled, kept, grown, probe)


def shards(consensus, duals, probes, amplitudes, offsets, counts):
    m1, m2 = (jnp.asarray(table) for table in transform_tables())
    cons, dual, probe = consensus[0], duals[0, 0], probes[0]
    measured, corners = amplitudes[0, 0], jnp.swapaxes(offsets[0, 0], 0, 1)
    wide, near = open_halo(cons, corners, counts)
    center, rr, rb, psum, inv = patches(True, corners, counts, wide, probe, measured, m1, m2, near=near)
    est, wide = middle(center, rr, rb, inv, cons, dual)
    center, rr, rb, psum = patches(False, corners, counts, wide, probe, measured, m1, m2, prev=psum)
    settled, kept, grown = close(center, rr, rb, cons, dual, est, inv, psum)
    cons_new, dual_new, probe_new = finish(settled, kept, grown, probe)
    return cons_new[None], dual_new[None, None], probe_new[None]


def solution(mesh):
    placed = (
        P("tile", None, None, None),
        P("scan", "tile", None, None, None),
        P("scan", None, None, None),
        P("scan", "tile", None, None, None),
        P("scan", "tile", None, None),
        P("scan", "tile"),
    )
    return jax.shard_map(
        shards,
        mesh=mesh,
        in_specs=placed,
        out_specs=(
            P("tile", None, None, None),
            P("scan", "tile", None, None, None),
            P("scan", None, None, None),
        ),
        check_vma=False,
    )
```

```python
import functools
import math

import jax
import jax.numpy as jnp
import ml_dtypes
import numpy as np
from jax import lax
from jax.experimental import pallas as pl
from jax.experimental.pallas import tpu as pltpu
from jax.sharding import PartitionSpec as P

PS = 256
TS = 256
OVER = 128
SPAN = TS + OVER
TGW = 4
SLOTS = 4
TILES = 96
RING = 12
RUN = 4
COLS = 4
LAPS = 3
LANES = 128
penalty = 0.5
smoothing = 0.05
probe_step = 3.0
MESH = pl.DeviceIdType.MESH
VMEM = pl.BlockSpec(memory_space=pltpu.VMEM)
SMEM = pl.BlockSpec(memory_space=pltpu.SMEM)


def transform_tables():
    index = np.arange(PS, dtype=np.int64)
    angle = ((index[:, None] * index[None, :]) % PS).astype(np.float64) * (2.0 * math.pi / PS)
    scale = 1.0 / math.sqrt(PS)
    real = (np.cos(angle) * scale).astype(np.float32)
    imag = (-np.sin(angle) * scale).astype(np.float32)
    forward = np.block([[real, -imag], [imag, real]])
    return forward.astype(ml_dtypes.bfloat16), forward.T.astype(ml_dtypes.bfloat16)


def shifted_in(block, col, lane):
    amount = lax.rem(LANES - col, LANES)
    turned = [pltpu.roll(piece, amount, axis=1) for piece in block]
    keep = lane < LANES - col
    return [jnp.where(keep, turned[k], turned[k + 1]) for k in range(2)]


def shifted_out(left, right, col, lane):
    amount = lax.rem(col, LANES)
    left = pltpu.roll(left, amount, axis=1)
    right = pltpu.roll(right, amount, axis=1)
    past = lane >= col
    zero = jnp.zeros_like(left)
    return [jnp.where(past, left, zero), jnp.where(past, right, left), jnp.where(past, zero, right)]


def patches_kernel(first, *refs):
    if first:
        (off_ref, cnt_ref, near_ref, wide_ref, probe_ref, amp_ref, m1_ref, m2_ref,
         center_ref, rr_ref, rb_ref, acc_ref, inv_ref,
         tot_ref, e_ref, r_ref, win_ref, power_ref, weight_ref) = refs
    else:
        (off_ref, cnt_ref, wide_ref, probe_ref, amp_ref, m1_ref, m2_ref, prev_ref,
         center_ref, rr_ref, rb_ref, psum_ref,
         tot_ref, e_ref, r_ref, win_ref, acc_ref) = refs
    tot_ref[...] = jnp.zeros_like(tot_ref)
    if first:
        acc_ref[...] = jnp.zeros_like(acc_ref)
    else:
        acc_ref[...] = prev_ref[...]
    half = [pl.ds(0, LANES), pl.ds(LANES, LANES)]
    lane = lax.broadcasted_iota(jnp.int32, (PS, LANES), 1)

    def gather(slot, at):
        row = off_ref[0, slot]
        col = off_ref[1, slot]
        real = shifted_in([wide_ref[0, k, pl.ds(row, PS), :] for k in range(3)], col, lane)
        imag = shifted_in([wide_ref[1, k, pl.ds(row, PS), :] for k in range(3)], col, lane)
        for h in range(2):
            wr, wi = real[h], imag[h]
            pr = probe_ref[0, :, half[h]]
            pi = probe_ref[1, :, half[h]]
            win_ref[at, 0, :, half[h]] = wr
            win_ref[at, 1, :, half[h]] = wi
            e_ref[at, :PS, half[h]] = (pr * wr - pi * wi).astype(jnp.bfloat16)
            e_ref[at, PS:, half[h]] = (pr * wi + pi * wr).astype(jnp.bfloat16)

    def transform(left_ref, right_ref, field_ref, at):
        re = jnp.dot(left_ref[:PS, :], field_ref[at], preferred_element_type=jnp.float32)
        im = jnp.dot(left_ref[PS:, :], field_ref[at], preferred_element_type=jnp.float32)
        inner = jnp.concatenate([re.astype(jnp.bfloat16), im.astype(jnp.bfloat16)], 1)
        return jnp.dot(inner, right_ref[...], preferred_element_type=jnp.float32)

    def replace(slot, at):
        wave = transform(m1_ref, m2_ref, e_ref, at)
        wr, wi = wave[:, :PS], wave[:, PS:]
        factor = amp_ref[slot].astype(jnp.float32) * lax.rsqrt(wr * wr + wi * wi + smoothing) - 1.0
        r_ref[at, :PS, :] = (wr * factor).astype(jnp.bfloat16)
        r_ref[at, PS:, :] = (wi * factor).astype(jnp.bfloat16)

    def scatter(slot, at):
        row = off_ref[0, slot]
        col = off_ref[1, slot]
        back = transform(m2_ref, m1_ref, r_ref, at)
        terms = [[], []]
        for h in range(2):
            br = back[:, h * LANES:(h + 1) * LANES]
            bi = back[:, PS + h * LANES:PS + (h + 1) * LANES]
            pr = probe_ref[0, :, half[h]]
            pi = probe_ref[1, :, half[h]]
            wr = win_ref[at, 0, :, half[h]]
            wi = win_ref[at, 1, :, half[h]]
            terms[0].append(pr * br + pi * bi)
            terms[1].append(pr * bi - pi * br)
            acc_ref[0, :, half[h]] += wr * br + wi * bi
            acc_ref[1, :, half[h]] += wr * bi - wi * br
            acc_ref[2, :, half[h]] += wr * wr + wi * wi
        for c in range(2):
            out = shifted_out(terms[c][0], terms[c][1], col, lane)
            for k in range(3):
                tot_ref[c, k, pl.ds(row, PS), :] += out[k]

    def visit(slots):
        for stage in (gather, replace, scatter):
            for at, slot in enumerate(slots):
                stage(slot, at)

    count = cnt_ref[0, 0]

    for full in range(1, SLOTS + 1):
        @pl.when(count == full)
        def _(full=full):
            visit(list(range(full)))

    for k in range(2):
        center_ref[:, :, half[k]] = tot_ref[:, k, :TS, :]
        rb_ref[k] = tot_ref[:, k, TS:, :].astype(jnp.bfloat16)
    rr_ref[...] = tot_ref[:, 2].astype(jnp.bfloat16)
    if first:
        weight_ref[...] = jnp.zeros_like(weight_ref)
        power_ref[...] = probe_ref[0] * probe_ref[0] + probe_ref[1] * probe_ref[1]

        def weigh(at, col, aside, skip=0):
            rows = pl.ds(skip, PS - skip)
            out = shifted_out(power_ref[rows, half[0]], power_ref[rows, half[1]], col, lane[skip:])
            at = pl.ds(at + skip, PS - skip)
            if aside:
                weight_ref[0, at, :] += out[2]
            else:
                weight_ref[0, at, :] += out[0]
                weight_ref[1, at, :] += out[1]

        def own(slot, carry):
            weigh(off_ref[0, slot] + TS, off_ref[1, slot], False)
            return carry

        def left(slot, carry):
            weigh(near_ref[0, 0, slot] + TS, near_ref[0, 1, slot], True)
            return carry

        def above(slot, carry):
            weigh(near_ref[1, 0, slot], near_ref[1, 1, slot], False, OVER)
            return carry

        def corner(slot, carry):
            weigh(near_ref[2, 0, slot], near_ref[2, 1, slot], True, OVER)
            return carry

        lax.fori_loop(0, cnt_ref[0, 0], own, 0)
        lax.fori_loop(0, near_ref[0, 2, 0], left, 0)
        lax.fori_loop(0, near_ref[1, 2, 0], above, 0)
        lax.fori_loop(0, near_ref[2, 2, 0], corner, 0)
        for k in range(2):
            inv_ref[:, half[k]] = 1.0 / (weight_ref[k, TS:2 * TS, :] + penalty)
    else:
        for part in range(8):
            rows = pl.ds(part * 32, 32)
            for c in range(3):
                psum_ref[part // 4, part % 4, c] = acc_ref[c, rows, :].astype(jnp.bfloat16)


def busy(microseconds):
    return pl.CostEstimate(flops=microseconds * 1_000_000_000, bytes_accessed=microseconds * 3_000_000, transcendentals=0)


def patches(first, corners, count, wide, probe, measured, m1, m2, near=None, prev=None):
    shape = jax.ShapeDtypeStruct
    out_shape = [
        shape((2, TS, TS), jnp.float32),
        shape((2, SPAN, OVER), jnp.bfloat16),
        shape((2, 2, OVER, OVER), jnp.bfloat16),
    ]
    scratch = [
        pltpu.VMEM((2, 3, SPAN, LANES), jnp.float32),
        pltpu.VMEM((4, 2 * PS, PS), jnp.bfloat16),
        pltpu.VMEM((4, 2 * PS, PS), jnp.bfloat16),
        pltpu.VMEM((4, 2, PS, PS), jnp.float32),
    ]
    if first:
        args = [corners, count, near, wide, probe, measured, m1, m2]
        scalars = 3
        out_shape += [shape((3, PS, PS), jnp.float32), shape((TS, TS), jnp.float32)]
        scratch += [pltpu.VMEM((PS, PS), jnp.float32), pltpu.VMEM((2, TS + SPAN, LANES), jnp.float32)]
    else:
        args = [corners, count, wide, probe, measured, m1, m2, prev]
        scalars = 2
        out_shape += [shape((2, RUN, 3, 32, PS), jnp.bfloat16)]
        scratch += [pltpu.VMEM((3, PS, PS), jnp.float32)]
    return pl.pallas_call(
        functools.partial(patches_kernel, first),
        out_shape=tuple(out_shape),
        in_specs=[SMEM] * scalars + [VMEM] * (len(args) - scalars),
        out_specs=(VMEM,) * len(out_shape),
        scratch_shapes=scratch,
        compiler_params=pltpu.CompilerParams(vmem_limit_bytes=16 * 1024 * 1024),
        name="patches", cost_estimate=busy(8),
    )(*args)


def moved(t, by):
    return lax.rem(t + (by + TILES), TILES)


def remote(src, dst, sends, recvs, at, slot, target):
    return pltpu.make_async_remote_copy(
        src_ref=src, dst_ref=dst, send_sem=sends.at[at], recv_sem=recvs.at[slot],
        device_id=target, device_id_type=MESH,
    )


def hail(targets):
    for target in targets:
        pl.semaphore_signal(pltpu.get_barrier_semaphore(), inc=1, device_id=target, device_id_type=MESH)
    return len(targets)


def meet(count):
    pl.semaphore_wait(pltpu.get_barrier_semaphore(), count)


def start_if(flag, *copies):
    @pl.when(flag)
    def _():
        for copy in copies:
            copy.start()


def wait_if(flag, *copies):
    @pl.when(flag)
    def _():
        for copy in copies:
            copy.wait_recv()


def sent_if(flag, *copies):
    @pl.when(flag)
    def _():
        for copy in copies:
            copy.wait_send()


def clear_if(flag, *refs):
    @pl.when(flag)
    def _():
        for ref in refs:
            ref[...] = jnp.zeros_like(ref)


def sides(t):
    column = lax.rem(t, TGW)
    return column > 0, column < TGW - 1, t >= TGW, t < TILES - TGW


def block(at):
    return pl.ds(at * OVER, OVER)


class Pull:
    def __init__(self, t, quads, below_in, right_in, corner_in, sends, recvs, base):
        self.left, self.right, self.above, self.below = sides(t)
        self.refs = quads, below_in, right_in, corner_in
        up, back = {"tile": moved(t, -TGW)}, {"tile": moved(t, -1)}
        make = lambda src, dst, at, to: remote(src, dst, sends, recvs, at, at, to)
        self.up = [[make(quads.at[b, c], below_in.at[b, c], base + 2 * b + c, up) for c in range(2)] for b in range(2)]
        self.side = [[make(quads.at[2 * a, c], right_in.at[a, c], base + 4 + 2 * a + c, back) for c in range(2)] for a in range(2)]
        self.relay = [make(below_in.at[0, c], corner_in.at[c], base + 8 + c, back) for c in range(2)]

    def clear(self):
        quads, below_in, right_in, corner_in = self.refs
        clear_if(jnp.logical_not(self.right), right_in, corner_in)
        clear_if(jnp.logical_not(self.below), below_in)

    def offer(self, value, c, a, b, wide_ref):
        rounded = value.astype(jnp.bfloat16)
        wide_ref[c, b, block(a), :] = rounded.astype(jnp.float32)
        if not (a and b):
            self.refs[0][2 * a + b, c] = rounded

    def begin(self, c, a, b):
        if a == 0:
            start_if(self.above, self.up[b][c])
        if b == 0:
            start_if(self.left, self.side[a][c])

    def finish(self, wide_ref):
        quads, below_in, right_in, corner_in = self.refs
        for c in range(2):
            wait_if(self.below, self.up[0][c])
            start_if(self.left, self.relay[c])
        for c in range(2):
            wait_if(self.right, self.side[0][c], self.side[1][c])
            for a in range(2):
                wide_ref[c, 2, block(a), :] = right_in[a, c].astype(jnp.float32)
            wait_if(self.below, self.up[1][c])
            for b in range(2):
                wide_ref[c, b, TS:, :] = below_in[b, c].astype(jnp.float32)
        for c in range(2):
            wait_if(self.right, self.relay[c])
            wide_ref[c, 2, TS:, :] = corner_in[c].astype(jnp.float32)
        for c in range(2):
            sent_if(self.above, self.up[0][c], self.up[1][c])
            sent_if(self.left, self.side[0][c], self.side[1][c], self.relay[c])


def open_kernel(cons_ref, corner_ref, count_ref, wide_ref, near_ref,
                quads, below_in, right_in, corner_in, note, note_in, sends, recvs):
    t = lax.axis_index("tile")
    hailed = hail([{"tile": moved(t, by)} for by in (1, TGW, -1, -TGW, -TGW - 1)])
    pull = Pull(t, quads, below_in, right_in, corner_in, sends, recvs, 0)
    pull.clear()
    line = lax.broadcasted_iota(jnp.int32, note.shape, 0)
    lane = lax.broadcasted_iota(jnp.int32, note.shape, 1)
    filled = jnp.where(jnp.logical_and(line == 2, lane == 0), count_ref[0, 0], 0)
    for axis in range(2):
        for slot in range(SLOTS):
            filled = jnp.where(jnp.logical_and(line == axis, lane == slot), corner_ref[axis, slot], filled)
    note[...] = filled
    notes = [
        remote(note, note_in.at[k], sends, recvs, 10 + k, 10 + k, {"tile": moved(t, by)})
        for k, by in enumerate((1, TGW, TGW + 1))
    ]
    quarters = ((0, 0), (0, 1), (1, 0), (1, 1))
    for a, b in quarters:
        for c in range(2):
            pull.offer(cons_ref[c, block(a), block(b)], c, a, b, wide_ref)
    meet(hailed)
    start_if(pull.above, *pull.up[0], *pull.up[1])
    start_if(pull.left, *pull.side[0], *pull.side[1])
    for copy in notes:
        copy.start()
    pull.finish(wide_ref)
    for copy in notes:
        copy.wait()
    for k, flag in enumerate((pull.left, pull.above, jnp.logical_and(pull.left, pull.above))):
        near_ref[k] = note_in[k] * jnp.where(flag, 1, 0)


def middle_kernel(center_ref, rr, rb, inv_ref, cons_ref, dual_ref, est_ref, wide_ref,
                  left_in, above_in, lowered, quads, below_in, right_in, corner_in, sends, recvs):
    t = lax.axis_index("tile")
    left, right, above, below = sides(t)
    hailed = hail([{"tile": moved(t, by)} for by in (1, TGW, -1, -TGW)])
    pull = Pull(t, quads, below_in, right_in, corner_in, sends, recvs, 6)
    pull.clear()
    clear_if(jnp.logical_not(left), left_in)
    clear_if(jnp.logical_not(above), above_in)
    on, down = {"tile": moved(t, 1)}, {"tile": moved(t, TGW)}
    make = lambda src, dst, at, to: remote(src, dst, sends, recvs, at, at, to)
    push_on = [make(rr.at[c], left_in.at[c], c, on) for c in range(2)]
    push_far = [make(rb.at[1, c], above_in.at[1, c], 2 + c, down) for c in range(2)]
    push_low = [make(lowered.at[c], above_in.at[0, c], 4 + c, down) for c in range(2)]

    def push(c):
        start_if(right, push_on[c])
        start_if(below, push_far[c])

    def relay(c):
        wait_if(left, push_on[c])
        lowered[c] = (rb[0, c].astype(jnp.float32) + left_in[c, TS:, :].astype(jnp.float32)).astype(jnp.bfloat16)
        start_if(below, push_low[c])

    def update(c, a, b):
        rows, cols = block(a), block(b)
        total = center_ref[c, rows, cols]
        if a == 0:
            total = total + above_in[b, c].astype(jnp.float32)
        if b == 0:
            total = total + left_in[c, rows, :].astype(jnp.float32)
        value = cons_ref[c, rows, cols] + (total - penalty * dual_ref[c, rows, cols]) * inv_ref[rows, cols]
        est_ref[c, rows, cols] = value
        pull.offer(value, c, a, b, wide_ref)
        pull.begin(c, a, b)

    update(0, 1, 1)
    update(1, 1, 1)
    meet(hailed)
    push(0)
    relay(0)
    push(1)
    for c in range(2):
        if c == 1:
            relay(1)
        update(c, 1, 0)
        wait_if(above, push_far[c])
        update(c, 0, 1)
        wait_if(above, push_low[c])
        update(c, 0, 0)
    pull.finish(wide_ref)
    for c in range(2):
        sent_if(right, push_on[c])
        sent_if(below, push_far[c], push_low[c])


def close_kernel(center_ref, rr, rb, cons_ref, dual_ref, est_ref, inv_ref, psum,
                 settled_out, kept, grown_out,
                 left_in, above_in, lowered, half_in, half, run_in, ring_out, ring_in, tri_out, tri_in, grown,
                 mine, cols_in, part, part_in, settled,
                 rim_s, rim_r, half_s, half_r, run_s, run_r, ring_s, ring_r, tri_s, tri_r, grow_s, grow_r,
                 wide_s, wide_r, back_s, back_r, col_s, col_r, pair_s, pair_r, out_s, out_r):
    t = lax.axis_index("tile")
    left, right, above, below = sides(t)
    core = lax.rem(t, 2)
    z = lax.rem(lax.div(t, 2), RING)
    y = lax.div(t, 2 * RING)
    scan = lax.axis_index("scan")
    yh = lax.rem(scan, 2)
    x = lax.div(scan, 2)
    tile_at = lambda y_, z_, c_: {"tile": (y_ * RING + z_) * 2 + c_}
    scan_at = lambda x_, h_: {"scan": x_ * 2 + h_}
    ys = [lax.rem(y + k, RUN) for k in range(1, RUN)]
    xs = [lax.rem(x + k, COLS) for k in range(1, COLS)]
    lap, seat = lax.div(z, RUN), lax.rem(z, RUN)
    seats = [lax.rem(seat + k, RUN) for k in range(1, RUN)]
    laps = [lax.rem(lap + k, LAPS) for k in range(1, LAPS)]
    at_seat = lambda k: tile_at(y, lap * RUN + k, core)
    at_lap = lambda k: tile_at(y, k * RUN + seat, core)
    sibling = tile_at(y, z, 1 - core)
    twin = scan_at(x, 1 - yh)
    on, down = {"tile": moved(t, 1)}, {"tile": moved(t, TGW)}
    push_on = remote(rr, left_in, rim_s, rim_r, 0, 0, on)
    push_far = remote(rb.at[1], above_in.at[1], rim_s, rim_r, 1, 1, down)
    push_low = remote(lowered, above_in.at[0], rim_s, rim_r, 2, 2, down)
    to_half = remote(psum.at[1 - core], half_in, half_s, half_r, 0, 0, sibling)

    hailed = hail([{"tile": moved(t, by)} for by in (-1, -TGW)] + [sibling, twin]
                  + [tile_at(k, z, core) for k in ys] + [scan_at(k, yh) for k in xs]
                  + [at_seat(k) for k in seats] + [at_lap(k) for k in laps])
    clear_if(jnp.logical_not(left), left_in)
    clear_if(jnp.logical_not(above), above_in)

    def cross(n, k, at, other):
        return remote(mine.at[n, k], cols_in.at[n, at], col_s, col_r, (n, k), (n, at), scan_at(other, yh))

    def pair(n):
        return remote(part.at[n], part_in.at[n], pair_s, pair_r, n, n, twin)

    def spread(n, k, at, other):
        own = settled.at[n, at]
        return remote(own, own, out_s, out_r, (n, k), (n, at), scan_at(other, yh))

    def update(a, b):
        rows, cols = block(a), block(b)
        inv = inv_ref[rows, cols]
        for c in range(2):
            total = center_ref[c, rows, cols]
            if a == 0:
                total = total + above_in[b, c].astype(jnp.float32)
            if b == 0:
                total = total + left_in[c, rows, :].astype(jnp.float32)
            dual = dual_ref[c, rows, cols]
            estimate = est_ref[c, rows, cols]
            value = estimate + (total + penalty * (cons_ref[c, rows, cols] - dual - estimate)) * inv + dual
            kept[c, rows, cols] = value
            value = value.astype(jnp.bfloat16)
            for q in range(COLS):
                mine[a, q, c, :, cols] = value[q * 32:(q + 1) * 32]

    def share(n):
        for k in xs:
            cross(n, k, x, k).start()

    def combine(n):
        for k in xs:
            cross(n, k, k, k).wait_recv()
        cols_in[n, x] = mine[n, x]
        for c in range(2):
            summed = cols_in[n, 0, c].astype(jnp.float32)
            for k in range(1, COLS):
                summed = summed + cols_in[n, k, c].astype(jnp.float32)
            part[n, c] = summed.astype(jnp.bfloat16)
        pair(n).start()

    def settle(n):
        pair(n).wait_recv()
        shares = [(part[n, c].astype(jnp.float32) + part_in[n, c].astype(jnp.float32)) * 0.125 for c in range(2)]
        modulus = jnp.sqrt(shares[0] * shares[0] + shares[1] * shares[1])
        bound = 1.0 / jnp.maximum(modulus, 1.0)
        for c in range(2):
            settled[n, x, c] = (shares[c] * bound).astype(jnp.bfloat16)
        for k in xs:
            spread(n, k, x, k).start()

    def give(n):
        for k in xs:
            spread(n, k, k, k).wait_recv()
        settled_out[n] = settled[n]

    def run_copy(k, at):
        return remote(half.at[k], run_in.at[at], run_s, run_r, k, at, tile_at(k, z, core))

    def ring_copy(k, at):
        return remote(ring_out.at[k], ring_in.at[at], ring_s, ring_r, k, at, at_seat(k))

    def tri_copy(k, at):
        return remote(tri_out, tri_in.at[at], tri_s, tri_r, k, at, at_lap(k))

    def grow_copy(k, at):
        own = grown.at[core, y, at]
        return remote(own, own, grow_s, grow_r, k, at, at_seat(k))

    def wide_copy(k, at):
        own = grown.at[core, at]
        return remote(own, own, wide_s, wide_r, k, at, tile_at(k, z, core))

    def back_copy(at):
        own = grown.at[at]
        return remote(own, own, back_s, back_r, 0, 0, sibling)

    def probe_run():
        to_half.wait_recv()
        for k in ys + [y]:
            half[k] = (psum[core, k].astype(jnp.float32) + half_in[k].astype(jnp.float32)).astype(jnp.bfloat16)
            if k is not y:
                run_copy(k, y).start()

    def probe_ring():
        for k in ys:
            run_copy(k, k).wait_recv()
        run_in[y] = half[y]
        for c in range(3):
            summed = run_in[0, c].astype(jnp.float32)
            for k in range(1, RUN):
                summed = summed + run_in[k, c].astype(jnp.float32)
            summed = summed.astype(jnp.bfloat16)
            for k in range(RUN):
                ring_out[k, c] = summed[k * 8:k * 8 + 8]
        for k in seats:
            ring_copy(k, seat).start()

    def probe_tri():
        for k in seats:
            ring_copy(k, k).wait_recv()
        ring_in[seat] = ring_out[seat]
        for c in range(3):
            summed = ring_in[0, c].astype(jnp.float32)
            for k in range(1, RUN):
                summed = summed + ring_in[k, c].astype(jnp.float32)
            tri_out[c] = summed.astype(jnp.bfloat16)
        for k in laps:
            tri_copy(k, lap).start()

    def probe_grow():
        for k in laps:
            tri_copy(k, k).wait_recv()
        tri_in[lap] = tri_out[...]
        sums = []
        for c in range(3):
            summed = tri_in[0, c].astype(jnp.float32)
            for k in range(1, LAPS):
                summed = summed + tri_in[k, c].astype(jnp.float32)
            sums.append(summed)
        scale = probe_step * lax.rsqrt(sums[2] + 1.0)
        for c in range(2):
            grown[core, y, seat, c] = (sums[c] * scale).astype(jnp.bfloat16)
        for k in seats:
            grow_copy(k, seat).start()

    def probe_wide():
        for k in seats:
            grow_copy(k, k).wait_recv()
        for k in ys:
            wide_copy(k, y).start()

    def probe_back():
        for k in ys:
            wide_copy(k, k).wait_recv()
        back_copy(core).start()

    def probe_give():
        back_copy(1 - core).wait_recv()
        grown_out[...] = grown[...]

    update(1, 1)
    meet(hailed)
    to_half.start()
    start_if(right, push_on)
    start_if(below, push_far)
    probe_run()
    wait_if(left, push_on)
    for c in range(2):
        lowered[c] = (rb[0, c].astype(jnp.float32) + left_in[c, TS:, :].astype(jnp.float32)).astype(jnp.bfloat16)
    start_if(below, push_low)
    update(1, 0)
    share(1)
    probe_ring()
    wait_if(above, push_far)
    update(0, 1)
    combine(1)
    wait_if(above, push_low)
    update(0, 0)
    share(0)
    probe_tri()
    combine(0)
    settle(1)
    probe_grow()
    probe_wide()
    settle(0)
    give(1)
    probe_back()
    give(0)
    probe_give()

    sent_if(right, push_on)
    sent_if(below, push_far, push_low)
    to_half.wait_send()
    back_copy(core).wait_send()
    for k in ys:
        run_copy(k, y).wait_send()
        wide_copy(k, y).wait_send()
    for k in seats:
        ring_copy(k, seat).wait_send()
        grow_copy(k, seat).wait_send()
    for k in laps:
        tri_copy(k, lap).wait_send()
    for n in range(2):
        pair(n).wait_send()
        for k in xs:
            cross(n, k, x, k).wait_send()
            spread(n, k, x, k).wait_send()


def params(identity, grant):
    return pltpu.CompilerParams(
        collective_id=identity, has_side_effects=True, vmem_limit_bytes=grant * 1024 * 1024
    )


def buffer(*shape):
    return pltpu.VMEM(shape, jnp.bfloat16)


def pull_buffers():
    return [
        buffer(3, 2, OVER, OVER), buffer(2, 2, OVER, OVER), buffer(2, 2, OVER, OVER), buffer(2, OVER, OVER)
    ]


def copies_of(*count):
    return [pltpu.SemaphoreType.DMA(count), pltpu.SemaphoreType.DMA(count)]


WIDE = jax.ShapeDtypeStruct((2, 3, SPAN, LANES), jnp.float32)
FIELD = jax.ShapeDtypeStruct((2, TS, TS), jnp.float32)


def open_halo(cons, corners, counts):
    return pl.pallas_call(
        open_kernel, out_shape=(WIDE, jax.ShapeDtypeStruct((3, 8, LANES), jnp.int32)),
        in_specs=[VMEM, SMEM, SMEM], out_specs=(VMEM,) * 2,
        scratch_shapes=pull_buffers() + [pltpu.VMEM((8, LANES), jnp.int32), pltpu.VMEM((3, 8, LANES), jnp.int32)]
        + copies_of(13),
        compiler_params=params(1, 6), name="open_halo", cost_estimate=busy(10),
    )(cons, corners, counts)


def middle(center, rr, rb, inv, cons, dual):
    return pl.pallas_call(
        middle_kernel,
        out_shape=(FIELD, WIDE),
        in_specs=[VMEM] * 6, out_specs=(VMEM,) * 2,
        scratch_shapes=[buffer(2, SPAN, OVER), buffer(2, 2, OVER, OVER), buffer(2, OVER, OVER)]
        + pull_buffers() + copies_of(16),
        compiler_params=params(2, 10), name="middle", cost_estimate=busy(15),
    )(center, rr, rb, inv, cons, dual)


def close(center, rr, rb, cons, dual, est, inv, psum):
    scratch = [
        buffer(2, SPAN, OVER), buffer(2, 2, OVER, OVER), buffer(2, OVER, OVER),
        buffer(RUN, 3, 32, PS), buffer(RUN, 3, 32, PS), buffer(RUN, 3, 32, PS),
        buffer(RUN, 3, 8, PS), buffer(RUN, 3, 8, PS), buffer(3, 8, PS), buffer(LAPS, 3, 8, PS),
        buffer(2, RUN, RUN, 2, 8, PS),
        buffer(2, COLS, 2, 32, TS), buffer(2, COLS, 2, 32, TS), buffer(2, 2, 32, TS),
        buffer(2, 2, 32, TS), buffer(2, COLS, 2, 32, TS),
    ]
    for count in ((3,), (1,), (RUN,), (RUN,), (LAPS,), (RUN,), (RUN,), (1,), (2, COLS), (2,), (2, COLS)):
        scratch += copies_of(*count)
    return pl.pallas_call(
        close_kernel,
        out_shape=(
            jax.ShapeDtypeStruct((2, COLS, 2, 32, TS), jnp.bfloat16), FIELD,
            jax.ShapeDtypeStruct((2, RUN, RUN, 2, 8, PS), jnp.bfloat16),
        ),
        in_specs=[VMEM] * 8, out_specs=(VMEM,) * 3,
        scratch_shapes=scratch, compiler_params=params(3, 12), name="close", cost_estimate=busy(25),
    )(center, rr, rb, cons, dual, est, inv, psum)


def finish_kernel(settled, kept, grown, probe_ref, cons_out, dual_out, probe_out):
    for n in range(2):
        for q in range(COLS):
            rows = pl.ds(n * OVER + q * 32, 32)
            for c in range(2):
                value = settled[n, q, c].astype(jnp.float32)
                cons_out[c, rows, :] = value
                dual_out[c, rows, :] = kept[c, rows, :] - value
    for part_at in range(8):
        for k in range(RUN):
            rows = pl.ds(part_at * 32 + k * 8, 8)
            for c in range(2):
                step = grown[part_at // 4, part_at % 4, k, c].astype(jnp.float32)
                probe_out[c, rows, :] = probe_ref[c, rows, :] + step


def finish(settled, kept, grown, probe):
    return pl.pallas_call(
        finish_kernel, out_shape=(FIELD,) * 3, in_specs=[VMEM] * 4, out_specs=(VMEM,) * 3,
        compiler_params=pltpu.CompilerParams(vmem_limit_bytes=8 * 1024 * 1024),
        name="finish", cost_estimate=busy(1),
    )(settled, kept, grown, probe)


def shards(consensus, duals, probes, amplitudes, offsets, counts):
    m1, m2 = (jnp.asarray(table) for table in transform_tables())
    cons, dual, probe = consensus[0], duals[0, 0], probes[0]
    measured, corners = amplitudes[0, 0], jnp.swapaxes(offsets[0, 0], 0, 1)
    wide, near = open_halo(cons, corners, counts)
    center, rr, rb, psum, inv = patches(True, corners, counts, wide, probe, measured, m1, m2, near=near)
    est, wide = middle(center, rr, rb, inv, cons, dual)
    center, rr, rb, psum = patches(False, corners, counts, wide, probe, measured, m1, m2, prev=psum)
    settled, kept, grown = close(center, rr, rb, cons, dual, est, inv, psum)
    cons_new, dual_new, probe_new = finish(settled, kept, grown, probe)
    return cons_new[None], dual_new[None, None], probe_new[None]


def solution(mesh):
    placed = (
        P("tile", None, None, None),
        P("scan", "tile", None, None, None),
        P("scan", None, None, None),
        P("scan", "tile", None, None, None),
        P("scan", "tile", None, None),
        P("scan", "tile"),
    )
    return jax.shard_map(
        shards,
        mesh=mesh,
        in_specs=placed,
        out_specs=(
            P("tile", None, None, None),
            P("scan", "tile", None, None, None),
            P("scan", None, None, None),
        ),
        check_vma=False,
    )
```

```python
import functools
import math

import jax
import jax.numpy as jnp
import ml_dtypes
import numpy as np
from jax import lax
from jax.experimental import pallas as pl
from jax.experimental.pallas import tpu as pltpu
from jax.sharding import PartitionSpec as P

PS = 256
TS = 256
OVER = 128
SPAN = TS + OVER
TGW = 4
SLOTS = 4
TILES = 96
RING = 12
RUN = 4
COLS = 4
LAPS = 3
LANES = 128
penalty = 0.5
smoothing = 0.05
probe_step = 3.0
MESH = pl.DeviceIdType.MESH
VMEM = pl.BlockSpec(memory_space=pltpu.VMEM)
SMEM = pl.BlockSpec(memory_space=pltpu.SMEM)


def transform_tables():
    index = np.arange(PS, dtype=np.int64)
    angle = ((index[:, None] * index[None, :]) % PS).astype(np.float64) * (2.0 * math.pi / PS)
    scale = 1.0 / math.sqrt(PS)
    real = (np.cos(angle) * scale).astype(np.float32)
    imag = (-np.sin(angle) * scale).astype(np.float32)
    forward = np.block([[real, -imag], [imag, real]])
    return forward.astype(ml_dtypes.bfloat16), forward.T.astype(ml_dtypes.bfloat16)


def shifted_in(block, col, lane):
    amount = lax.rem(LANES - col, LANES)
    turned = [pltpu.roll(piece, amount, axis=1) for piece in block]
    keep = lane < LANES - col
    return [jnp.where(keep, turned[k], turned[k + 1]) for k in range(2)]


def shifted_out(left, right, col, lane):
    amount = lax.rem(col, LANES)
    left = pltpu.roll(left, amount, axis=1)
    right = pltpu.roll(right, amount, axis=1)
    past = lane >= col
    zero = jnp.zeros_like(left)
    return [jnp.where(past, left, zero), jnp.where(past, right, left), jnp.where(past, zero, right)]


def patches_kernel(first, *refs):
    if first:
        (off_ref, cnt_ref, near_ref, wide_ref, probe_ref, amp_ref, m1_ref, m2_ref,
         center_ref, rr_ref, rb_ref, acc_ref, inv_ref,
         tot_ref, e_ref, r_ref, win_ref, power_ref, weight_ref) = refs
    else:
        (off_ref, cnt_ref, wide_ref, probe_ref, amp_ref, m1_ref, m2_ref, prev_ref,
         center_ref, rr_ref, rb_ref, psum_ref,
         tot_ref, e_ref, r_ref, win_ref, acc_ref) = refs
    tot_ref[...] = jnp.zeros_like(tot_ref)
    if first:
        acc_ref[...] = jnp.zeros_like(acc_ref)
    else:
        acc_ref[...] = prev_ref[...]
    half = [pl.ds(0, LANES), pl.ds(LANES, LANES)]
    lane = lax.broadcasted_iota(jnp.int32, (PS, LANES), 1)

    def gather(slot, at):
        row = off_ref[0, slot]
        col = off_ref[1, slot]
        real = shifted_in([wide_ref[0, k, pl.ds(row, PS), :] for k in range(3)], col, lane)
        imag = shifted_in([wide_ref[1, k, pl.ds(row, PS), :] for k in range(3)], col, lane)
        for h in range(2):
            wr, wi = real[h], imag[h]
            pr = probe_ref[0, :, half[h]]
            pi = probe_ref[1, :, half[h]]
            win_ref[at, 0, :, half[h]] = wr
            win_ref[at, 1, :, half[h]] = wi
            e_ref[at, :PS, half[h]] = (pr * wr - pi * wi).astype(jnp.bfloat16)
            e_ref[at, PS:, half[h]] = (pr * wi + pi * wr).astype(jnp.bfloat16)

    def transform(left_ref, right_ref, field_ref, at):
        re = jnp.dot(left_ref[:PS, :], field_ref[at], preferred_element_type=jnp.float32)
        im = jnp.dot(left_ref[PS:, :], field_ref[at], preferred_element_type=jnp.float32)
        inner = jnp.concatenate([re.astype(jnp.bfloat16), im.astype(jnp.bfloat16)], 1)
        return jnp.dot(inner, right_ref[...], preferred_element_type=jnp.float32)

    def replace(slot, at):
        wave = transform(m1_ref, m2_ref, e_ref, at)
        wr, wi = wave[:, :PS], wave[:, PS:]
        factor = amp_ref[slot].astype(jnp.float32) * lax.rsqrt(wr * wr + wi * wi + smoothing) - 1.0
        r_ref[at, :PS, :] = (wr * factor).astype(jnp.bfloat16)
        r_ref[at, PS:, :] = (wi * factor).astype(jnp.bfloat16)

    def scatter(slot, at):
        row = off_ref[0, slot]
        col = off_ref[1, slot]
        back = transform(m2_ref, m1_ref, r_ref, at)
        terms = [[], []]
        for h in range(2):
            br = back[:, h * LANES:(h + 1) * LANES]
            bi = back[:, PS + h * LANES:PS + (h + 1) * LANES]
            pr = probe_ref[0, :, half[h]]
            pi = probe_ref[1, :, half[h]]
            wr = win_ref[at, 0, :, half[h]]
            wi = win_ref[at, 1, :, half[h]]
            terms[0].append(pr * br + pi * bi)
            terms[1].append(pr * bi - pi * br)
            acc_ref[0, :, half[h]] += wr * br + wi * bi
            acc_ref[1, :, half[h]] += wr * bi - wi * br
            acc_ref[2, :, half[h]] += wr * wr + wi * wi
        for c in range(2):
            out = shifted_out(terms[c][0], terms[c][1], col, lane)
            for k in range(3):
                tot_ref[c, k, pl.ds(row, PS), :] += out[k]

    def visit(slots):
        for stage in (gather, replace, scatter):
            for at, slot in enumerate(slots):
                stage(slot, at)

    count = cnt_ref[0, 0]

    for full in range(1, SLOTS + 1):
        @pl.when(count == full)
        def _(full=full):
            visit(list(range(full)))

    for k in range(2):
        center_ref[:, :, half[k]] = tot_ref[:, k, :TS, :]
        rb_ref[k] = tot_ref[:, k, TS:, :].astype(jnp.bfloat16)
    rr_ref[...] = tot_ref[:, 2].astype(jnp.bfloat16)
    if first:
        weight_ref[...] = jnp.zeros_like(weight_ref)
        power_ref[...] = probe_ref[0] * probe_ref[0] + probe_ref[1] * probe_ref[1]

        def weigh(at, col, aside, skip=0):
            rows = pl.ds(skip, PS - skip)
            out = shifted_out(power_ref[rows, half[0]], power_ref[rows, half[1]], col, lane[skip:])
            at = pl.ds(at + skip, PS - skip)
            if aside:
                weight_ref[0, at, :] += out[2]
            else:
                weight_ref[0, at, :] += out[0]
                weight_ref[1, at, :] += out[1]

        def own(slot, carry):
            weigh(off_ref[0, slot] + TS, off_ref[1, slot], False)
            return carry

        def left(slot, carry):
            weigh(near_ref[0, 0, slot] + TS, near_ref[0, 1, slot], True)
            return carry

        def above(slot, carry):
            weigh(near_ref[1, 0, slot], near_ref[1, 1, slot], False, OVER)
            return carry

        def corner(slot, carry):
            weigh(near_ref[2, 0, slot], near_ref[2, 1, slot], True, OVER)
            return carry

        lax.fori_loop(0, cnt_ref[0, 0], own, 0)
        lax.fori_loop(0, near_ref[0, 2, 0], left, 0)
        lax.fori_loop(0, near_ref[1, 2, 0], above, 0)
        lax.fori_loop(0, near_ref[2, 2, 0], corner, 0)
        for k in range(2):
            inv_ref[:, half[k]] = 1.0 / (weight_ref[k, TS:2 * TS, :] + penalty)
    else:
        for part in range(8):
            rows = pl.ds(part * 32, 32)
            for c in range(3):
                psum_ref[part // 4, part % 4, c] = acc_ref[c, rows, :].astype(jnp.bfloat16)


def busy(microseconds):
    return pl.CostEstimate(flops=microseconds * 1_000_000_000, bytes_accessed=microseconds * 3_000_000, transcendentals=0)


def patches(first, corners, count, wide, probe, measured, m1, m2, near=None, prev=None):
    shape = jax.ShapeDtypeStruct
    out_shape = [
        shape((2, TS, TS), jnp.float32),
        shape((2, SPAN, OVER), jnp.bfloat16),
        shape((2, 2, OVER, OVER), jnp.bfloat16),
    ]
    scratch = [
        pltpu.VMEM((2, 3, SPAN, LANES), jnp.float32),
        pltpu.VMEM((4, 2 * PS, PS), jnp.bfloat16),
        pltpu.VMEM((4, 2 * PS, PS), jnp.bfloat16),
        pltpu.VMEM((4, 2, PS, PS), jnp.float32),
    ]
    if first:
        args = [corners, count, near, wide, probe, measured, m1, m2]
        scalars = 3
        out_shape += [shape((3, PS, PS), jnp.float32), shape((TS, TS), jnp.float32)]
        scratch += [pltpu.VMEM((PS, PS), jnp.float32), pltpu.VMEM((2, TS + SPAN, LANES), jnp.float32)]
    else:
        args = [corners, count, wide, probe, measured, m1, m2, prev]
        scalars = 2
        out_shape += [shape((2, RUN, 3, 32, PS), jnp.bfloat16)]
        scratch += [pltpu.VMEM((3, PS, PS), jnp.float32)]
    return pl.pallas_call(
        functools.partial(patches_kernel, first),
        out_shape=tuple(out_shape),
        in_specs=[SMEM] * scalars + [VMEM] * (len(args) - scalars),
        out_specs=(VMEM,) * len(out_shape),
        scratch_shapes=scratch,
        compiler_params=pltpu.CompilerParams(vmem_limit_bytes=16 * 1024 * 1024),
        name="patches", cost_estimate=busy(8),
    )(*args)


def moved(t, by):
    return lax.rem(t + (by + TILES), TILES)


def remote(src, dst, sends, recvs, at, slot, target):
    return pltpu.make_async_remote_copy(
        src_ref=src, dst_ref=dst, send_sem=sends.at[at], recv_sem=recvs.at[slot],
        device_id=target, device_id_type=MESH,
    )


def hail(targets):
    for target in targets:
        pl.semaphore_signal(pltpu.get_barrier_semaphore(), inc=1, device_id=target, device_id_type=MESH)
    return len(targets)


def meet(count):
    pl.semaphore_wait(pltpu.get_barrier_semaphore(), count)


def start_if(flag, *copies):
    @pl.when(flag)
    def _():
        for copy in copies:
            copy.start()


def wait_if(flag, *copies):
    @pl.when(flag)
    def _():
        for copy in copies:
            copy.wait_recv()


def sent_if(flag, *copies):
    @pl.when(flag)
    def _():
        for copy in copies:
            copy.wait_send()


def clear_if(flag, *refs):
    @pl.when(flag)
    def _():
        for ref in refs:
            ref[...] = jnp.zeros_like(ref)


def sides(t):
    column = lax.rem(t, TGW)
    return column > 0, column < TGW - 1, t >= TGW, t < TILES - TGW


def block(at):
    return pl.ds(at * OVER, OVER)


class Pull:
    def __init__(self, t, quads, below_in, right_in, corner_in, sends, recvs, base):
        self.left, self.right, self.above, self.below = sides(t)
        self.refs = quads, below_in, right_in, corner_in
        up, back = {"tile": moved(t, -TGW)}, {"tile": moved(t, -1)}
        make = lambda src, dst, at, to: remote(src, dst, sends, recvs, at, at, to)
        self.up = [[make(quads.at[b, c], below_in.at[b, c], base + 2 * b + c, up) for c in range(2)] for b in range(2)]
        self.side = [[make(quads.at[2 * a, c], right_in.at[a, c], base + 4 + 2 * a + c, back) for c in range(2)] for a in range(2)]
        self.relay = [make(below_in.at[0, c], corner_in.at[c], base + 8 + c, back) for c in range(2)]

    def clear(self):
        quads, below_in, right_in, corner_in = self.refs
        clear_if(jnp.logical_not(self.right), right_in, corner_in)
        clear_if(jnp.logical_not(self.below), below_in)

    def offer(self, value, c, a, b, wide_ref):
        rounded = value.astype(jnp.bfloat16)
        wide_ref[c, b, block(a), :] = rounded.astype(jnp.float32)
        if not (a and b):
            self.refs[0][2 * a + b, c] = rounded

    def begin(self, c, a, b):
        if a == 0:
            start_if(self.above, self.up[b][c])
        if b == 0:
            start_if(self.left, self.side[a][c])

    def finish(self, wide_ref):
        quads, below_in, right_in, corner_in = self.refs
        for c in range(2):
            wait_if(self.below, self.up[0][c])
            start_if(self.left, self.relay[c])
        for c in range(2):
            wait_if(self.right, self.side[0][c], self.side[1][c])
            for a in range(2):
                wide_ref[c, 2, block(a), :] = right_in[a, c].astype(jnp.float32)
            wait_if(self.below, self.up[1][c])
            for b in range(2):
                wide_ref[c, b, TS:, :] = below_in[b, c].astype(jnp.float32)
        for c in range(2):
            sent_if(self.above, self.up[0][c], self.up[1][c])
            sent_if(self.left, self.side[0][c], self.side[1][c])
        for c in range(2):
            wait_if(self.right, self.relay[c])
            wide_ref[c, 2, TS:, :] = corner_in[c].astype(jnp.float32)
        sent_if(self.left, *self.relay)


def open_kernel(cons_ref, corner_ref, count_ref, wide_ref, near_ref,
                quads, below_in, right_in, corner_in, note, note_in, sends, recvs):
    t = lax.axis_index("tile")
    hailed = hail([{"tile": moved(t, by)} for by in (1, TGW, -1, -TGW, -TGW - 1)])
    pull = Pull(t, quads, below_in, right_in, corner_in, sends, recvs, 0)
    pull.clear()
    line = lax.broadcasted_iota(jnp.int32, note.shape, 0)
    lane = lax.broadcasted_iota(jnp.int32, note.shape, 1)
    filled = jnp.where(jnp.logical_and(line == 2, lane == 0), count_ref[0, 0], 0)
    for axis in range(2):
        for slot in range(SLOTS):
            filled = jnp.where(jnp.logical_and(line == axis, lane == slot), corner_ref[axis, slot], filled)
    note[...] = filled
    notes = [
        remote(note, note_in.at[k], sends, recvs, 10 + k, 10 + k, {"tile": moved(t, by)})
        for k, by in enumerate((1, TGW, TGW + 1))
    ]
    quarters = ((0, 0), (0, 1), (1, 0), (1, 1))
    for a, b in quarters:
        for c in range(2):
            pull.offer(cons_ref[c, block(a), block(b)], c, a, b, wide_ref)
    meet(hailed)
    start_if(pull.above, *pull.up[0], *pull.up[1])
    start_if(pull.left, *pull.side[0], *pull.side[1])
    for copy in notes:
        copy.start()
    pull.finish(wide_ref)
    for copy in notes:
        copy.wait()
    for k, flag in enumerate((pull.left, pull.above, jnp.logical_and(pull.left, pull.above))):
        near_ref[k] = note_in[k] * jnp.where(flag, 1, 0)


def middle_kernel(center_ref, rr, rb, inv_ref, cons_ref, dual_ref, est_ref, wide_ref,
                  left_in, above_in, lowered, quads, below_in, right_in, corner_in, sends, recvs):
    t = lax.axis_index("tile")
    left, right, above, below = sides(t)
    hailed = hail([{"tile": moved(t, by)} for by in (1, TGW, -1, -TGW)])
    pull = Pull(t, quads, below_in, right_in, corner_in, sends, recvs, 6)
    pull.clear()
    clear_if(jnp.logical_not(left), left_in)
    clear_if(jnp.logical_not(above), above_in)
    on, down = {"tile": moved(t, 1)}, {"tile": moved(t, TGW)}
    make = lambda src, dst, at, to: remote(src, dst, sends, recvs, at, at, to)
    push_on = [make(rr.at[c], left_in.at[c], c, on) for c in range(2)]
    push_far = [make(rb.at[1, c], above_in.at[1, c], 2 + c, down) for c in range(2)]
    push_low = [make(lowered.at[c], above_in.at[0, c], 4 + c, down) for c in range(2)]

    def push(c):
        start_if(right, push_on[c])
        start_if(below, push_far[c])

    def relay(c):
        wait_if(left, push_on[c])
        lowered[c] = (rb[0, c].astype(jnp.float32) + left_in[c, TS:, :].astype(jnp.float32)).astype(jnp.bfloat16)
        start_if(below, push_low[c])

    def update(c, a, b):
        rows, cols = block(a), block(b)
        total = center_ref[c, rows, cols]
        if a == 0:
            total = total + above_in[b, c].astype(jnp.float32)
        if b == 0:
            total = total + left_in[c, rows, :].astype(jnp.float32)
        value = cons_ref[c, rows, cols] + (total - penalty * dual_ref[c, rows, cols]) * inv_ref[rows, cols]
        est_ref[c, rows, cols] = value
        pull.offer(value, c, a, b, wide_ref)
        pull.begin(c, a, b)

    update(0, 1, 1)
    update(1, 1, 1)
    meet(hailed)
    push(0)
    relay(0)
    push(1)
    for c in range(2):
        if c == 1:
            relay(1)
        update(c, 1, 0)
        wait_if(above, push_far[c])
        update(c, 0, 1)
        wait_if(above, push_low[c])
        update(c, 0, 0)
    for c in range(2):
        sent_if(right, push_on[c])
        sent_if(below, push_far[c], push_low[c])
    pull.finish(wide_ref)


def close_kernel(center_ref, rr, rb, cons_ref, dual_ref, est_ref, inv_ref, psum,
                 settled_out, kept, grown_out,
                 left_in, above_in, lowered, half_in, half, run_in, ring_out, ring_in, tri_out, tri_in, grown,
                 mine, cols_in, part, part_in, settled,
                 rim_s, rim_r, half_s, half_r, run_s, run_r, ring_s, ring_r, tri_s, tri_r, grow_s, grow_r,
                 wide_s, wide_r, back_s, back_r, col_s, col_r, pair_s, pair_r, out_s, out_r):
    t = lax.axis_index("tile")
    left, right, above, below = sides(t)
    core = lax.rem(t, 2)
    z = lax.rem(lax.div(t, 2), RING)
    y = lax.div(t, 2 * RING)
    scan = lax.axis_index("scan")
    yh = lax.rem(scan, 2)
    x = lax.div(scan, 2)
    tile_at = lambda y_, z_, c_: {"tile": (y_ * RING + z_) * 2 + c_}
    scan_at = lambda x_, h_: {"scan": x_ * 2 + h_}
    ys = [lax.rem(y + k, RUN) for k in range(1, RUN)]
    xs = [lax.rem(x + k, COLS) for k in range(1, COLS)]
    lap, seat = lax.div(z, RUN), lax.rem(z, RUN)
    seats = [lax.rem(seat + k, RUN) for k in range(1, RUN)]
    laps = [lax.rem(lap + k, LAPS) for k in range(1, LAPS)]
    at_seat = lambda k: tile_at(y, lap * RUN + k, core)
    at_lap = lambda k: tile_at(y, k * RUN + seat, core)
    sibling = tile_at(y, z, 1 - core)
    twin = scan_at(x, 1 - yh)
    on, down = {"tile": moved(t, 1)}, {"tile": moved(t, TGW)}
    push_on = remote(rr, left_in, rim_s, rim_r, 0, 0, on)
    push_far = remote(rb.at[1], above_in.at[1], rim_s, rim_r, 1, 1, down)
    push_low = remote(lowered, above_in.at[0], rim_s, rim_r, 2, 2, down)
    to_half = remote(psum.at[1 - core], half_in, half_s, half_r, 0, 0, sibling)

    hailed = hail([sibling] + [{"tile": moved(t, by)} for by in (-1, -TGW)] + [twin]
                  + [tile_at(k, z, core) for k in ys] + [scan_at(k, yh) for k in xs]
                  + [at_seat(k) for k in seats] + [at_lap(k) for k in laps])
    clear_if(jnp.logical_not(left), left_in)
    clear_if(jnp.logical_not(above), above_in)

    def cross(n, k, at, other):
        return remote(mine.at[n, k], cols_in.at[n, at], col_s, col_r, (n, k), (n, at), scan_at(other, yh))

    def pair(n):
        return remote(part.at[n], part_in.at[n], pair_s, pair_r, n, n, twin)

    def spread(n, k, at, other):
        own = settled.at[n, at]
        return remote(own, own, out_s, out_r, (n, k), (n, at), scan_at(other, yh))

    def update(a, b):
        rows, cols = block(a), block(b)
        inv = inv_ref[rows, cols]
        for c in range(2):
            total = center_ref[c, rows, cols]
            if a == 0:
                total = total + above_in[b, c].astype(jnp.float32)
            if b == 0:
                total = total + left_in[c, rows, :].astype(jnp.float32)
            dual = dual_ref[c, rows, cols]
            estimate = est_ref[c, rows, cols]
            value = estimate + (total + penalty * (cons_ref[c, rows, cols] - dual - estimate)) * inv + dual
            kept[c, rows, cols] = value
            value = value.astype(jnp.bfloat16)
            for q in range(COLS):
                mine[a, q, c, :, cols] = value[q * 32:(q + 1) * 32]

    def share(n):
        for k in xs:
            cross(n, k, x, k).start()

    def combine(n):
        for k in xs:
            cross(n, k, k, k).wait_recv()
        cols_in[n, x] = mine[n, x]
        for c in range(2):
            summed = cols_in[n, 0, c].astype(jnp.float32)
            for k in range(1, COLS):
                summed = summed + cols_in[n, k, c].astype(jnp.float32)
            part[n, c] = summed.astype(jnp.bfloat16)
        pair(n).start()

    def settle(n):
        pair(n).wait_recv()
        shares = [(part[n, c].astype(jnp.float32) + part_in[n, c].astype(jnp.float32)) * 0.125 for c in range(2)]
        modulus = jnp.sqrt(shares[0] * shares[0] + shares[1] * shares[1])
        bound = 1.0 / jnp.maximum(modulus, 1.0)
        for c in range(2):
            settled[n, x, c] = (shares[c] * bound).astype(jnp.bfloat16)
        for k in xs:
            spread(n, k, x, k).start()

    def give(n):
        for k in xs:
            spread(n, k, k, k).wait_recv()
        settled_out[n] = settled[n]

    def run_copy(k, at):
        return remote(half.at[k], run_in.at[at], run_s, run_r, k, at, tile_at(k, z, core))

    def ring_copy(k, at):
        return remote(ring_out.at[k], ring_in.at[at], ring_s, ring_r, k, at, at_seat(k))

    def tri_copy(k, at):
        return remote(tri_out, tri_in.at[at], tri_s, tri_r, k, at, at_lap(k))

    def grow_copy(k, at):
        own = grown.at[core, y, at]
        return remote(own, own, grow_s, grow_r, k, at, at_seat(k))

    def wide_copy(k, at):
        own = grown.at[core, at]
        return remote(own, own, wide_s, wide_r, k, at, tile_at(k, z, core))

    def back_copy(at):
        own = grown.at[at]
        return remote(own, own, back_s, back_r, 0, 0, sibling)

    def probe_run():
        to_half.wait_recv()
        for k in ys + [y]:
            half[k] = (psum[core, k].astype(jnp.float32) + half_in[k].astype(jnp.float32)).astype(jnp.bfloat16)
            if k is not y:
                run_copy(k, y).start()

    def probe_ring():
        for k in ys:
            run_copy(k, k).wait_recv()
        run_in[y] = half[y]
        for c in range(3):
            summed = run_in[0, c].astype(jnp.float32)
            for k in range(1, RUN):
                summed = summed + run_in[k, c].astype(jnp.float32)
            summed = summed.astype(jnp.bfloat16)
            for k in range(RUN):
                ring_out[k, c] = summed[k * 8:k * 8 + 8]
        for k in seats:
            ring_copy(k, seat).start()

    def probe_tri():
        for k in seats:
            ring_copy(k, k).wait_recv()
        ring_in[seat] = ring_out[seat]
        for c in range(3):
            summed = ring_in[0, c].astype(jnp.float32)
            for k in range(1, RUN):
                summed = summed + ring_in[k, c].astype(jnp.float32)
            tri_out[c] = summed.astype(jnp.bfloat16)
        for k in laps:
            tri_copy(k, lap).start()

    def probe_grow():
        for k in laps:
            tri_copy(k, k).wait_recv()
        tri_in[lap] = tri_out[...]
        sums = []
        for c in range(3):
            summed = tri_in[0, c].astype(jnp.float32)
            for k in range(1, LAPS):
                summed = summed + tri_in[k, c].astype(jnp.float32)
            sums.append(summed)
        scale = probe_step * lax.rsqrt(sums[2] + 1.0)
        for c in range(2):
            grown[core, y, seat, c] = (sums[c] * scale).astype(jnp.bfloat16)
        for k in seats:
            grow_copy(k, seat).start()

    def probe_wide():
        for k in seats:
            grow_copy(k, k).wait_recv()
        for k in ys:
            wide_copy(k, y).start()

    def probe_back():
        for k in ys:
            wide_copy(k, k).wait_recv()
        back_copy(core).start()

    def probe_give():
        back_copy(1 - core).wait_recv()
        grown_out[...] = grown[...]

    update(1, 1)
    meet(hailed)
    to_half.start()
    start_if(right, push_on)
    start_if(below, push_far)
    probe_run()
    wait_if(left, push_on)
    for c in range(2):
        lowered[c] = (rb[0, c].astype(jnp.float32) + left_in[c, TS:, :].astype(jnp.float32)).astype(jnp.bfloat16)
    start_if(below, push_low)
    update(1, 0)
    share(1)
    probe_ring()
    wait_if(above, push_far)
    update(0, 1)
    combine(1)
    wait_if(above, push_low)
    update(0, 0)
    share(0)
    probe_tri()
    combine(0)
    settle(1)
    probe_grow()
    for k in ys:
        run_copy(k, y).wait_send()
    to_half.wait_send()
    sent_if(right, push_on)
    sent_if(below, push_far, push_low)
    pair(1).wait_send()
    for k in xs:
        cross(1, k, x, k).wait_send()
    probe_wide()
    settle(0)
    for k in seats:
        ring_copy(k, seat).wait_send()
        grow_copy(k, seat).wait_send()
    for k in laps:
        tri_copy(k, lap).wait_send()
    pair(0).wait_send()
    for k in xs:
        cross(0, k, x, k).wait_send()
    give(1)
    probe_back()
    for k in ys:
        wide_copy(k, y).wait_send()
    give(0)
    for n in range(2):
        for k in xs:
            spread(n, k, x, k).wait_send()
    probe_give()
    back_copy(core).wait_send()


def params(identity, grant):
    return pltpu.CompilerParams(
        collective_id=identity, has_side_effects=True, vmem_limit_bytes=grant * 1024 * 1024
    )


def buffer(*shape):
    return pltpu.VMEM(shape, jnp.bfloat16)


def pull_buffers():
    return [
        buffer(3, 2, OVER, OVER), buffer(2, 2, OVER, OVER), buffer(2, 2, OVER, OVER), buffer(2, OVER, OVER)
    ]


def copies_of(*count):
    return [pltpu.SemaphoreType.DMA(count), pltpu.SemaphoreType.DMA(count)]


WIDE = jax.ShapeDtypeStruct((2, 3, SPAN, LANES), jnp.float32)
FIELD = jax.ShapeDtypeStruct((2, TS, TS), jnp.float32)


def open_halo(cons, corners, counts):
    return pl.pallas_call(
        open_kernel, out_shape=(WIDE, jax.ShapeDtypeStruct((3, 8, LANES), jnp.int32)),
        in_specs=[VMEM, SMEM, SMEM], out_specs=(VMEM,) * 2,
        scratch_shapes=pull_buffers() + [pltpu.VMEM((8, LANES), jnp.int32), pltpu.VMEM((3, 8, LANES), jnp.int32)]
        + copies_of(13),
        compiler_params=params(1, 6), name="open_halo", cost_estimate=busy(10),
    )(cons, corners, counts)


def middle(center, rr, rb, inv, cons, dual):
    return pl.pallas_call(
        middle_kernel,
        out_shape=(FIELD, WIDE),
        in_specs=[VMEM] * 6, out_specs=(VMEM,) * 2,
        scratch_shapes=[buffer(2, SPAN, OVER), buffer(2, 2, OVER, OVER), buffer(2, OVER, OVER)]
        + pull_buffers() + copies_of(16),
        compiler_params=params(2, 10), name="middle", cost_estimate=busy(15),
    )(center, rr, rb, inv, cons, dual)


def close(center, rr, rb, cons, dual, est, inv, psum):
    scratch = [
        buffer(2, SPAN, OVER), buffer(2, 2, OVER, OVER), buffer(2, OVER, OVER),
        buffer(RUN, 3, 32, PS), buffer(RUN, 3, 32, PS), buffer(RUN, 3, 32, PS),
        buffer(RUN, 3, 8, PS), buffer(RUN, 3, 8, PS), buffer(3, 8, PS), buffer(LAPS, 3, 8, PS),
        buffer(2, RUN, RUN, 2, 8, PS),
        buffer(2, COLS, 2, 32, TS), buffer(2, COLS, 2, 32, TS), buffer(2, 2, 32, TS),
        buffer(2, 2, 32, TS), buffer(2, COLS, 2, 32, TS),
    ]
    for count in ((3,), (1,), (RUN,), (RUN,), (LAPS,), (RUN,), (RUN,), (1,), (2, COLS), (2,), (2, COLS)):
        scratch += copies_of(*count)
    return pl.pallas_call(
        close_kernel,
        out_shape=(
            jax.ShapeDtypeStruct((2, COLS, 2, 32, TS), jnp.bfloat16), FIELD,
            jax.ShapeDtypeStruct((2, RUN, RUN, 2, 8, PS), jnp.bfloat16),
        ),
        in_specs=[VMEM] * 8, out_specs=(VMEM,) * 3,
        scratch_shapes=scratch, compiler_params=params(3, 12), name="close", cost_estimate=busy(25),
    )(center, rr, rb, cons, dual, est, inv, psum)


def finish_kernel(settled, kept, grown, probe_ref, cons_out, dual_out, probe_out):
    for n in range(2):
        for q in range(COLS):
            rows = pl.ds(n * OVER + q * 32, 32)
            for c in range(2):
                value = settled[n, q, c].astype(jnp.float32)
                cons_out[c, rows, :] = value
                dual_out[c, rows, :] = kept[c, rows, :] - value
    for part_at in range(8):
        for k in range(RUN):
            rows = pl.ds(part_at * 32 + k * 8, 8)
            for c in range(2):
                step = grown[part_at // 4, part_at % 4, k, c].astype(jnp.float32)
                probe_out[c, rows, :] = probe_ref[c, rows, :] + step


def finish(settled, kept, grown, probe):
    return pl.pallas_call(
        finish_kernel, out_shape=(FIELD,) * 3, in_specs=[VMEM] * 4, out_specs=(VMEM,) * 3,
        compiler_params=pltpu.CompilerParams(vmem_limit_bytes=8 * 1024 * 1024),
        name="finish", cost_estimate=busy(1),
    )(settled, kept, grown, probe)


def shards(consensus, duals, probes, amplitudes, offsets, counts):
    m1, m2 = (jnp.asarray(table) for table in transform_tables())
    cons, dual, probe = consensus[0], duals[0, 0], probes[0]
    measured, corners = amplitudes[0, 0], jnp.swapaxes(offsets[0, 0], 0, 1)
    wide, near = open_halo(cons, corners, counts)
    center, rr, rb, psum, inv = patches(True, corners, counts, wide, probe, measured, m1, m2, near=near)
    est, wide = middle(center, rr, rb, inv, cons, dual)
    center, rr, rb, psum = patches(False, corners, counts, wide, probe, measured, m1, m2, prev=psum)
    settled, kept, grown = close(center, rr, rb, cons, dual, est, inv, psum)
    cons_new, dual_new, probe_new = finish(settled, kept, grown, probe)
    return cons_new[None], dual_new[None, None], probe_new[None]


def solution(mesh):
    placed = (
        P("tile", None, None, None),
        P("scan", "tile", None, None, None),
        P("scan", None, None, None),
        P("scan", "tile", None, None, None),
        P("scan", "tile", None, None),
        P("scan", "tile"),
    )
    return jax.shard_map(
        shards,
        mesh=mesh,
        in_specs=placed,
        out_specs=(
            P("tile", None, None, None),
            P("scan", "tile", None, None, None),
            P("scan", None, None, None),
        ),
        check_vma=False,
    )
```

```python
import functools
import math

import jax
import jax.numpy as jnp
import ml_dtypes
import numpy as np
from jax import lax
from jax.experimental import pallas as pl
from jax.experimental.pallas import tpu as pltpu
from jax.sharding import PartitionSpec as P

PS = 256
TS = 256
OVER = 128
SPAN = TS + OVER
TGW = 4
SLOTS = 4
TILES = 96
RING = 12
RUN = 4
COLS = 4
LAPS = 3
LANES = 128
penalty = 0.5
smoothing = 0.05
probe_step = 3.0
MESH = pl.DeviceIdType.MESH
VMEM = pl.BlockSpec(memory_space=pltpu.VMEM)
SMEM = pl.BlockSpec(memory_space=pltpu.SMEM)


def transform_tables():
    index = np.arange(PS, dtype=np.int64)
    angle = ((index[:, None] * index[None, :]) % PS).astype(np.float64) * (2.0 * math.pi / PS)
    scale = 1.0 / math.sqrt(PS)
    real = (np.cos(angle) * scale).astype(np.float32)
    imag = (-np.sin(angle) * scale).astype(np.float32)
    forward = np.block([[real, -imag], [imag, real]])
    return forward.astype(ml_dtypes.bfloat16), forward.T.astype(ml_dtypes.bfloat16)


def shifted_in(block, col, lane):
    amount = lax.rem(LANES - col, LANES)
    turned = [pltpu.roll(piece, amount, axis=1) for piece in block]
    keep = lane < LANES - col
    return [jnp.where(keep, turned[k], turned[k + 1]) for k in range(2)]


def shifted_out(left, right, col, lane):
    amount = lax.rem(col, LANES)
    left = pltpu.roll(left, amount, axis=1)
    right = pltpu.roll(right, amount, axis=1)
    past = lane >= col
    zero = jnp.zeros_like(left)
    return [jnp.where(past, left, zero), jnp.where(past, right, left), jnp.where(past, zero, right)]


def patches_kernel(first, *refs):
    if first:
        (off_ref, cnt_ref, near_ref, wide_ref, probe_ref, amp_ref, m1_ref, m2_ref,
         center_ref, rr_ref, rb_ref, acc_ref, inv_ref,
         tot_ref, e_ref, r_ref, win_ref, power_ref, weight_ref) = refs
    else:
        (off_ref, cnt_ref, wide_ref, probe_ref, amp_ref, m1_ref, m2_ref, prev_ref,
         center_ref, rr_ref, rb_ref, psum_ref,
         tot_ref, e_ref, r_ref, win_ref, acc_ref) = refs
    tot_ref[...] = jnp.zeros_like(tot_ref)
    if first:
        acc_ref[...] = jnp.zeros_like(acc_ref)
    else:
        acc_ref[...] = prev_ref[...]
    half = [pl.ds(0, LANES), pl.ds(LANES, LANES)]
    lane = lax.broadcasted_iota(jnp.int32, (PS, LANES), 1)

    def gather(slot, at):
        row = off_ref[0, slot]
        col = off_ref[1, slot]
        real = shifted_in([wide_ref[0, k, pl.ds(row, PS), :] for k in range(3)], col, lane)
        imag = shifted_in([wide_ref[1, k, pl.ds(row, PS), :] for k in range(3)], col, lane)
        for h in range(2):
            wr, wi = real[h], imag[h]
            pr = probe_ref[0, :, half[h]]
            pi = probe_ref[1, :, half[h]]
            win_ref[at, 0, :, half[h]] = wr
            win_ref[at, 1, :, half[h]] = wi
            e_ref[at, :PS, half[h]] = (pr * wr - pi * wi).astype(jnp.bfloat16)
            e_ref[at, PS:, half[h]] = (pr * wi + pi * wr).astype(jnp.bfloat16)

    def transform(left_ref, right_ref, field_ref, at):
        re = jnp.dot(left_ref[:PS, :], field_ref[at], preferred_element_type=jnp.float32)
        im = jnp.dot(left_ref[PS:, :], field_ref[at], preferred_element_type=jnp.float32)
        inner = jnp.concatenate([re.astype(jnp.bfloat16), im.astype(jnp.bfloat16)], 1)
        return jnp.dot(inner, right_ref[...], preferred_element_type=jnp.float32)

    def replace(slot, at):
        wave = transform(m1_ref, m2_ref, e_ref, at)
        wr, wi = wave[:, :PS], wave[:, PS:]
        factor = amp_ref[slot].astype(jnp.float32) * lax.rsqrt(wr * wr + wi * wi + smoothing) - 1.0
        r_ref[at, :PS, :] = (wr * factor).astype(jnp.bfloat16)
        r_ref[at, PS:, :] = (wi * factor).astype(jnp.bfloat16)

    def scatter(slot, at):
        row = off_ref[0, slot]
        col = off_ref[1, slot]
        back = transform(m2_ref, m1_ref, r_ref, at)
        terms = [[], []]
        for h in range(2):
            br = back[:, h * LANES:(h + 1) * LANES]
            bi = back[:, PS + h * LANES:PS + (h + 1) * LANES]
            pr = probe_ref[0, :, half[h]]
            pi = probe_ref[1, :, half[h]]
            wr = win_ref[at, 0, :, half[h]]
            wi = win_ref[at, 1, :, half[h]]
            terms[0].append(pr * br + pi * bi)
            terms[1].append(pr * bi - pi * br)
            acc_ref[0, :, half[h]] += wr * br + wi * bi
            acc_ref[1, :, half[h]] += wr * bi - wi * br
            acc_ref[2, :, half[h]] += wr * wr + wi * wi
        for c in range(2):
            out = shifted_out(terms[c][0], terms[c][1], col, lane)
            for k in range(3):
                tot_ref[c, k, pl.ds(row, PS), :] += out[k]

    def visit(slots):
        for stage in (gather, replace, scatter):
            for at, slot in enumerate(slots):
                stage(slot, at)

    count = cnt_ref[0, 0]

    for full in range(1, SLOTS + 1):
        @pl.when(count == full)
        def _(full=full):
            visit(list(range(full)))

    for k in range(2):
        center_ref[:, :, half[k]] = tot_ref[:, k, :TS, :]
        rb_ref[k] = tot_ref[:, k, TS:, :].astype(jnp.bfloat16)
    rr_ref[...] = tot_ref[:, 2].astype(jnp.bfloat16)
    if first:
        weight_ref[...] = jnp.zeros_like(weight_ref)
        power_ref[...] = probe_ref[0] * probe_ref[0] + probe_ref[1] * probe_ref[1]

        def weigh(at, col, aside, skip=0):
            rows = pl.ds(skip, PS - skip)
            out = shifted_out(power_ref[rows, half[0]], power_ref[rows, half[1]], col, lane[skip:])
            at = pl.ds(at + skip, PS - skip)
            if aside:
                weight_ref[0, at, :] += out[2]
            else:
                weight_ref[0, at, :] += out[0]
                weight_ref[1, at, :] += out[1]

        def own(slot, carry):
            weigh(off_ref[0, slot] + TS, off_ref[1, slot], False)
            return carry

        def left(slot, carry):
            weigh(near_ref[0, 0, slot] + TS, near_ref[0, 1, slot], True)
            return carry

        def above(slot, carry):
            weigh(near_ref[1, 0, slot], near_ref[1, 1, slot], False, OVER)
            return carry

        def corner(slot, carry):
            weigh(near_ref[2, 0, slot], near_ref[2, 1, slot], True, OVER)
            return carry

        lax.fori_loop(0, cnt_ref[0, 0], own, 0)
        lax.fori_loop(0, near_ref[0, 2, 0], left, 0)
        lax.fori_loop(0, near_ref[1, 2, 0], above, 0)
        lax.fori_loop(0, near_ref[2, 2, 0], corner, 0)
        for k in range(2):
            inv_ref[:, half[k]] = 1.0 / (weight_ref[k, TS:2 * TS, :] + penalty)
    else:
        for part in range(8):
            rows = pl.ds(part * 32, 32)
            for c in range(3):
                psum_ref[part // 4, part % 4, c] = acc_ref[c, rows, :].astype(jnp.bfloat16)


def busy(microseconds):
    return pl.CostEstimate(flops=microseconds * 1_000_000_000, bytes_accessed=microseconds * 3_000_000, transcendentals=0)


def patches(first, corners, count, wide, probe, measured, m1, m2, near=None, prev=None):
    shape = jax.ShapeDtypeStruct
    out_shape = [
        shape((2, TS, TS), jnp.float32),
        shape((2, SPAN, OVER), jnp.bfloat16),
        shape((2, 2, OVER, OVER), jnp.bfloat16),
    ]
    scratch = [
        pltpu.VMEM((2, 3, SPAN, LANES), jnp.float32),
        pltpu.VMEM((4, 2 * PS, PS), jnp.bfloat16),
        pltpu.VMEM((4, 2 * PS, PS), jnp.bfloat16),
        pltpu.VMEM((4, 2, PS, PS), jnp.float32),
    ]
    if first:
        args = [corners, count, near, wide, probe, measured, m1, m2]
        scalars = 3
        out_shape += [shape((3, PS, PS), jnp.float32), shape((TS, TS), jnp.float32)]
        scratch += [pltpu.VMEM((PS, PS), jnp.float32), pltpu.VMEM((2, TS + SPAN, LANES), jnp.float32)]
    else:
        args = [corners, count, wide, probe, measured, m1, m2, prev]
        scalars = 2
        out_shape += [shape((2, RUN, 3, 32, PS), jnp.bfloat16)]
        scratch += [pltpu.VMEM((3, PS, PS), jnp.float32)]
    return pl.pallas_call(
        functools.partial(patches_kernel, first),
        out_shape=tuple(out_shape),
        in_specs=[SMEM] * scalars + [VMEM] * (len(args) - scalars),
        out_specs=(VMEM,) * len(out_shape),
        scratch_shapes=scratch,
        compiler_params=pltpu.CompilerParams(vmem_limit_bytes=16 * 1024 * 1024),
        name="patches", cost_estimate=busy(8),
    )(*args)


def moved(t, by):
    return lax.rem(t + (by + TILES), TILES)


def remote(src, dst, sends, recvs, at, slot, target):
    return pltpu.make_async_remote_copy(
        src_ref=src, dst_ref=dst, send_sem=sends.at[at], recv_sem=recvs.at[slot],
        device_id=target, device_id_type=MESH,
    )


def hail(targets):
    for target in targets:
        pl.semaphore_signal(pltpu.get_barrier_semaphore(), inc=1, device_id=target, device_id_type=MESH)
    return len(targets)


def meet(count):
    pl.semaphore_wait(pltpu.get_barrier_semaphore(), count)


def start_if(flag, *copies):
    @pl.when(flag)
    def _():
        for copy in copies:
            copy.start()


def wait_if(flag, *copies):
    @pl.when(flag)
    def _():
        for copy in copies:
            copy.wait_recv()


def sent_if(flag, *copies):
    @pl.when(flag)
    def _():
        for copy in copies:
            copy.wait_send()


def clear_if(flag, *refs):
    @pl.when(flag)
    def _():
        for ref in refs:
            ref[...] = jnp.zeros_like(ref)


def sides(t):
    column = lax.rem(t, TGW)
    return column > 0, column < TGW - 1, t >= TGW, t < TILES - TGW


def block(at):
    return pl.ds(at * OVER, OVER)


class Pull:
    def __init__(self, t, quads, below_in, right_in, corner_in, sends, recvs, base):
        self.left, self.right, self.above, self.below = sides(t)
        self.refs = quads, below_in, right_in, corner_in
        up, back = {"tile": moved(t, -TGW)}, {"tile": moved(t, -1)}
        make = lambda src, dst, at, to: remote(src, dst, sends, recvs, at, at, to)
        self.up = [[make(quads.at[b, c], below_in.at[b, c], base + 2 * b + c, up) for c in range(2)] for b in range(2)]
        self.side = [[make(quads.at[2 * a, c], right_in.at[a, c], base + 4 + 2 * a + c, back) for c in range(2)] for a in range(2)]
        self.relay = [make(below_in.at[0, c], corner_in.at[c], base + 8 + c, back) for c in range(2)]

    def clear(self):
        quads, below_in, right_in, corner_in = self.refs
        clear_if(jnp.logical_not(self.right), right_in, corner_in)
        clear_if(jnp.logical_not(self.below), below_in)

    def offer(self, value, c, a, b, wide_ref):
        rounded = value.astype(jnp.bfloat16)
        wide_ref[c, b, block(a), :] = rounded.astype(jnp.float32)
        if not (a and b):
            self.refs[0][2 * a + b, c] = rounded

    def begin(self, c, a, b):
        if a == 0:
            start_if(self.above, self.up[b][c])
        if b == 0:
            start_if(self.left, self.side[a][c])

    def finish(self, wide_ref):
        quads, below_in, right_in, corner_in = self.refs
        for c in range(2):
            wait_if(self.below, self.up[0][c])
            start_if(self.left, self.relay[c])
        for c in range(2):
            wait_if(self.right, self.side[0][c], self.side[1][c])
            for a in range(2):
                wide_ref[c, 2, block(a), :] = right_in[a, c].astype(jnp.float32)
            wait_if(self.below, self.up[1][c])
            for b in range(2):
                wide_ref[c, b, TS:, :] = below_in[b, c].astype(jnp.float32)
        for c in range(2):
            sent_if(self.above, self.up[0][c], self.up[1][c])
            sent_if(self.left, self.side[0][c], self.side[1][c])
        for c in range(2):
            wait_if(self.right, self.relay[c])
            wide_ref[c, 2, TS:, :] = corner_in[c].astype(jnp.float32)
        sent_if(self.left, *self.relay)


def open_kernel(cons_ref, corner_ref, count_ref, wide_ref, near_ref,
                quads, below_in, right_in, corner_in, note, note_in, sends, recvs):
    t = lax.axis_index("tile")
    hailed = hail([{"tile": moved(t, by)} for by in (1, TGW, -1, -TGW, -TGW - 1)])
    pull = Pull(t, quads, below_in, right_in, corner_in, sends, recvs, 0)
    pull.clear()
    line = lax.broadcasted_iota(jnp.int32, note.shape, 0)
    lane = lax.broadcasted_iota(jnp.int32, note.shape, 1)
    filled = jnp.where(jnp.logical_and(line == 2, lane == 0), count_ref[0, 0], 0)
    for axis in range(2):
        for slot in range(SLOTS):
            filled = jnp.where(jnp.logical_and(line == axis, lane == slot), corner_ref[axis, slot], filled)
    note[...] = filled
    notes = [
        remote(note, note_in.at[k], sends, recvs, 10 + k, 10 + k, {"tile": moved(t, by)})
        for k, by in enumerate((1, TGW, TGW + 1))
    ]
    quarters = ((0, 0), (0, 1), (1, 0), (1, 1))
    for a, b in quarters:
        for c in range(2):
            pull.offer(cons_ref[c, block(a), block(b)], c, a, b, wide_ref)
    meet(hailed)
    start_if(pull.above, *pull.up[0], *pull.up[1])
    start_if(pull.left, *pull.side[0], *pull.side[1])
    for copy in notes:
        copy.start()
    pull.finish(wide_ref)
    for copy in notes:
        copy.wait()
    for k, flag in enumerate((pull.left, pull.above, jnp.logical_and(pull.left, pull.above))):
        near_ref[k] = note_in[k] * jnp.where(flag, 1, 0)


def middle_kernel(center_ref, rr, rb, inv_ref, cons_ref, dual_ref, est_ref, wide_ref,
                  left_in, above_in, lowered, quads, below_in, right_in, corner_in, sends, recvs):
    t = lax.axis_index("tile")
    left, right, above, below = sides(t)
    hailed = hail([{"tile": moved(t, by)} for by in (1, TGW, -1, -TGW)])
    pull = Pull(t, quads, below_in, right_in, corner_in, sends, recvs, 6)
    pull.clear()
    clear_if(jnp.logical_not(left), left_in)
    clear_if(jnp.logical_not(above), above_in)
    on, down = {"tile": moved(t, 1)}, {"tile": moved(t, TGW)}
    make = lambda src, dst, at, to: remote(src, dst, sends, recvs, at, at, to)
    push_on = [make(rr.at[c], left_in.at[c], c, on) for c in range(2)]
    push_far = [make(rb.at[1, c], above_in.at[1, c], 2 + c, down) for c in range(2)]
    push_low = [make(lowered.at[c], above_in.at[0, c], 4 + c, down) for c in range(2)]

    def relay(c):
        wait_if(left, push_on[c])
        lowered[c] = (rb[0, c].astype(jnp.float32) + left_in[c, TS:, :].astype(jnp.float32)).astype(jnp.bfloat16)
        start_if(below, push_low[c])

    def update(c, a, b):
        rows, cols = block(a), block(b)
        total = center_ref[c, rows, cols]
        if a == 0:
            total = total + above_in[b, c].astype(jnp.float32)
        if b == 0:
            total = total + left_in[c, rows, :].astype(jnp.float32)
        value = cons_ref[c, rows, cols] + (total - penalty * dual_ref[c, rows, cols]) * inv_ref[rows, cols]
        est_ref[c, rows, cols] = value
        pull.offer(value, c, a, b, wide_ref)
        pull.begin(c, a, b)

    update(0, 1, 1)
    update(1, 1, 1)
    meet(hailed)
    start_if(right, *push_on)
    start_if(below, *push_far)
    relay(0)
    relay(1)
    for c in range(2):
        update(c, 1, 0)
    for c in range(2):
        wait_if(above, push_far[c])
        update(c, 0, 1)
    for c in range(2):
        wait_if(above, push_low[c])
        update(c, 0, 0)
    for c in range(2):
        sent_if(right, push_on[c])
        sent_if(below, push_far[c], push_low[c])
    pull.finish(wide_ref)


def close_kernel(center_ref, rr, rb, cons_ref, dual_ref, est_ref, inv_ref, psum,
                 settled_out, kept, grown_out,
                 left_in, above_in, lowered, half_in, half, run_in, ring_out, ring_in, tri_out, tri_in, grown,
                 mine, cols_in, part, part_in, settled,
                 rim_s, rim_r, half_s, half_r, run_s, run_r, ring_s, ring_r, tri_s, tri_r, grow_s, grow_r,
                 wide_s, wide_r, back_s, back_r, col_s, col_r, pair_s, pair_r, out_s, out_r):
    t = lax.axis_index("tile")
    left, right, above, below = sides(t)
    core = lax.rem(t, 2)
    z = lax.rem(lax.div(t, 2), RING)
    y = lax.div(t, 2 * RING)
    scan = lax.axis_index("scan")
    yh = lax.rem(scan, 2)
    x = lax.div(scan, 2)
    tile_at = lambda y_, z_, c_: {"tile": (y_ * RING + z_) * 2 + c_}
    scan_at = lambda x_, h_: {"scan": x_ * 2 + h_}
    ys = [lax.rem(y + k, RUN) for k in range(1, RUN)]
    xs = [lax.rem(x + k, COLS) for k in range(1, COLS)]
    lap, seat = lax.div(z, RUN), lax.rem(z, RUN)
    seats = [lax.rem(seat + k, RUN) for k in range(1, RUN)]
    laps = [lax.rem(lap + k, LAPS) for k in range(1, LAPS)]
    at_seat = lambda k: tile_at(y, lap * RUN + k, core)
    at_lap = lambda k: tile_at(y, k * RUN + seat, core)
    sibling = tile_at(y, z, 1 - core)
    twin = scan_at(x, 1 - yh)
    on, down = {"tile": moved(t, 1)}, {"tile": moved(t, TGW)}
    push_on = remote(rr, left_in, rim_s, rim_r, 0, 0, on)
    push_far = remote(rb.at[1], above_in.at[1], rim_s, rim_r, 1, 1, down)
    push_low = remote(lowered, above_in.at[0], rim_s, rim_r, 2, 2, down)
    to_half = remote(psum.at[1 - core], half_in, half_s, half_r, 0, 0, sibling)

    hailed = hail([sibling] + [{"tile": moved(t, by)} for by in (-1, -TGW)] + [twin]
                  + [tile_at(k, z, core) for k in ys] + [scan_at(k, yh) for k in xs]
                  + [at_seat(k) for k in seats] + [at_lap(k) for k in laps])
    clear_if(jnp.logical_not(left), left_in)
    clear_if(jnp.logical_not(above), above_in)

    def cross(n, k, at, other):
        return remote(mine.at[n, k], cols_in.at[n, at], col_s, col_r, (n, k), (n, at), scan_at(other, yh))

    def pair(n):
        return remote(part.at[n], part_in.at[n], pair_s, pair_r, n, n, twin)

    def spread(n, k, at, other):
        own = settled.at[n, at]
        return remote(own, own, out_s, out_r, (n, k), (n, at), scan_at(other, yh))

    def update(a, b):
        rows, cols = block(a), block(b)
        inv = inv_ref[rows, cols]
        for c in range(2):
            total = center_ref[c, rows, cols]
            if a == 0:
                total = total + above_in[b, c].astype(jnp.float32)
            if b == 0:
                total = total + left_in[c, rows, :].astype(jnp.float32)
            dual = dual_ref[c, rows, cols]
            estimate = est_ref[c, rows, cols]
            value = estimate + (total + penalty * (cons_ref[c, rows, cols] - dual - estimate)) * inv + dual
            kept[c, rows, cols] = value
            value = value.astype(jnp.bfloat16)
            for q in range(COLS):
                mine[a, q, c, :, cols] = value[q * 32:(q + 1) * 32]

    def share(n):
        for k in xs:
            cross(n, k, x, k).start()

    def combine(n):
        for k in xs:
            cross(n, k, k, k).wait_recv()
        cols_in[n, x] = mine[n, x]
        for c in range(2):
            summed = cols_in[n, 0, c].astype(jnp.float32)
            for k in range(1, COLS):
                summed = summed + cols_in[n, k, c].astype(jnp.float32)
            part[n, c] = summed.astype(jnp.bfloat16)
        pair(n).start()

    def settle(n):
        pair(n).wait_recv()
        shares = [(part[n, c].astype(jnp.float32) + part_in[n, c].astype(jnp.float32)) * 0.125 for c in range(2)]
        modulus = jnp.sqrt(shares[0] * shares[0] + shares[1] * shares[1])
        bound = 1.0 / jnp.maximum(modulus, 1.0)
        for c in range(2):
            settled[n, x, c] = (shares[c] * bound).astype(jnp.bfloat16)
        for k in xs:
            spread(n, k, x, k).start()

    def give(n):
        for k in xs:
            spread(n, k, k, k).wait_recv()
        settled_out[n] = settled[n]

    def run_copy(k, at):
        return remote(half.at[k], run_in.at[at], run_s, run_r, k, at, tile_at(k, z, core))

    def ring_copy(k, at):
        return remote(ring_out.at[k], ring_in.at[at], ring_s, ring_r, k, at, at_seat(k))

    def tri_copy(k, at):
        return remote(tri_out, tri_in.at[at], tri_s, tri_r, k, at, at_lap(k))

    def grow_copy(k, at):
        own = grown.at[core, y, at]
        return remote(own, own, grow_s, grow_r, k, at, at_seat(k))

    def wide_copy(k, at):
        own = grown.at[core, at]
        return remote(own, own, wide_s, wide_r, k, at, tile_at(k, z, core))

    def back_copy(at):
        own = grown.at[at]
        return remote(own, own, back_s, back_r, 0, 0, sibling)

    def probe_run():
        to_half.wait_recv()
        for k in ys + [y]:
            half[k] = (psum[core, k].astype(jnp.float32) + half_in[k].astype(jnp.float32)).astype(jnp.bfloat16)
            if k is not y:
                run_copy(k, y).start()

    def probe_ring():
        for k in ys:
            run_copy(k, k).wait_recv()
        run_in[y] = half[y]
        for c in range(3):
            summed = run_in[0, c].astype(jnp.float32)
            for k in range(1, RUN):
                summed = summed + run_in[k, c].astype(jnp.float32)
            summed = summed.astype(jnp.bfloat16)
            for k in range(RUN):
                ring_out[k, c] = summed[k * 8:k * 8 + 8]
        for k in seats:
            ring_copy(k, seat).start()

    def probe_tri():
        for k in seats:
            ring_copy(k, k).wait_recv()
        ring_in[seat] = ring_out[seat]
        for c in range(3):
            summed = ring_in[0, c].astype(jnp.float32)
            for k in range(1, RUN):
                summed = summed + ring_in[k, c].astype(jnp.float32)
            tri_out[c] = summed.astype(jnp.bfloat16)
        for k in laps:
            tri_copy(k, lap).start()

    def probe_grow():
        for k in laps:
            tri_copy(k, k).wait_recv()
        tri_in[lap] = tri_out[...]
        sums = []
        for c in range(3):
            summed = tri_in[0, c].astype(jnp.float32)
            for k in range(1, LAPS):
                summed = summed + tri_in[k, c].astype(jnp.float32)
            sums.append(summed)
        scale = probe_step * lax.rsqrt(sums[2] + 1.0)
        for c in range(2):
            grown[core, y, seat, c] = (sums[c] * scale).astype(jnp.bfloat16)
        for k in seats:
            grow_copy(k, seat).start()

    def probe_wide():
        for k in seats:
            grow_copy(k, k).wait_recv()
        for k in ys:
            wide_copy(k, y).start()

    def probe_back():
        for k in ys:
            wide_copy(k, k).wait_recv()
        back_copy(core).start()

    def probe_give():
        back_copy(1 - core).wait_recv()
        grown_out[...] = grown[...]

    update(1, 1)
    meet(hailed)
    to_half.start()
    start_if(right, push_on)
    start_if(below, push_far)
    probe_run()
    wait_if(left, push_on)
    for c in range(2):
        lowered[c] = (rb[0, c].astype(jnp.float32) + left_in[c, TS:, :].astype(jnp.float32)).astype(jnp.bfloat16)
    start_if(below, push_low)
    update(1, 0)
    share(1)
    probe_ring()
    wait_if(above, push_far)
    update(0, 1)
    combine(1)
    wait_if(above, push_low)
    update(0, 0)
    share(0)
    probe_tri()
    combine(0)
    settle(1)
    probe_grow()
    for k in ys:
        run_copy(k, y).wait_send()
    to_half.wait_send()
    sent_if(right, push_on)
    sent_if(below, push_far, push_low)
    pair(1).wait_send()
    for k in xs:
        cross(1, k, x, k).wait_send()
    probe_wide()
    settle(0)
    for k in seats:
        ring_copy(k, seat).wait_send()
        grow_copy(k, seat).wait_send()
    for k in laps:
        tri_copy(k, lap).wait_send()
    pair(0).wait_send()
    for k in xs:
        cross(0, k, x, k).wait_send()
    give(1)
    probe_back()
    for k in ys:
        wide_copy(k, y).wait_send()
    give(0)
    for n in range(2):
        for k in xs:
            spread(n, k, x, k).wait_send()
    probe_give()
    back_copy(core).wait_send()


def params(identity, grant):
    return pltpu.CompilerParams(
        collective_id=identity, has_side_effects=True, vmem_limit_bytes=grant * 1024 * 1024
    )


def buffer(*shape):
    return pltpu.VMEM(shape, jnp.bfloat16)


def pull_buffers():
    return [
        buffer(3, 2, OVER, OVER), buffer(2, 2, OVER, OVER), buffer(2, 2, OVER, OVER), buffer(2, OVER, OVER)
    ]


def copies_of(*count):
    return [pltpu.SemaphoreType.DMA(count), pltpu.SemaphoreType.DMA(count)]


WIDE = jax.ShapeDtypeStruct((2, 3, SPAN, LANES), jnp.float32)
FIELD = jax.ShapeDtypeStruct((2, TS, TS), jnp.float32)


def open_halo(cons, corners, counts):
    return pl.pallas_call(
        open_kernel, out_shape=(WIDE, jax.ShapeDtypeStruct((3, 8, LANES), jnp.int32)),
        in_specs=[VMEM, SMEM, SMEM], out_specs=(VMEM,) * 2,
        scratch_shapes=pull_buffers() + [pltpu.VMEM((8, LANES), jnp.int32), pltpu.VMEM((3, 8, LANES), jnp.int32)]
        + copies_of(13),
        compiler_params=params(1, 6), name="open_halo", cost_estimate=busy(10),
    )(cons, corners, counts)


def middle(center, rr, rb, inv, cons, dual):
    return pl.pallas_call(
        middle_kernel,
        out_shape=(FIELD, WIDE),
        in_specs=[VMEM] * 6, out_specs=(VMEM,) * 2,
        scratch_shapes=[buffer(2, SPAN, OVER), buffer(2, 2, OVER, OVER), buffer(2, OVER, OVER)]
        + pull_buffers() + copies_of(16),
        compiler_params=params(2, 10), name="middle", cost_estimate=busy(15),
    )(center, rr, rb, inv, cons, dual)


def close(center, rr, rb, cons, dual, est, inv, psum):
    scratch = [
        buffer(2, SPAN, OVER), buffer(2, 2, OVER, OVER), buffer(2, OVER, OVER),
        buffer(RUN, 3, 32, PS), buffer(RUN, 3, 32, PS), buffer(RUN, 3, 32, PS),
        buffer(RUN, 3, 8, PS), buffer(RUN, 3, 8, PS), buffer(3, 8, PS), buffer(LAPS, 3, 8, PS),
        buffer(2, RUN, RUN, 2, 8, PS),
        buffer(2, COLS, 2, 32, TS), buffer(2, COLS, 2, 32, TS), buffer(2, 2, 32, TS),
        buffer(2, 2, 32, TS), buffer(2, COLS, 2, 32, TS),
    ]
    for count in ((3,), (1,), (RUN,), (RUN,), (LAPS,), (RUN,), (RUN,), (1,), (2, COLS), (2,), (2, COLS)):
        scratch += copies_of(*count)
    return pl.pallas_call(
        close_kernel,
        out_shape=(
            jax.ShapeDtypeStruct((2, COLS, 2, 32, TS), jnp.bfloat16), FIELD,
            jax.ShapeDtypeStruct((2, RUN, RUN, 2, 8, PS), jnp.bfloat16),
        ),
        in_specs=[VMEM] * 8, out_specs=(VMEM,) * 3,
        scratch_shapes=scratch, compiler_params=params(3, 12), name="close", cost_estimate=busy(25),
    )(center, rr, rb, cons, dual, est, inv, psum)


def finish_kernel(settled, kept, grown, probe_ref, cons_out, dual_out, probe_out):
    for n in range(2):
        for q in range(COLS):
            rows = pl.ds(n * OVER + q * 32, 32)
            for c in range(2):
                value = settled[n, q, c].astype(jnp.float32)
                cons_out[c, rows, :] = value
                dual_out[c, rows, :] = kept[c, rows, :] - value
    for part_at in range(8):
        for k in range(RUN):
            rows = pl.ds(part_at * 32 + k * 8, 8)
            for c in range(2):
                step = grown[part_at // 4, part_at % 4, k, c].astype(jnp.float32)
                probe_out[c, rows, :] = probe_ref[c, rows, :] + step


def finish(settled, kept, grown, probe):
    return pl.pallas_call(
        finish_kernel, out_shape=(FIELD,) * 3, in_specs=[VMEM] * 4, out_specs=(VMEM,) * 3,
        compiler_params=pltpu.CompilerParams(vmem_limit_bytes=8 * 1024 * 1024),
        name="finish", cost_estimate=busy(1),
    )(settled, kept, grown, probe)


def shards(consensus, duals, probes, amplitudes, offsets, counts):
    m1, m2 = (jnp.asarray(table) for table in transform_tables())
    cons, dual, probe = consensus[0], duals[0, 0], probes[0]
    measured, corners = amplitudes[0, 0], jnp.swapaxes(offsets[0, 0], 0, 1)
    wide, near = open_halo(cons, corners, counts)
    center, rr, rb, psum, inv = patches(True, corners, counts, wide, probe, measured, m1, m2, near=near)
    est, wide = middle(center, rr, rb, inv, cons, dual)
    center, rr, rb, psum = patches(False, corners, counts, wide, probe, measured, m1, m2, prev=psum)
    settled, kept, grown = close(center, rr, rb, cons, dual, est, inv, psum)
    cons_new, dual_new, probe_new = finish(settled, kept, grown, probe)
    return cons_new[None], dual_new[None, None], probe_new[None]


def solution(mesh):
    placed = (
        P("tile", None, None, None),
        P("scan", "tile", None, None, None),
        P("scan", None, None, None),
        P("scan", "tile", None, None, None),
        P("scan", "tile", None, None),
        P("scan", "tile"),
    )
    return jax.shard_map(
        shards,
        mesh=mesh,
        in_specs=placed,
        out_specs=(
            P("tile", None, None, None),
            P("scan", "tile", None, None, None),
            P("scan", None, None, None),
        ),
        check_vma=False,
    )
```

```python
import functools
import math

import jax
import jax.numpy as jnp
import ml_dtypes
import numpy as np
from jax import lax
from jax.experimental import pallas as pl
from jax.experimental.pallas import tpu as pltpu
from jax.sharding import PartitionSpec as P

PS = 256
TS = 256
OVER = 128
SPAN = TS + OVER
TGW = 4
SLOTS = 4
TILES = 96
RING = 12
RUN = 4
COLS = 4
LAPS = 3
LANES = 128
penalty = 0.5
smoothing = 0.05
probe_step = 3.0
MESH = pl.DeviceIdType.MESH
VMEM = pl.BlockSpec(memory_space=pltpu.VMEM)
SMEM = pl.BlockSpec(memory_space=pltpu.SMEM)


def transform_tables():
    index = np.arange(PS, dtype=np.int64)
    angle = ((index[:, None] * index[None, :]) % PS).astype(np.float64) * (2.0 * math.pi / PS)
    scale = 1.0 / math.sqrt(PS)
    real = (np.cos(angle) * scale).astype(np.float32)
    imag = (-np.sin(angle) * scale).astype(np.float32)
    forward = np.block([[real, -imag], [imag, real]])
    return forward.astype(ml_dtypes.bfloat16), forward.T.astype(ml_dtypes.bfloat16)


def shifted_in(block, col, lane):
    amount = lax.rem(LANES - col, LANES)
    turned = [pltpu.roll(piece, amount, axis=1) for piece in block]
    keep = lane < LANES - col
    return [jnp.where(keep, turned[k], turned[k + 1]) for k in range(2)]


def shifted_out(left, right, col, lane):
    amount = lax.rem(col, LANES)
    left = pltpu.roll(left, amount, axis=1)
    right = pltpu.roll(right, amount, axis=1)
    past = lane >= col
    zero = jnp.zeros_like(left)
    return [jnp.where(past, left, zero), jnp.where(past, right, left), jnp.where(past, zero, right)]


def patches_kernel(first, *refs):
    if first:
        (off_ref, cnt_ref, near_ref, wide_ref, probe_ref, amp_ref, m1_ref, m2_ref,
         center_ref, rr_ref, rb_ref, acc_ref, inv_ref,
         tot_ref, e_ref, r_ref, win_ref, power_ref, weight_ref) = refs
    else:
        (off_ref, cnt_ref, wide_ref, probe_ref, amp_ref, m1_ref, m2_ref, prev_ref,
         center_ref, rr_ref, rb_ref, psum_ref,
         tot_ref, e_ref, r_ref, win_ref, acc_ref) = refs
    tot_ref[...] = jnp.zeros_like(tot_ref)
    if first:
        acc_ref[...] = jnp.zeros_like(acc_ref)
    else:
        acc_ref[...] = prev_ref[...]
    half = [pl.ds(0, LANES), pl.ds(LANES, LANES)]
    lane = lax.broadcasted_iota(jnp.int32, (PS, LANES), 1)

    def gather(slot, at):
        row = off_ref[0, slot]
        col = off_ref[1, slot]
        real = shifted_in([wide_ref[0, k, pl.ds(row, PS), :] for k in range(3)], col, lane)
        imag = shifted_in([wide_ref[1, k, pl.ds(row, PS), :] for k in range(3)], col, lane)
        for h in range(2):
            wr, wi = real[h], imag[h]
            pr = probe_ref[0, :, half[h]]
            pi = probe_ref[1, :, half[h]]
            win_ref[at, 0, :, half[h]] = wr
            win_ref[at, 1, :, half[h]] = wi
            e_ref[at, :PS, half[h]] = (pr * wr - pi * wi).astype(jnp.bfloat16)
            e_ref[at, PS:, half[h]] = (pr * wi + pi * wr).astype(jnp.bfloat16)

    def transform(left_ref, right_ref, field_ref, at):
        re = jnp.dot(left_ref[:PS, :], field_ref[at], preferred_element_type=jnp.float32)
        im = jnp.dot(left_ref[PS:, :], field_ref[at], preferred_element_type=jnp.float32)
        inner = jnp.concatenate([re.astype(jnp.bfloat16), im.astype(jnp.bfloat16)], 1)
        return jnp.dot(inner, right_ref[...], preferred_element_type=jnp.float32)

    def replace(slot, at):
        wave = transform(m1_ref, m2_ref, e_ref, at)
        wr, wi = wave[:, :PS], wave[:, PS:]
        factor = amp_ref[slot].astype(jnp.float32) * lax.rsqrt(wr * wr + wi * wi + smoothing) - 1.0
        r_ref[at, :PS, :] = (wr * factor).astype(jnp.bfloat16)
        r_ref[at, PS:, :] = (wi * factor).astype(jnp.bfloat16)

    def scatter(slot, at):
        row = off_ref[0, slot]
        col = off_ref[1, slot]
        back = transform(m2_ref, m1_ref, r_ref, at)
        terms = [[], []]
        for h in range(2):
            br = back[:, h * LANES:(h + 1) * LANES]
            bi = back[:, PS + h * LANES:PS + (h + 1) * LANES]
            pr = probe_ref[0, :, half[h]]
            pi = probe_ref[1, :, half[h]]
            wr = win_ref[at, 0, :, half[h]]
            wi = win_ref[at, 1, :, half[h]]
            terms[0].append(pr * br + pi * bi)
            terms[1].append(pr * bi - pi * br)
            acc_ref[0, :, half[h]] += wr * br + wi * bi
            acc_ref[1, :, half[h]] += wr * bi - wi * br
            acc_ref[2, :, half[h]] += wr * wr + wi * wi
        for c in range(2):
            out = shifted_out(terms[c][0], terms[c][1], col, lane)
            for k in range(3):
                tot_ref[c, k, pl.ds(row, PS), :] += out[k]

    def visit(slots):
        for stage in (gather, replace, scatter):
            for at, slot in enumerate(slots):
                stage(slot, at)

    count = cnt_ref[0, 0]

    for full in range(1, SLOTS + 1):
        @pl.when(count == full)
        def _(full=full):
            visit(list(range(full)))

    for k in range(2):
        center_ref[:, :, half[k]] = tot_ref[:, k, :TS, :]
        rb_ref[k] = tot_ref[:, k, TS:, :].astype(jnp.bfloat16)
    rr_ref[...] = tot_ref[:, 2].astype(jnp.bfloat16)
    if first:
        weight_ref[...] = jnp.zeros_like(weight_ref)
        power_ref[...] = probe_ref[0] * probe_ref[0] + probe_ref[1] * probe_ref[1]

        def weigh(at, col, aside, skip=0):
            rows = pl.ds(skip, PS - skip)
            out = shifted_out(power_ref[rows, half[0]], power_ref[rows, half[1]], col, lane[skip:])
            at = pl.ds(at + skip, PS - skip)
            if aside:
                weight_ref[0, at, :] += out[2]
            else:
                weight_ref[0, at, :] += out[0]
                weight_ref[1, at, :] += out[1]

        def own(slot, carry):
            weigh(off_ref[0, slot] + TS, off_ref[1, slot], False)
            return carry

        def left(slot, carry):
            weigh(near_ref[0, 0, slot] + TS, near_ref[0, 1, slot], True)
            return carry

        def above(slot, carry):
            weigh(near_ref[1, 0, slot], near_ref[1, 1, slot], False, OVER)
            return carry

        def corner(slot, carry):
            weigh(near_ref[2, 0, slot], near_ref[2, 1, slot], True, OVER)
            return carry

        lax.fori_loop(0, cnt_ref[0, 0], own, 0)
        lax.fori_loop(0, near_ref[0, 2, 0], left, 0)
        lax.fori_loop(0, near_ref[1, 2, 0], above, 0)
        lax.fori_loop(0, near_ref[2, 2, 0], corner, 0)
        for k in range(2):
            inv_ref[:, half[k]] = 1.0 / (weight_ref[k, TS:2 * TS, :] + penalty)
    else:
        for part in range(8):
            rows = pl.ds(part * 32, 32)
            for c in range(3):
                psum_ref[part // 4, part % 4, c] = acc_ref[c, rows, :].astype(jnp.bfloat16)


def busy(microseconds):
    return pl.CostEstimate(flops=microseconds * 1_000_000_000, bytes_accessed=microseconds * 3_000_000, transcendentals=0)


def patches(first, corners, count, wide, probe, measured, m1, m2, near=None, prev=None):
    shape = jax.ShapeDtypeStruct
    out_shape = [
        shape((2, TS, TS), jnp.float32),
        shape((2, SPAN, OVER), jnp.bfloat16),
        shape((2, 2, OVER, OVER), jnp.bfloat16),
    ]
    scratch = [
        pltpu.VMEM((2, 3, SPAN, LANES), jnp.float32),
        pltpu.VMEM((4, 2 * PS, PS), jnp.bfloat16),
        pltpu.VMEM((4, 2 * PS, PS), jnp.bfloat16),
        pltpu.VMEM((4, 2, PS, PS), jnp.float32),
    ]
    if first:
        args = [corners, count, near, wide, probe, measured, m1, m2]
        scalars = 3
        out_shape += [shape((3, PS, PS), jnp.float32), shape((TS, TS), jnp.float32)]
        scratch += [pltpu.VMEM((PS, PS), jnp.float32), pltpu.VMEM((2, TS + SPAN, LANES), jnp.float32)]
    else:
        args = [corners, count, wide, probe, measured, m1, m2, prev]
        scalars = 2
        out_shape += [shape((2, RUN, 3, 32, PS), jnp.bfloat16)]
        scratch += [pltpu.VMEM((3, PS, PS), jnp.float32)]
    return pl.pallas_call(
        functools.partial(patches_kernel, first),
        out_shape=tuple(out_shape),
        in_specs=[SMEM] * scalars + [VMEM] * (len(args) - scalars),
        out_specs=(VMEM,) * len(out_shape),
        scratch_shapes=scratch,
        compiler_params=pltpu.CompilerParams(vmem_limit_bytes=16 * 1024 * 1024),
        name="patches", cost_estimate=busy(8),
    )(*args)


def moved(t, by):
    return lax.rem(t + (by + TILES), TILES)


def remote(src, dst, sends, recvs, at, slot, target):
    return pltpu.make_async_remote_copy(
        src_ref=src, dst_ref=dst, send_sem=sends.at[at], recv_sem=recvs.at[slot],
        device_id=target, device_id_type=MESH,
    )


def hail(targets):
    for target in targets:
        pl.semaphore_signal(pltpu.get_barrier_semaphore(), inc=1, device_id=target, device_id_type=MESH)
    return len(targets)


def meet(count):
    pl.semaphore_wait(pltpu.get_barrier_semaphore(), count)


def start_if(flag, *copies):
    @pl.when(flag)
    def _():
        for copy in copies:
            copy.start()


def wait_if(flag, *copies):
    @pl.when(flag)
    def _():
        for copy in copies:
            copy.wait_recv()


def sent_if(flag, *copies):
    @pl.when(flag)
    def _():
        for copy in copies:
            copy.wait_send()


def clear_if(flag, *refs):
    @pl.when(flag)
    def _():
        for ref in refs:
            ref[...] = jnp.zeros_like(ref)


def sides(t):
    column = lax.rem(t, TGW)
    return column > 0, column < TGW - 1, t >= TGW, t < TILES - TGW


def block(at):
    return pl.ds(at * OVER, OVER)


class Pull:
    def __init__(self, t, quads, below_in, right_in, corner_in, sends, recvs, base):
        self.left, self.right, self.above, self.below = sides(t)
        self.refs = quads, below_in, right_in, corner_in
        up, back = {"tile": moved(t, -TGW)}, {"tile": moved(t, -1)}
        make = lambda src, dst, at, to: remote(src, dst, sends, recvs, at, at, to)
        self.up = [[make(quads.at[b, c], below_in.at[b, c], base + 2 * b + c, up) for c in range(2)] for b in range(2)]
        self.side = [[make(quads.at[2 * a, c], right_in.at[a, c], base + 4 + 2 * a + c, back) for c in range(2)] for a in range(2)]
        self.relay = [make(below_in.at[0, c], corner_in.at[c], base + 8 + c, back) for c in range(2)]

    def clear(self):
        quads, below_in, right_in, corner_in = self.refs
        clear_if(jnp.logical_not(self.right), right_in, corner_in)
        clear_if(jnp.logical_not(self.below), below_in)

    def offer(self, value, c, a, b, wide_ref):
        rounded = value.astype(jnp.bfloat16)
        wide_ref[c, b, block(a), :] = rounded.astype(jnp.float32)
        if not (a and b):
            self.refs[0][2 * a + b, c] = rounded

    def begin(self, c, a, b):
        if a == 0:
            start_if(self.above, self.up[b][c])
        if b == 0:
            start_if(self.left, self.side[a][c])

    def finish(self, wide_ref):
        quads, below_in, right_in, corner_in = self.refs
        for c in range(2):
            wait_if(self.below, self.up[0][c])
            start_if(self.left, self.relay[c])
        for c in range(2):
            wait_if(self.right, self.side[0][c], self.side[1][c])
            for a in range(2):
                wide_ref[c, 2, block(a), :] = right_in[a, c].astype(jnp.float32)
            wait_if(self.below, self.up[1][c])
            for b in range(2):
                wide_ref[c, b, TS:, :] = below_in[b, c].astype(jnp.float32)
        for c in range(2):
            sent_if(self.above, self.up[0][c], self.up[1][c])
            sent_if(self.left, self.side[0][c], self.side[1][c])
        for c in range(2):
            wait_if(self.right, self.relay[c])
            wide_ref[c, 2, TS:, :] = corner_in[c].astype(jnp.float32)
        sent_if(self.left, *self.relay)


def open_kernel(cons_ref, corner_ref, count_ref, wide_ref, near_ref,
                quads, below_in, right_in, corner_in, note, note_in, sends, recvs):
    t = lax.axis_index("tile")
    hailed = hail([{"tile": moved(t, by)} for by in (1, TGW, -1, -TGW, -TGW - 1)])
    pull = Pull(t, quads, below_in, right_in, corner_in, sends, recvs, 0)
    pull.clear()
    line = lax.broadcasted_iota(jnp.int32, note.shape, 0)
    lane = lax.broadcasted_iota(jnp.int32, note.shape, 1)
    filled = jnp.where(jnp.logical_and(line == 2, lane == 0), count_ref[0, 0], 0)
    for axis in range(2):
        for slot in range(SLOTS):
            filled = jnp.where(jnp.logical_and(line == axis, lane == slot), corner_ref[axis, slot], filled)
    note[...] = filled
    notes = [
        remote(note, note_in.at[k], sends, recvs, 10 + k, 10 + k, {"tile": moved(t, by)})
        for k, by in enumerate((1, TGW, TGW + 1))
    ]
    quarters = ((0, 0), (0, 1), (1, 0), (1, 1))
    for a, b in quarters:
        for c in range(2):
            pull.offer(cons_ref[c, block(a), block(b)], c, a, b, wide_ref)
    meet(hailed)
    start_if(pull.above, *pull.up[0], *pull.up[1])
    start_if(pull.left, *pull.side[0], *pull.side[1])
    for copy in notes:
        copy.start()
    pull.finish(wide_ref)
    for copy in notes:
        copy.wait()
    for k, flag in enumerate((pull.left, pull.above, jnp.logical_and(pull.left, pull.above))):
        near_ref[k] = note_in[k] * jnp.where(flag, 1, 0)


def middle_kernel(center_ref, rr, rb, inv_ref, cons_ref, dual_ref, est_ref, wide_ref,
                  left_in, above_in, lowered, quads, below_in, right_in, corner_in, sends, recvs):
    t = lax.axis_index("tile")
    left, right, above, below = sides(t)
    hailed = hail([{"tile": moved(t, by)} for by in (1, TGW, -1, -TGW)])
    pull = Pull(t, quads, below_in, right_in, corner_in, sends, recvs, 6)
    pull.clear()
    clear_if(jnp.logical_not(left), left_in)
    clear_if(jnp.logical_not(above), above_in)
    on, down = {"tile": moved(t, 1)}, {"tile": moved(t, TGW)}
    make = lambda src, dst, at, to: remote(src, dst, sends, recvs, at, at, to)
    push_on = [make(rr.at[c], left_in.at[c], c, on) for c in range(2)]
    push_far = [make(rb.at[1, c], above_in.at[1, c], 2 + c, down) for c in range(2)]
    push_low = [make(lowered.at[c], above_in.at[0, c], 4 + c, down) for c in range(2)]

    def relay(c):
        wait_if(left, push_on[c])
        lowered[c] = (rb[0, c].astype(jnp.float32) + left_in[c, TS:, :].astype(jnp.float32)).astype(jnp.bfloat16)
        start_if(below, push_low[c])

    def update(c, a, b):
        rows, cols = block(a), block(b)
        total = center_ref[c, rows, cols]
        if a == 0:
            total = total + above_in[b, c].astype(jnp.float32)
        if b == 0:
            total = total + left_in[c, rows, :].astype(jnp.float32)
        value = cons_ref[c, rows, cols] + (total - penalty * dual_ref[c, rows, cols]) * inv_ref[rows, cols]
        est_ref[c, rows, cols] = value
        pull.offer(value, c, a, b, wide_ref)
        pull.begin(c, a, b)

    update(0, 1, 1)
    update(1, 1, 1)
    meet(hailed)
    start_if(right, *push_on)
    start_if(below, *push_far)
    relay(0)
    relay(1)
    for c in range(2):
        update(c, 1, 0)
    for c in range(2):
        wait_if(above, push_far[c])
        update(c, 0, 1)
    for c in range(2):
        wait_if(above, push_low[c])
        update(c, 0, 0)
    for c in range(2):
        sent_if(right, push_on[c])
        sent_if(below, push_far[c], push_low[c])
    pull.finish(wide_ref)


def close_kernel(center_ref, rr, rb, cons_ref, dual_ref, est_ref, inv_ref, psum,
                 settled_out, kept, grown_out,
                 left_in, above_in, lowered, half_in, half, run_in, ring_out, ring_in, tri_out, tri_in, grown,
                 mine, cols_in, part, part_in, settled,
                 rim_s, rim_r, half_s, half_r, run_s, run_r, ring_s, ring_r, tri_s, tri_r, grow_s, grow_r,
                 wide_s, wide_r, back_s, back_r, col_s, col_r, pair_s, pair_r, out_s, out_r):
    t = lax.axis_index("tile")
    left, right, above, below = sides(t)
    core = lax.rem(t, 2)
    z = lax.rem(lax.div(t, 2), RING)
    y = lax.div(t, 2 * RING)
    scan = lax.axis_index("scan")
    yh = lax.rem(scan, 2)
    x = lax.div(scan, 2)
    tile_at = lambda y_, z_, c_: {"tile": (y_ * RING + z_) * 2 + c_}
    scan_at = lambda x_, h_: {"scan": x_ * 2 + h_}
    ys = [lax.rem(y + k, RUN) for k in range(1, RUN)]
    xs = [lax.rem(x + k, COLS) for k in range(1, COLS)]
    lap, seat = lax.div(z, RUN), lax.rem(z, RUN)
    seats = [lax.rem(seat + k, RUN) for k in range(1, RUN)]
    laps = [lax.rem(lap + k, LAPS) for k in range(1, LAPS)]
    at_seat = lambda k: tile_at(y, lap * RUN + k, core)
    at_lap = lambda k: tile_at(y, k * RUN + seat, core)
    sibling = tile_at(y, z, 1 - core)
    twin = scan_at(x, 1 - yh)
    on, down = {"tile": moved(t, 1)}, {"tile": moved(t, TGW)}
    push_on = remote(rr, left_in, rim_s, rim_r, 0, 0, on)
    push_far = remote(rb.at[1], above_in.at[1], rim_s, rim_r, 1, 1, down)
    push_low = remote(lowered, above_in.at[0], rim_s, rim_r, 2, 2, down)
    to_half = remote(psum.at[1 - core], half_in, half_s, half_r, 0, 0, sibling)

    hailed = hail([sibling] + [{"tile": moved(t, by)} for by in (-1, -TGW)] + [twin]
                  + [tile_at(k, z, core) for k in ys] + [scan_at(k, yh) for k in xs]
                  + [at_seat(k) for k in seats] + [at_lap(k) for k in laps])
    clear_if(jnp.logical_not(left), left_in)
    clear_if(jnp.logical_not(above), above_in)

    def cross(n, k, at, other):
        return remote(mine.at[n, k], cols_in.at[n, at], col_s, col_r, (n, k), (n, at), scan_at(other, yh))

    def pair(n):
        return remote(part.at[n], part_in.at[n], pair_s, pair_r, n, n, twin)

    def spread(n, k, at, other):
        own = settled.at[n, at]
        return remote(own, own, out_s, out_r, (n, k), (n, at), scan_at(other, yh))

    def update(a, b):
        rows, cols = block(a), block(b)
        inv = inv_ref[rows, cols]
        for c in range(2):
            total = center_ref[c, rows, cols]
            if a == 0:
                total = total + above_in[b, c].astype(jnp.float32)
            if b == 0:
                total = total + left_in[c, rows, :].astype(jnp.float32)
            dual = dual_ref[c, rows, cols]
            estimate = est_ref[c, rows, cols]
            value = estimate + (total + penalty * (cons_ref[c, rows, cols] - dual - estimate)) * inv + dual
            kept[c, rows, cols] = value
            value = value.astype(jnp.bfloat16)
            for q in range(COLS):
                mine[a, q, c, :, cols] = value[q * 32:(q + 1) * 32]

    def share(n):
        for k in xs:
            cross(n, k, x, k).start()

    def combine(n):
        for k in xs:
            cross(n, k, k, k).wait_recv()
        cols_in[n, x] = mine[n, x]
        for c in range(2):
            summed = cols_in[n, 0, c].astype(jnp.float32)
            for k in range(1, COLS):
                summed = summed + cols_in[n, k, c].astype(jnp.float32)
            part[n, c] = summed.astype(jnp.bfloat16)
        pair(n).start()

    def settle(n):
        pair(n).wait_recv()
        shares = [(part[n, c].astype(jnp.float32) + part_in[n, c].astype(jnp.float32)) * 0.125 for c in range(2)]
        modulus = jnp.sqrt(shares[0] * shares[0] + shares[1] * shares[1])
        bound = 1.0 / jnp.maximum(modulus, 1.0)
        for c in range(2):
            settled[n, x, c] = (shares[c] * bound).astype(jnp.bfloat16)
        for k in xs:
            spread(n, k, x, k).start()

    def give(n):
        for k in xs:
            spread(n, k, k, k).wait_recv()
        settled_out[n] = settled[n]

    def run_copy(k, at):
        return remote(half.at[k], run_in.at[at], run_s, run_r, k, at, tile_at(k, z, core))

    def ring_copy(k, at):
        return remote(ring_out.at[k], ring_in.at[at], ring_s, ring_r, k, at, at_seat(k))

    def tri_copy(k, at):
        return remote(tri_out, tri_in.at[at], tri_s, tri_r, k, at, at_lap(k))

    def grow_copy(k, at):
        own = grown.at[core, y, at]
        return remote(own, own, grow_s, grow_r, k, at, at_seat(k))

    def wide_copy(k, at):
        own = grown.at[core, at]
        return remote(own, own, wide_s, wide_r, k, at, tile_at(k, z, core))

    def back_copy(at):
        own = grown.at[at]
        return remote(own, own, back_s, back_r, 0, 0, sibling)

    def probe_run():
        to_half.wait_recv()
        for k in ys + [y]:
            half[k] = (psum[core, k].astype(jnp.float32) + half_in[k].astype(jnp.float32)).astype(jnp.bfloat16)
            if k is not y:
                run_copy(k, y).start()

    def probe_ring():
        for k in ys:
            run_copy(k, k).wait_recv()
        run_in[y] = half[y]
        for c in range(3):
            summed = run_in[0, c].astype(jnp.float32)
            for k in range(1, RUN):
                summed = summed + run_in[k, c].astype(jnp.float32)
            summed = summed.astype(jnp.bfloat16)
            for k in range(RUN):
                ring_out[k, c] = summed[k * 8:k * 8 + 8]
        for k in seats:
            ring_copy(k, seat).start()

    def probe_tri():
        for k in seats:
            ring_copy(k, k).wait_recv()
        ring_in[seat] = ring_out[seat]
        for c in range(3):
            summed = ring_in[0, c].astype(jnp.float32)
            for k in range(1, RUN):
                summed = summed + ring_in[k, c].astype(jnp.float32)
            tri_out[c] = summed.astype(jnp.bfloat16)
        for k in laps:
            tri_copy(k, lap).start()

    def probe_grow():
        for k in laps:
            tri_copy(k, k).wait_recv()
        tri_in[lap] = tri_out[...]
        sums = []
        for c in range(3):
            summed = tri_in[0, c].astype(jnp.float32)
            for k in range(1, LAPS):
                summed = summed + tri_in[k, c].astype(jnp.float32)
            sums.append(summed)
        scale = probe_step * lax.rsqrt(sums[2] + 1.0)
        for c in range(2):
            grown[core, y, seat, c] = (sums[c] * scale).astype(jnp.bfloat16)
        for k in seats:
            grow_copy(k, seat).start()

    def probe_wide():
        for k in seats:
            grow_copy(k, k).wait_recv()
        for k in ys:
            wide_copy(k, y).start()

    def probe_back():
        for k in ys:
            wide_copy(k, k).wait_recv()
        back_copy(core).start()

    def probe_give():
        back_copy(1 - core).wait_recv()
        grown_out[...] = grown[...]

    update(1, 1)
    meet(hailed)
    to_half.start()
    start_if(right, push_on)
    start_if(below, push_far)
    probe_run()
    wait_if(left, push_on)
    for c in range(2):
        lowered[c] = (rb[0, c].astype(jnp.float32) + left_in[c, TS:, :].astype(jnp.float32)).astype(jnp.bfloat16)
    start_if(below, push_low)
    update(1, 0)
    share(1)
    probe_ring()
    wait_if(above, push_far)
    update(0, 1)
    combine(1)
    wait_if(above, push_low)
    update(0, 0)
    share(0)
    probe_tri()
    combine(0)
    probe_grow()
    settle(1)
    for k in ys:
        run_copy(k, y).wait_send()
    to_half.wait_send()
    sent_if(right, push_on)
    sent_if(below, push_far, push_low)
    pair(1).wait_send()
    for k in xs:
        cross(1, k, x, k).wait_send()
    probe_wide()
    settle(0)
    for k in seats:
        ring_copy(k, seat).wait_send()
        grow_copy(k, seat).wait_send()
    for k in laps:
        tri_copy(k, lap).wait_send()
    pair(0).wait_send()
    for k in xs:
        cross(0, k, x, k).wait_send()
    give(1)
    probe_back()
    for k in ys:
        wide_copy(k, y).wait_send()
    give(0)
    for n in range(2):
        for k in xs:
            spread(n, k, x, k).wait_send()
    probe_give()
    back_copy(core).wait_send()


def params(identity, grant):
    return pltpu.CompilerParams(
        collective_id=identity, has_side_effects=True, vmem_limit_bytes=grant * 1024 * 1024
    )


def buffer(*shape):
    return pltpu.VMEM(shape, jnp.bfloat16)


def pull_buffers():
    return [
        buffer(3, 2, OVER, OVER), buffer(2, 2, OVER, OVER), buffer(2, 2, OVER, OVER), buffer(2, OVER, OVER)
    ]


def copies_of(*count):
    return [pltpu.SemaphoreType.DMA(count), pltpu.SemaphoreType.DMA(count)]


WIDE = jax.ShapeDtypeStruct((2, 3, SPAN, LANES), jnp.float32)
FIELD = jax.ShapeDtypeStruct((2, TS, TS), jnp.float32)


def open_halo(cons, corners, counts):
    return pl.pallas_call(
        open_kernel, out_shape=(WIDE, jax.ShapeDtypeStruct((3, 8, LANES), jnp.int32)),
        in_specs=[VMEM, SMEM, SMEM], out_specs=(VMEM,) * 2,
        scratch_shapes=pull_buffers() + [pltpu.VMEM((8, LANES), jnp.int32), pltpu.VMEM((3, 8, LANES), jnp.int32)]
        + copies_of(13),
        compiler_params=params(1, 6), name="open_halo", cost_estimate=busy(10),
    )(cons, corners, counts)


def middle(center, rr, rb, inv, cons, dual):
    return pl.pallas_call(
        middle_kernel,
        out_shape=(FIELD, WIDE),
        in_specs=[VMEM] * 6, out_specs=(VMEM,) * 2,
        scratch_shapes=[buffer(2, SPAN, OVER), buffer(2, 2, OVER, OVER), buffer(2, OVER, OVER)]
        + pull_buffers() + copies_of(16),
        compiler_params=params(2, 10), name="middle", cost_estimate=busy(15),
    )(center, rr, rb, inv, cons, dual)


def close(center, rr, rb, cons, dual, est, inv, psum):
    scratch = [
        buffer(2, SPAN, OVER), buffer(2, 2, OVER, OVER), buffer(2, OVER, OVER),
        buffer(RUN, 3, 32, PS), buffer(RUN, 3, 32, PS), buffer(RUN, 3, 32, PS),
        buffer(RUN, 3, 8, PS), buffer(RUN, 3, 8, PS), buffer(3, 8, PS), buffer(LAPS, 3, 8, PS),
        buffer(2, RUN, RUN, 2, 8, PS),
        buffer(2, COLS, 2, 32, TS), buffer(2, COLS, 2, 32, TS), buffer(2, 2, 32, TS),
        buffer(2, 2, 32, TS), buffer(2, COLS, 2, 32, TS),
    ]
    for count in ((3,), (1,), (RUN,), (RUN,), (LAPS,), (RUN,), (RUN,), (1,), (2, COLS), (2,), (2, COLS)):
        scratch += copies_of(*count)
    return pl.pallas_call(
        close_kernel,
        out_shape=(
            jax.ShapeDtypeStruct((2, COLS, 2, 32, TS), jnp.bfloat16), FIELD,
            jax.ShapeDtypeStruct((2, RUN, RUN, 2, 8, PS), jnp.bfloat16),
        ),
        in_specs=[VMEM] * 8, out_specs=(VMEM,) * 3,
        scratch_shapes=scratch, compiler_params=params(3, 12), name="close", cost_estimate=busy(25),
    )(center, rr, rb, cons, dual, est, inv, psum)


def finish_kernel(settled, kept, grown, probe_ref, cons_out, dual_out, probe_out):
    for n in range(2):
        for q in range(COLS):
            rows = pl.ds(n * OVER + q * 32, 32)
            for c in range(2):
                value = settled[n, q, c].astype(jnp.float32)
                cons_out[c, rows, :] = value
                dual_out[c, rows, :] = kept[c, rows, :] - value
    for part_at in range(8):
        for k in range(RUN):
            rows = pl.ds(part_at * 32 + k * 8, 8)
            for c in range(2):
                step = grown[part_at // 4, part_at % 4, k, c].astype(jnp.float32)
                probe_out[c, rows, :] = probe_ref[c, rows, :] + step


def finish(settled, kept, grown, probe):
    return pl.pallas_call(
        finish_kernel, out_shape=(FIELD,) * 3, in_specs=[VMEM] * 4, out_specs=(VMEM,) * 3,
        compiler_params=pltpu.CompilerParams(vmem_limit_bytes=8 * 1024 * 1024),
        name="finish", cost_estimate=busy(1),
    )(settled, kept, grown, probe)


def shards(consensus, duals, probes, amplitudes, offsets, counts):
    m1, m2 = (jnp.asarray(table) for table in transform_tables())
    cons, dual, probe = consensus[0], duals[0, 0], probes[0]
    measured, corners = amplitudes[0, 0], jnp.swapaxes(offsets[0, 0], 0, 1)
    wide, near = open_halo(cons, corners, counts)
    center, rr, rb, psum, inv = patches(True, corners, counts, wide, probe, measured, m1, m2, near=near)
    est, wide = middle(center, rr, rb, inv, cons, dual)
    center, rr, rb, psum = patches(False, corners, counts, wide, probe, measured, m1, m2, prev=psum)
    settled, kept, grown = close(center, rr, rb, cons, dual, est, inv, psum)
    cons_new, dual_new, probe_new = finish(settled, kept, grown, probe)
    return cons_new[None], dual_new[None, None], probe_new[None]


def solution(mesh):
    placed = (
        P("tile", None, None, None),
        P("scan", "tile", None, None, None),
        P("scan", None, None, None),
        P("scan", "tile", None, None, None),
        P("scan", "tile", None, None),
        P("scan", "tile"),
    )
    return jax.shard_map(
        shards,
        mesh=mesh,
        in_specs=placed,
        out_specs=(
            P("tile", None, None, None),
            P("scan", "tile", None, None, None),
            P("scan", None, None, None),
        ),
        check_vma=False,
    )
```
